32 devices in a mesh: groups: 2 (over x), seq: 16 (over z, y, core).
Axes of the slice: x: 2, y: 2, z: 4, core: 2. Of those that a mesh axis runs over, the one named last changes fastest.
Arguments:
- query_in: bfloat16 [16384, 128], P(('groups', 'seq')), parts along dimension 0, may hold values from -6 to 6
- key_in: bfloat16 [16384, 128], P(('groups', 'seq')), parts along dimension 0, may hold values from -6 to 6
- value_in: bfloat16 [16384, 1024], P(('groups', 'seq')), parts along dimension 0, may hold values from -6 to 6
- conv_query: float32 [3, 128], replicated, may hold values from -3.5 to 3.5
- conv_key: float32 [3, 128], replicated, may hold values from -3.5 to 3.5
- conv_value: float32 [3, 1024], replicated, may hold values from -3.5 to 3.5
- norm_gain: float32 [1024], replicated, may hold values from 0.25 to 1.75
- grad_out: bfloat16 [16384, 1024], P(('groups', 'seq')), parts along dimension 0, may hold values from -6 to 6
Outputs:
- out_tokens: bfloat16 [16384, 1024], P(('groups', 'seq')), parts along dimension 0
- grad_query: bfloat16 [16384, 128], P(('groups', 'seq')), parts along dimension 0
- grad_key: bfloat16 [16384, 128], P(('groups', 'seq')), parts along dimension 0
- grad_value: bfloat16 [16384, 1024], P(('groups', 'seq')), parts along dimension 0
- grad_conv_query: float32 [6, 128], P('groups'), parts along dimension 0
- grad_conv_key: float32 [6, 128], P('groups'), parts along dimension 0
- grad_conv_value: float32 [6, 1024], P('groups'), parts along dimension 0
- grad_gain: float32 [2048], P('groups'), parts along dimension 0
The draws below stay inside these ranges and needn't reach their ends.
There are 2 independent parts, one for each index of `groups`. The reference program is written for one: setup_inputs(seed, part) draws one part's arguments, and reference() takes and returns one part's arrays. A program takes and returns all parts, laid end to end along the dimension named above; an argument that names none is the same for every part. Nothing has to cross between parts.
All inputs are finite; a program needn't handle non-finite values.
Results may differ from the reference program's by a relative error of at most 0.0088.
Values may be sent and summed in bfloat16 or wider, within the bound.
No kernel may reach another device: no remote copies, remote signals or barrier semaphores. Data moves between devices by JAX's collectives and lax.ppermute only.
A program may use at most 192 MiB of HBM per device.

```python
import jax
import jax.numpy as jnp
from jax import lax

HEADS = 8
FEAT = 16
HEAD_DIM = 128
TAPS = 3
BLOCK = 512
SEQ = 8192
QW = 128
VW = 1024


def block_scale(key, extent, split, low, top_value):
    level = 1.0
    for position, blocks in split:
        steps = jax.random.uniform(jax.random.fold_in(jax.random.fold_in(key, 6), position), (blocks,), jnp.float32, low / len(split), top_value / len(split))
        level = level * jnp.repeat(jnp.exp(steps), extent[position] // blocks).reshape((-1,) + (1,) * (len(extent) - 1 - position))
    return level


def centred(key, shape, deviation, reach, cuts=(), kind=jnp.bfloat16):
    level = block_scale(key, shape, cuts, -0.22, 0.18) if cuts else 1.0
    array = jax.random.normal(key, shape, jnp.float32) * deviation * level
    return jnp.minimum(jnp.maximum(array, -reach), reach).astype(kind)


def setup_inputs(seed: int = 0, part: int = 0) -> dict:
    keys = jax.random.split(jax.random.key(seed), 9)
    own_keys = jax.random.split(jax.random.fold_in(keys[8], part), 9)
    query_in = centred(own_keys[0], (SEQ, QW), 1.0, 6.0, ((0, 16),))
    key_in = centred(own_keys[1], (SEQ, QW), 1.0, 6.0, ((0, 16),))
    value_in = centred(own_keys[2], (SEQ, VW), 1.0, 6.0, ((0, 16),))
    conv_query = centred(keys[3], (TAPS, QW), TAPS ** -0.5, 3.5, (), jnp.float32)
    conv_key = centred(keys[4], (TAPS, QW), TAPS ** -0.5, 3.5, (), jnp.float32)
    conv_value = centred(keys[5], (TAPS, VW), TAPS ** -0.5, 3.5, (), jnp.float32)
    norm_gain = jnp.clip(1.0 + 0.15 * jax.random.normal(keys[6], (VW,), jnp.float32), 0.25, 1.75)
    grad_out = centred(own_keys[7], (SEQ, VW), 1.0, 6.0, ((0, 16),))
    return {"query_in": query_in, "key_in": key_in, "value_in": value_in, "conv_query": conv_query, "conv_key": conv_key, "conv_value": conv_value, "norm_gain": norm_gain, "grad_out": grad_out}


EPSILON = 1e-06
HIGHEST_PRECISION = lax.Precision.HIGHEST

def rounded(values):
    return lax.optimization_barrier(values.astype(jnp.bfloat16)).astype(jnp.float32)

def conv_input(signal, taps):
    margin = taps - 1
    return jnp.concatenate([jnp.zeros((margin, signal.shape[1]), jnp.float32), signal.astype(jnp.float32)], axis=0)

def conv_apply(wide, taps, length):
    total = jnp.zeros((length, wide.shape[1]), jnp.float32)
    for offset in range(taps.shape[0]):
        total = total + taps[offset] * wide[offset:offset + length]
    return total

def conv_grads(wide, taps, grad):
    length = grad.shape[0]
    margin = taps.shape[0] - 1
    grad_wide = jnp.concatenate([grad, jnp.zeros((margin, grad.shape[1]), jnp.float32)], axis=0)
    grad_signal = jnp.zeros(grad.shape, jnp.float32)
    for offset in range(taps.shape[0]):
        grad_signal = grad_signal + taps[offset] * grad_wide[margin - offset:margin - offset + length]
    grad_taps = jnp.stack([lax.optimization_barrier(jnp.sum(grad * wide[offset:offset + length], axis=0)) for offset in range(taps.shape[0])])
    return (grad_signal, grad_taps)

def feature_maps(values):
    feature = values.shape[-1]
    linear = rounded(values * feature ** (-0.25))
    square = values[..., :, None] * values[..., None, :] * (0.5 / feature) ** 0.5
    return (linear, rounded(square.reshape(values.shape[:-1] + (feature * feature,))))

def block_states(linear, square, values):
    return (lax.optimization_barrier(jnp.sum(values, axis=0)), jnp.einsum('shf,shd->hfd', linear, values, precision=HIGHEST_PRECISION), jnp.einsum('shg,shd->hgd', square, values, precision=HIGHEST_PRECISION))

def carried_values(linear, square, state):
    first = rounded(state[1])
    second = rounded(state[2])
    return state[0][None] + jnp.einsum('thf,hfd->thd', linear, first, precision=HIGHEST_PRECISION) + jnp.einsum('thg,hgd->thd', square, second, precision=HIGHEST_PRECISION)

def kernel_block(query_block, key_block):
    feature = query_block.shape[-1]
    length = query_block.shape[0]
    sigma = jnp.einsum('thf,shf->hts', query_block, key_block, precision=HIGHEST_PRECISION)
    weight = 1.0 + sigma * feature ** (-0.5) + sigma * sigma * (0.5 / feature)
    causal = lax.broadcasted_iota(jnp.int32, (length, length), 0) >= lax.broadcasted_iota(jnp.int32, (length, length), 1)
    return (sigma, causal, rounded(jnp.where(causal[None], weight, 0.0)))

def numerator(query_block, key_block, value_block, prefix):
    sigma, causal, weights = kernel_block(query_block, key_block)
    local = jnp.einsum('hts,shd->thd', weights, value_block, precision=HIGHEST_PRECISION)
    linear, square = feature_maps(query_block)
    return (local + carried_values(linear, square, prefix), linear, square)

def norm_pass(summed, gain, grad_block):
    scale = lax.rsqrt(lax.optimization_barrier(jnp.mean(summed * summed, axis=-1, keepdims=True)) + EPSILON)
    normal = summed * scale
    output = normal * gain
    incoming = grad_block.astype(jnp.float32)
    upstream = incoming * gain
    grad_sum = scale * (upstream - normal * lax.optimization_barrier(jnp.mean(normal * upstream, axis=-1, keepdims=True)))
    return (output, rounded(grad_sum), lax.optimization_barrier(jnp.sum(incoming * normal, axis=0)))

def feature_grad(point, vector, state):
    feature = point.shape[-1]
    first = rounded(state[1])
    second = rounded(state[2])
    linear_grad = jnp.einsum('nhd,hfd->nhf', vector, first, precision=HIGHEST_PRECISION)
    quadratic = jnp.einsum('nhd,hgd->nhg', vector, second, precision=HIGHEST_PRECISION)
    quadratic = quadratic.reshape(point.shape[:-1] + (feature, feature))
    crossed = jnp.einsum('nhab,nhb->nha', quadratic, point, precision=HIGHEST_PRECISION) + jnp.einsum('nhba,nhb->nha', quadratic, point, precision=HIGHEST_PRECISION)
    return linear_grad * feature ** (-0.25) + crossed * (0.5 / feature) ** 0.5

def backward_block(query_block, key_block, value_block, prefix, grad_sum, later):
    feature = query_block.shape[-1]
    sigma, causal, weights = kernel_block(query_block, key_block)
    grad_weights = jnp.einsum('thd,shd->hts', grad_sum, value_block, precision=HIGHEST_PRECISION)
    grad_sigma = rounded(jnp.where(causal[None], grad_weights * (feature ** (-0.5) + sigma / feature), 0.0))
    key_linear, key_square = feature_maps(key_block)
    grad_query = jnp.einsum('hts,shf->thf', grad_sigma, key_block, precision=HIGHEST_PRECISION) + feature_grad(query_block, grad_sum, prefix)
    grad_key = jnp.einsum('hts,thf->shf', grad_sigma, query_block, precision=HIGHEST_PRECISION) + feature_grad(key_block, value_block, later)
    grad_value = jnp.einsum('hts,thd->shd', weights, grad_sum, precision=HIGHEST_PRECISION) + carried_values(key_linear, key_square, later)
    return (grad_query, grad_key, grad_value)

def exclusive_sum(stack):
    running = jnp.cumsum(stack, axis=0)
    return jnp.concatenate([jnp.zeros_like(stack[:1]), running[:-1]], axis=0)

def reverse_exclusive(stack):
    return jnp.flip(exclusive_sum(jnp.flip(stack, 0)), 0)

def reference(query_in, key_in, value_in, conv_query, conv_key, conv_value, norm_gain, grad_out):
    length = query_in.shape[0]
    count = length // BLOCK
    query_wide = conv_input(query_in, conv_query.shape[0])
    key_wide = conv_input(key_in, conv_key.shape[0])
    value_wide = conv_input(value_in, conv_value.shape[0])
    query_round = rounded(conv_apply(query_wide, conv_query, length)).reshape(count, BLOCK, HEADS, FEAT)
    key_round = rounded(conv_apply(key_wide, conv_key, length)).reshape(count, BLOCK, HEADS, FEAT)
    value_round = rounded(conv_apply(value_wide, conv_value, length)).reshape(count, BLOCK, HEADS, HEAD_DIM)
    gain = norm_gain.reshape(HEADS, HEAD_DIM)
    grad_rows = grad_out.reshape(count, BLOCK, HEADS, HEAD_DIM)

    def key_pass(pieces):
        key_block, value_block = pieces
        linear, square = feature_maps(key_block)
        return block_states(linear, square, value_block)
    key_states = lax.map(key_pass, (key_round, value_round))
    prefixes = jax.tree.map(exclusive_sum, key_states)

    def forward_pass(pieces):
        query_block, key_block, value_block, prefix, grad_block = pieces
        summed, linear, square = numerator(query_block, key_block, value_block, prefix)
        output, grad_sum, gain_part = norm_pass(summed, gain, grad_block)
        return (output, grad_sum, gain_part, block_states(linear, square, grad_sum))
    outputs, grad_sums, gain_parts, grad_states = lax.map(forward_pass, (query_round, key_round, value_round, prefixes, grad_rows))
    laters = jax.tree.map(reverse_exclusive, grad_states)

    def backward_pass(pieces):
        query_block, key_block, value_block, prefix, grad_sum, later = pieces
        return backward_block(query_block, key_block, value_block, prefix, grad_sum, later)
    grad_query_conv, grad_key_conv, grad_value_conv = lax.map(backward_pass, (query_round, key_round, value_round, prefixes, grad_sums, laters))
    grad_query, taps_query = conv_grads(query_wide, conv_query, grad_query_conv.reshape(length, HEADS * FEAT))
    grad_key, taps_key = conv_grads(key_wide, conv_key, grad_key_conv.reshape(length, HEADS * FEAT))
    grad_value, taps_value = conv_grads(value_wide, conv_value, grad_value_conv.reshape(length, HEADS * HEAD_DIM))
    factor = length ** (-0.5)
    return (outputs.reshape(length, HEADS * HEAD_DIM).astype(jnp.bfloat16), grad_query.astype(jnp.bfloat16), grad_key.astype(jnp.bfloat16), grad_value.astype(jnp.bfloat16), taps_query * factor, taps_key * factor, taps_value * factor, lax.optimization_barrier(jnp.sum(gain_parts, axis=0)).reshape(HEADS * HEAD_DIM) * factor)
```

```python
import functools

import jax
import jax.numpy as jnp
from jax import lax
from jax.experimental import pallas as pl
from jax.experimental.pallas import tpu as pltpu
from jax.sharding import PartitionSpec as P

HEADS = 8
HALF = HEADS // 2
FEAT = 16
DIM = 128
EPSILON = 1e-06
LANES = HEADS * FEAT
WIDE = HEADS * DIM
ALL = 2 * LANES + WIDE
ROWS = 160
LIN = 128
TAIL = 144
RIM = 16
STEP = 128
F32 = jnp.float32
BF16 = jnp.bfloat16

NN = (((1,), (0,)), ((), ()))
NT = (((1,), (1,)), ((), ()))
TN = (((0,), (0,)), ((), ()))


def dot(a, b, dims):
    return lax.dot_general(a, b, dims, preferred_element_type=F32)


def head_rows(h):
    return slice(h * FEAT, (h + 1) * FEAT)


def head_lanes(h):
    return slice(h * DIM, (h + 1) * DIM)


def conv(wide_ref, taps, rows):
    margin = taps.shape[0] - 1
    total = taps[0:1] * wide_ref[RIM - margin : RIM - margin + rows]
    for o in range(1, margin + 1):
        total = total + taps[o : o + 1] * wide_ref[RIM - margin + o : RIM - margin + o + rows]
    return total


def tap_sums(grad, wide_ref, taps):
    rows = grad.shape[0]
    start = RIM - (taps - 1)
    return [
        jnp.sum(grad * wide_ref[start + o : start + o + rows], axis=0, keepdims=True)
        for o in range(taps)
    ]


def turned(x, shift):
    return x if shift % FEAT == 0 else pltpu.roll(x, shift % FEAT, 0)


def features(x):
    half = (0.5 / FEAT) ** 0.5
    pieces = [(x * turned(x, FEAT - d) * half).astype(BF16) for d in range(8)]
    pieces.append((x * FEAT ** (-0.25)).astype(BF16))
    rows = lax.broadcasted_iota(jnp.int32, (8, x.shape[1]), 0)
    one = jnp.where(rows == 0, 1.0, 0.0).astype(F32)
    pieces.append(jnp.concatenate([x[:8] * x[8:] * half, one], axis=0).astype(BF16))
    return jnp.concatenate(pieces, axis=0)


def feature_grad(x, state, vector):
    g = dot(state, vector, NT)
    crossed = 2.0 * g[0:FEAT] * x
    for d in range(1, 8):
        part = g[d * FEAT : (d + 1) * FEAT]
        crossed = crossed + part * turned(x, FEAT - d) + turned(part * x, d)
    part = g[TAIL : TAIL + 8]
    crossed = crossed + jnp.concatenate([part * x[8:], part * x[:8]], axis=0)
    return g[LIN:TAIL] * FEAT ** (-0.25) + crossed * (0.5 / FEAT) ** 0.5


def gather_state(own_ref, other_ref, state_ref):
    core = lax.rem(lax.axis_index("seq"), 2)
    rows = lax.broadcasted_iota(jnp.int32, (ROWS, DIM), 0)
    pair = ((rows >= FEAT) & (rows < LIN)) | ((rows >= TAIL) & (rows < TAIL + 8))
    weight = jnp.where(pair, 2.0, 1.0).astype(F32)
    for g in range(HALF):
        state_ref[core * HALF + g] = (own_ref[g].astype(F32) * weight).astype(BF16)
        state_ref[(1 - core) * HALF + g] = (other_ref[g].astype(F32) * weight).astype(BF16)


def hand_out(state_ref, keep_ref, send_ref):
    core = lax.rem(lax.axis_index("seq"), 2)
    keep_ref[...] = state_ref[pl.ds(core * HALF, HALF)]
    send_ref[...] = state_ref[pl.ds((1 - core) * HALF, HALF)]


def head_mask(h):
    lanes = lax.broadcasted_iota(jnp.int32, (1, LANES), 1)
    return jnp.where(lanes // FEAT == h, 1.0, 0.0).astype(F32).astype(BF16)


def key_kernel(key, value, rim, taps_k, taps_v, v_out, k_out, kt_out, fk_out, keep, send, wide, state):
    rows = key.shape[0]
    wide[0:RIM] = rim[:, LANES : 2 * LANES].astype(F32)
    wide[RIM : RIM + rows] = key[...].astype(F32)
    k = conv(wide, taps_k[...], rows).astype(BF16)
    k_out[...] = k
    kt = k.astype(F32).T
    kt_out[...] = kt.astype(BF16)
    for h in range(HEADS):
        f = features(kt[head_rows(h)])
        fk_out[h] = f
        wide[0:RIM] = rim[:, 2 * LANES + h * DIM : 2 * LANES + (h + 1) * DIM].astype(F32)
        wide[RIM : RIM + rows] = value[:, head_lanes(h)].astype(F32)
        v = conv(wide, taps_v[:, head_lanes(h)], rows).astype(BF16)
        v_out[:, head_lanes(h)] = v
        state[h] = dot(f, v, NN).astype(BF16)
    hand_out(state, keep, send)


def query_kernel(query, rim, taps_q, q_out, qt_out, fq_out, wide):
    rows = query.shape[0]
    wide[0:RIM] = rim[:, 0:LANES].astype(F32)
    wide[RIM : RIM + rows] = query[...].astype(F32)
    q = conv(wide, taps_q[...], rows).astype(BF16)
    q_out[...] = q
    qt = q.astype(F32).T
    qt_out[...] = qt.astype(BF16)
    for h in range(HEADS):
        fq_out[h] = features(qt[head_rows(h)])


def local_kernel(first, q_ref, k_ref, v_ref, out):
    rows = q_ref.shape[0]
    quarter = q_ref[...] * jnp.asarray(FEAT ** (-0.5), BF16)
    for g in range(HALF):
        qs = quarter * head_mask(first + g)
        for start in range(0, rows, STEP):
            stop = start + STEP
            t = dot(qs[start:stop], k_ref[0:stop], NT)
            w = (0.5 * t + 1.0) * t + 1.0
            at = lax.broadcasted_iota(jnp.int32, (STEP, stop), 0) + start
            w = jnp.where(at >= lax.broadcasted_iota(jnp.int32, (STEP, stop), 1), w, 0.0)
            out[start:stop, head_lanes(g)] = dot(
                w.astype(BF16), v_ref[0:stop, head_lanes(first + g)], NN
            )


def norm_kernel(low, high, fq, own, other, grad, gain, out, gs_out, keep, send, gain_out, pre, state):
    gather_state(own, other, pre)
    for h in range(HEADS):
        f = fq[h]
        local = (low if h < HALF else high)[:, head_lanes(h % HALF)]
        summed = local + dot(f, pre[h], TN)
        scale = lax.rsqrt(jnp.mean(summed * summed, axis=-1, keepdims=True) + EPSILON)
        normal = summed * scale
        weight = gain[h : h + 1]
        out[:, head_lanes(h)] = (normal * weight).astype(BF16)
        incoming = grad[:, head_lanes(h)].astype(F32)
        gain_out[h : h + 1] = jnp.sum(incoming * normal, axis=0, keepdims=True)
        upstream = incoming * weight
        gs = scale * (upstream - normal * jnp.mean(normal * upstream, axis=-1, keepdims=True))
        gs = gs.astype(BF16)
        gs_out[:, head_lanes(h)] = gs
        state[h] = dot(f, gs, NN).astype(BF16)
    hand_out(state, keep, send)


def back_kernel(first, q_ref, k_ref, qt_ref, kt_ref, v_ref, gs_ref, gv_out, gq_out, gk_out):
    rows = q_ref.shape[0]
    quarter = q_ref[...] * jnp.asarray(FEAT ** (-0.5), BF16)
    for g in range(HALF):
        h = first + g
        ks = k_ref[...] * head_mask(h)
        qt = qt_ref[head_rows(h)]
        kt = kt_ref[head_rows(h)]
        for start in range(0, rows, STEP):
            stop = start + STEP
            shape = (STEP, rows - start)
            t = dot(ks[start:stop], quarter[start:], NT)
            seen = lax.broadcasted_iota(jnp.int32, shape, 1) >= lax.broadcasted_iota(jnp.int32, shape, 0)
            w = jnp.where(seen, (0.5 * t + 1.0) * t + 1.0, 0.0).astype(BF16)
            gs = gs_ref[start:, head_lanes(h)]
            gv_out[start:stop, head_lanes(g)] = dot(w, gs, NN)
            gw = dot(v_ref[start:stop, head_lanes(h)], gs, NT)
            s = jnp.where(seen, gw * (FEAT ** (-0.5) + FEAT ** (-0.5) * t), 0.0).astype(BF16)
            part = dot(kt[:, start:stop], s, NN)
            if start == 0:
                gq_out[head_rows(g)] = part
            else:
                gq_out[head_rows(g), start:] += part
            gk_out[head_rows(g), start:stop] = dot(qt[:, start:], s, NT)


def query_grad_kernel(query, rim, qt_ref, gs_ref, own, other, low, high, taps_q, g_out, sums, wide, pre):
    rows = query.shape[0]
    gather_state(own, other, pre)
    pieces = []
    for h in range(HEADS):
        local = (low if h < HALF else high)[head_rows(h % HALF)]
        pieces.append(
            local + feature_grad(qt_ref[head_rows(h)].astype(F32), pre[h], gs_ref[:, head_lanes(h)])
        )
    grad = jnp.concatenate(pieces, axis=0).T
    g_out[...] = grad
    wide[0:RIM] = rim[:, 0:LANES].astype(F32)
    wide[RIM : RIM + rows] = query[...].astype(F32)
    for o, row in enumerate(tap_sums(grad, wide, taps_q.shape[0])):
        sums[o : o + 1] = row


def later_kernel(
    key, value, rim, kt_ref, fk, v_ref, own, other, gv_low, gv_high, gk_low, gk_high, gq, sums_q, gain_sum,
    gv_out, gk_out, head_out, sums, wide, post,
):
    rows = key.shape[0]
    taps = sums_q.shape[0]
    gather_state(own, other, post)
    pieces = []
    head_out[:, 0:LANES] = gq[...]
    sums[0:taps, 0:LANES] = sums_q[...]
    sums[taps : taps + 1, 0 : 2 * LANES] = jnp.zeros((1, 2 * LANES), F32)
    for h in range(HEADS):
        local = (gk_low if h < HALF else gk_high)[head_rows(h % HALF)]
        pieces.append(
            local + feature_grad(kt_ref[head_rows(h)].astype(F32), post[h], v_ref[:, head_lanes(h)])
        )
        local = (gv_low if h < HALF else gv_high)[:, head_lanes(h % HALF)]
        grad = local + dot(fk[h], post[h], TN)
        gv_out[:, head_lanes(h)] = grad
        place = slice(2 * LANES + h * DIM, 2 * LANES + (h + 1) * DIM)
        head_out[:, place] = grad[0:8]
        wide[0:RIM] = rim[:, place].astype(F32)
        wide[RIM : RIM + rows] = value[:, head_lanes(h)].astype(F32)
        for o, row in enumerate(tap_sums(grad, wide, taps)):
            sums[o : o + 1, place] = row
        sums[taps : taps + 1, place] = gain_sum[h : h + 1]
    grad = jnp.concatenate(pieces, axis=0).T
    gk_out[...] = grad
    head_out[:, LANES : 2 * LANES] = grad[0:8]
    wide[0:RIM] = rim[:, LANES : 2 * LANES].astype(F32)
    wide[RIM : RIM + rows] = key[...].astype(F32)
    for o, row in enumerate(tap_sums(grad, wide, taps)):
        sums[o : o + 1, LANES : 2 * LANES] = row


def signal_kernel(gq, gk, gv, follow, taps_q, taps_k, taps_v, q_out, k_out, v_out, wide):
    rows = gq.shape[0]
    count = taps_q.shape[0]

    def one(grad, place, taps):
        wide[0:rows] = grad
        wide[rows : rows + 8] = follow[:, place]
        total = taps[0:1] * wide[count - 1 : count - 1 + rows]
        for o in range(1, count):
            total = total + taps[o : o + 1] * wide[count - 1 - o : count - 1 - o + rows]
        return total.astype(BF16)

    q_out[...] = one(gq[...], slice(0, LANES), taps_q[...])
    k_out[...] = one(gk[...], slice(LANES, 2 * LANES), taps_k[...])
    for h in range(HEADS):
        place = slice(2 * LANES + h * DIM, 2 * LANES + (h + 1) * DIM)
        v_out[:, head_lanes(h)] = one(gv[:, head_lanes(h)], place, taps_v[:, head_lanes(h)])


def call(kernel, outs, scratch, args, flops, limit=24):
    size = lambda a: a.size * a.dtype.itemsize
    moved = sum(size(a) for a in args) + sum(size(o) for o in outs)
    return pl.pallas_call(
        kernel,
        out_shape=outs,
        scratch_shapes=scratch,
        compiler_params=pltpu.CompilerParams(vmem_limit_bytes=limit * 2**20),
        cost_estimate=pl.CostEstimate(flops=flops, bytes_accessed=moved, transcendentals=0),
    )(*args)


def exchange(x, distance):
    count = lax.axis_size("seq")
    return lax.ppermute(x, "seq", [(i, i ^ distance) for i in range(count)])


def beyond(keep, send, reverse):
    count, here = lax.axis_size("seq"), lax.axis_index("seq")

    def mine(bit):
        on = (here & bit) == 0 if reverse else (here & bit) != 0
        return jnp.where(on, 1.0, 0.0).astype(F32)

    near = exchange(send, 1)
    a, b = keep.astype(F32), near.astype(F32)
    total = a + b
    before = jnp.zeros_like(total)
    bit = 2
    while bit < count:
        got = exchange(total.astype(BF16), bit).astype(F32)
        before = before + mine(bit) * got
        total = total + got
        bit *= 2
    own = (before + mine(1) * b).astype(BF16)
    give = (before + (1.0 - mine(1)) * a).astype(BF16)
    return own, exchange(give, 1)


def shards(query_in, key_in, value_in, conv_query, conv_key, conv_value, norm_gain, grad_out):
    rows = query_in.shape[0]
    taps = conv_query.shape[0]
    count = lax.axis_size("seq")
    total_rows = rows * count
    st = jax.ShapeDtypeStruct
    half_state = st((HALF, ROWS, DIM), BF16)
    full_state = pltpu.VMEM((HEADS, ROWS, DIM), BF16)
    wide = pltpu.VMEM((RIM + rows, DIM), F32)
    gain = norm_gain.reshape(HEADS, DIM)
    state_flops = 2 * HEADS * ROWS * DIM * rows
    square_flops = 2 * HALF * rows * rows * DIM

    ends = jnp.concatenate([a[rows - RIM :] for a in (query_in, key_in, value_in)], axis=1)
    rim = lax.ppermute(ends, "seq", [(i, i + 1) for i in range(count - 1)])

    v, k, kt, fk, keep, send = call(
        key_kernel,
        [st((rows, WIDE), BF16), st((rows, LANES), BF16), st((LANES, rows), BF16), st((HEADS, ROWS, rows), BF16),
         half_state, half_state],
        [wide, full_state],
        (key_in, value_in, rim, conv_key, conv_value),
        state_flops,
    )
    q, qt, fq = call(
        query_kernel,
        [st((rows, LANES), BF16), st((LANES, rows), BF16), st((HEADS, ROWS, rows), BF16)],
        [wide],
        (query_in, rim, conv_query),
        state_flops,
    )
    local = [
        call(functools.partial(local_kernel, first), [st((rows, HALF * DIM), F32)], [], (q, k, v), 2 * square_flops)[0]
        for first in (0, HALF)
    ]
    own, other = beyond(keep, send, False)
    output, gs, keep, send, gain_sum = call(
        norm_kernel,
        [st((rows, WIDE), BF16), st((rows, WIDE), BF16), half_state, half_state, st((HEADS, DIM), F32)],
        [full_state, full_state],
        (*local, fq, own, other, grad_out, gain),
        2 * state_flops,
    )
    back = [
        call(
            functools.partial(back_kernel, first),
            [st((rows, HALF * DIM), F32), st((HALF * FEAT, rows), F32), st((HALF * FEAT, rows), F32)],
            [],
            (q, k, qt, kt, v, gs),
            4 * square_flops,
        )
        for first in (0, HALF)
    ]
    gq, sums_q = call(
        query_grad_kernel,
        [st((rows, LANES), F32), st((taps, LANES), F32)],
        [wide, full_state],
        (query_in, rim, qt, gs, own, other, back[0][1], back[1][1], conv_query),
        state_flops,
    )
    own, other = beyond(keep, send, True)
    gv, gk, heads, sums = call(
        later_kernel,
        [st((rows, WIDE), F32), st((rows, LANES), F32), st((8, ALL), F32), st((taps + 1, ALL), F32)],
        [wide, full_state],
        (key_in, value_in, rim, kt, fk, v, own, other, back[0][0], back[1][0], back[0][2], back[1][2],
         gq[0:8], sums_q, gain_sum),
        2 * state_flops,
    )
    follow = lax.ppermute(heads, "seq", [(i + 1, i) for i in range(count - 1)])
    bit = 1
    while bit < count:
        sums = sums + exchange(sums, bit)
        bit *= 2
    grad_query, grad_key, grad_value = call(
        signal_kernel,
        [st((rows, LANES), BF16), st((rows, LANES), BF16), st((rows, WIDE), BF16)],
        [pltpu.VMEM((rows + 8, DIM), F32)],
        (gq, gk, gv, follow, conv_query, conv_key, conv_value),
        state_flops,
    )
    sums = sums * total_rows ** (-0.5)
    return (
        output,
        grad_query,
        grad_key,
        grad_value,
        sums[0:taps, 0:LANES],
        sums[0:taps, LANES : 2 * LANES],
        sums[0:taps, 2 * LANES :],
        sums[taps, 2 * LANES :],
    )


def solution(mesh):
    rows = P(("groups", "seq"), None)
    return jax.shard_map(
        shards,
        mesh=mesh,
        in_specs=(rows, rows, rows, P(), P(), P(), P(), rows),
        out_specs=(rows, rows, rows, rows, P("groups", None), P("groups", None), P("groups", None), P("groups")),
        check_vma=False,
    )
```

```python
import functools

import jax
import jax.numpy as jnp
from jax import lax
from jax.experimental import pallas as pl
from jax.experimental.pallas import tpu as pltpu
from jax.sharding import PartitionSpec as P

HEADS = 8
HALF = HEADS // 2
PART = HEADS // 4
FEAT = 16
DIM = 128
EPSILON = 1e-06
LANES = HEADS * FEAT
WIDE = HEADS * DIM
ALL = 2 * LANES + WIDE
ROWS = 160
LIN = 128
TAIL = 144
RIM = 16
STEP = 128
F32 = jnp.float32
BF16 = jnp.bfloat16

NN = (((1,), (0,)), ((), ()))
NT = (((1,), (1,)), ((), ()))
TN = (((0,), (0,)), ((), ()))


def dot(a, b, dims):
    return lax.dot_general(a, b, dims, preferred_element_type=F32)


def head_rows(h):
    return slice(h * FEAT, (h + 1) * FEAT)


def head_lanes(h):
    return slice(h * DIM, (h + 1) * DIM)


def conv(wide_ref, taps, rows):
    margin = taps.shape[0] - 1
    total = taps[0:1] * wide_ref[RIM - margin : RIM - margin + rows]
    for o in range(1, margin + 1):
        total = total + taps[o : o + 1] * wide_ref[RIM - margin + o : RIM - margin + o + rows]
    return total


def tap_sums(grad, wide_ref, taps):
    rows = grad.shape[0]
    start = RIM - (taps - 1)
    return [
        jnp.sum(grad * wide_ref[start + o : start + o + rows], axis=0, keepdims=True)
        for o in range(taps)
    ]


def turned(x, shift):
    return x if shift % FEAT == 0 else pltpu.roll(x, shift % FEAT, 0)


def features(x):
    half = (0.5 / FEAT) ** 0.5
    pieces = [(x * turned(x, FEAT - d) * half).astype(BF16) for d in range(8)]
    pieces.append((x * FEAT ** (-0.25)).astype(BF16))
    rows = lax.broadcasted_iota(jnp.int32, (8, x.shape[1]), 0)
    one = jnp.where(rows == 0, 1.0, 0.0).astype(F32)
    pieces.append(jnp.concatenate([x[:8] * x[8:] * half, one], axis=0).astype(BF16))
    return jnp.concatenate(pieces, axis=0)


def feature_grad(x, state, vector):
    g = dot(state, vector, NT)
    crossed = 2.0 * g[0:FEAT] * x
    for d in range(1, 8):
        part = g[d * FEAT : (d + 1) * FEAT]
        crossed = crossed + part * turned(x, FEAT - d) + turned(part * x, d)
    part = g[TAIL : TAIL + 8]
    crossed = crossed + jnp.concatenate([part * x[8:], part * x[:8]], axis=0)
    return g[LIN:TAIL] * FEAT ** (-0.25) + crossed * (0.5 / FEAT) ** 0.5


def gather_state(own_ref, other_ref, state_ref):
    core = lax.rem(lax.axis_index("seq"), 2)
    rows = lax.broadcasted_iota(jnp.int32, (ROWS, DIM), 0)
    pair = ((rows >= FEAT) & (rows < LIN)) | ((rows >= TAIL) & (rows < TAIL + 8))
    weight = jnp.where(pair, 2.0, 1.0).astype(F32)
    for g in range(HALF):
        state_ref[core * HALF + g] = (own_ref[g].astype(F32) * weight).astype(BF16)
        state_ref[(1 - core) * HALF + g] = (other_ref[g].astype(F32) * weight).astype(BF16)


def hand_out(state_ref, keep_ref, send_ref):
    core = lax.rem(lax.axis_index("seq"), 2)
    keep_ref[...] = state_ref[pl.ds(core * HALF, HALF)]
    send_ref[...] = state_ref[pl.ds((1 - core) * HALF, HALF)]


def head_mask(h):
    lanes = lax.broadcasted_iota(jnp.int32, (1, LANES), 1)
    return jnp.where(lanes // FEAT == h, 1.0, 0.0).astype(F32).astype(BF16)


def end_kernel(query, key, value, out, sems):
    start = query.shape[0] - RIM
    copies = [
        pltpu.make_async_copy(ref.at[pl.ds(start, RIM)], out.at[:, pl.ds(lane, ref.shape[1])], sems.at[i])
        for i, (ref, lane) in enumerate(((query, 0), (key, LANES), (value, 2 * LANES)))
    ]
    for copy in copies:
        copy.start()
    for copy in copies:
        copy.wait()


def key_kernel(
    key_far, value_far, rim, taps_k, taps_v, v_out, k_out, kt_out, fk_out, keep, send, wide, state, key, value, sems
):
    rows = key.shape[0]
    key_copy = pltpu.make_async_copy(key_far, key, sems.at[0])
    value_copy = pltpu.make_async_copy(value_far, value, sems.at[1])
    key_copy.start()
    value_copy.start()
    key_copy.wait()
    wide[0:RIM] = rim[:, LANES : 2 * LANES].astype(F32)
    wide[RIM : RIM + rows] = key[...].astype(F32)
    k = conv(wide, taps_k[...], rows).astype(BF16)
    k_out[...] = k
    kt = k.astype(F32).T
    kt_out[...] = kt.astype(BF16)
    for h in range(HEADS):
        fk_out[h] = features(kt[head_rows(h)])
    value_copy.wait()
    for h in range(HEADS):
        f = fk_out[h]
        wide[0:RIM] = rim[:, 2 * LANES + h * DIM : 2 * LANES + (h + 1) * DIM].astype(F32)
        wide[RIM : RIM + rows] = value[:, head_lanes(h)].astype(F32)
        v = conv(wide, taps_v[:, head_lanes(h)], rows).astype(BF16)
        v_out[:, head_lanes(h)] = v
        state[h] = dot(f, v, NN).astype(BF16)
    hand_out(state, keep, send)


def query_kernel(query, rim, taps_q, q_out, qt_out, fq_out, wide):
    rows = query.shape[0]
    wide[0:RIM] = rim[:, 0:LANES].astype(F32)
    wide[RIM : RIM + rows] = query[...].astype(F32)
    q = conv(wide, taps_q[...], rows).astype(BF16)
    q_out[...] = q
    qt = q.astype(F32).T
    qt_out[...] = qt.astype(BF16)
    for h in range(HEADS):
        fq_out[h] = features(qt[head_rows(h)])


def local_kernel(first, q_ref, k_ref, v_ref, out):
    rows = q_ref.shape[0]
    quarter = q_ref[...] * jnp.asarray(FEAT ** (-0.5), BF16)
    for g in range(HALF):
        qs = quarter * head_mask(first + g)
        for start in range(0, rows, STEP):
            stop = start + STEP
            t = dot(qs[start:stop], k_ref[0:stop], NT)
            w = (0.5 * t + 1.0) * t + 1.0
            at = lax.broadcasted_iota(jnp.int32, (STEP, stop), 0) + start
            w = jnp.where(at >= lax.broadcasted_iota(jnp.int32, (STEP, stop), 1), w, 0.0)
            out[start:stop, head_lanes(g)] = dot(
                w.astype(BF16), v_ref[0:stop, head_lanes(first + g)], NN
            )


def norm_kernel(low, high, fq, own, other, grad, gain, out, gs_out, keep, send, gain_out, pre, state):
    gather_state(own, other, pre)
    for h in range(HEADS):
        f = fq[h]
        local = (low if h < HALF else high)[:, head_lanes(h % HALF)]
        summed = local + dot(f, pre[h], TN)
        scale = lax.rsqrt(jnp.mean(summed * summed, axis=-1, keepdims=True) + EPSILON)
        normal = summed * scale
        weight = gain[h : h + 1]
        out[:, head_lanes(h)] = (normal * weight).astype(BF16)
        incoming = grad[:, head_lanes(h)].astype(F32)
        gain_out[h : h + 1] = jnp.sum(incoming * normal, axis=0, keepdims=True)
        upstream = incoming * weight
        gs = scale * (upstream - normal * jnp.mean(normal * upstream, axis=-1, keepdims=True))
        gs = gs.astype(BF16)
        gs_out[:, head_lanes(h)] = gs
        state[h] = dot(f, gs, NN).astype(BF16)
    hand_out(state, keep, send)


def back_kernel(first, q_ref, k_ref, qt_ref, kt_ref, v_ref, gs_ref, gv_out, gq_out, gk_out):
    rows = q_ref.shape[0]
    quarter = q_ref[...] * jnp.asarray(FEAT ** (-0.5), BF16)
    for g in range(PART):
        h = first + g
        ks = k_ref[...] * head_mask(h)
        qt = qt_ref[head_rows(h)]
        kt = kt_ref[head_rows(h)]
        for start in range(0, rows, STEP):
            stop = start + STEP
            shape = (STEP, rows - start)
            t = dot(ks[start:stop], quarter[start:], NT)
            seen = lax.broadcasted_iota(jnp.int32, shape, 1) >= lax.broadcasted_iota(jnp.int32, shape, 0)
            w = jnp.where(seen, (0.5 * t + 1.0) * t + 1.0, 0.0).astype(BF16)
            gs = gs_ref[start:, head_lanes(h)]
            gv_out[start:stop, head_lanes(g)] = dot(w, gs, NN)
            gw = dot(v_ref[start:stop, head_lanes(h)], gs, NT)
            s = jnp.where(seen, gw * (FEAT ** (-0.5) + FEAT ** (-0.5) * t), 0.0).astype(BF16)
            part = dot(kt[:, start:stop], s, NN)
            if start == 0:
                gq_out[head_rows(g)] = part
            else:
                gq_out[head_rows(g), start:] += part
            gk_out[head_rows(g), start:stop] = dot(qt[:, start:], s, NT)


def query_grad_kernel(query, rim, qt_ref, gs_ref, own, other, l0, l1, l2, l3, taps_q, g_out, sums, wide, pre):
    rows = query.shape[0]
    locals_ = (l0, l1, l2, l3)
    gather_state(own, other, pre)
    pieces = []
    for h in range(HEADS):
        local = locals_[h // PART][head_rows(h % PART)]
        pieces.append(
            local + feature_grad(qt_ref[head_rows(h)].astype(F32), pre[h], gs_ref[:, head_lanes(h)])
        )
    grad = jnp.concatenate(pieces, axis=0).T
    g_out[...] = grad
    wide[0:RIM] = rim[:, 0:LANES].astype(F32)
    wide[RIM : RIM + rows] = query[...].astype(F32)
    for o, row in enumerate(tap_sums(grad, wide, taps_q.shape[0])):
        sums[o : o + 1] = row


def later_kernel(
    key, value, rim, kt_ref, fk, v_ref, own, other, v0, v1, v2, v3, k0, k1, k2, k3, gq, sums_q, gain_sum,
    gv_out, gk_out, head_out, sums, wide, post,
):
    rows = key.shape[0]
    taps = sums_q.shape[0]
    value_parts, key_parts = (v0, v1, v2, v3), (k0, k1, k2, k3)
    gather_state(own, other, post)
    pieces = []
    head_out[:, 0:LANES] = gq[0:8]
    sums[0:taps, 0:LANES] = sums_q[...]
    sums[taps : taps + 1, 0 : 2 * LANES] = jnp.zeros((1, 2 * LANES), F32)
    for h in range(HEADS):
        local = key_parts[h // PART][head_rows(h % PART)]
        pieces.append(
            local + feature_grad(kt_ref[head_rows(h)].astype(F32), post[h], v_ref[:, head_lanes(h)])
        )
        local = value_parts[h // PART][:, head_lanes(h % PART)]
        grad = local + dot(fk[h], post[h], TN)
        gv_out[:, head_lanes(h)] = grad
        place = slice(2 * LANES + h * DIM, 2 * LANES + (h + 1) * DIM)
        head_out[:, place] = grad[0:8]
        wide[0:RIM] = rim[:, place].astype(F32)
        wide[RIM : RIM + rows] = value[:, head_lanes(h)].astype(F32)
        for o, row in enumerate(tap_sums(grad, wide, taps)):
            sums[o : o + 1, place] = row
        sums[taps : taps + 1, place] = gain_sum[h : h + 1]
    grad = jnp.concatenate(pieces, axis=0).T
    gk_out[...] = grad
    head_out[:, LANES : 2 * LANES] = grad[0:8]
    wide[0:RIM] = rim[:, LANES : 2 * LANES].astype(F32)
    wide[RIM : RIM + rows] = key[...].astype(F32)
    for o, row in enumerate(tap_sums(grad, wide, taps)):
        sums[o : o + 1, LANES : 2 * LANES] = row


def signal_kernel(gq, gk, gv, follow, taps_q, taps_k, taps_v, q_out, k_out, v_out, wide):
    rows = gq.shape[0]
    count = taps_q.shape[0]

    def one(grad, place, taps):
        wide[0:rows] = grad
        wide[rows : rows + 8] = follow[:, place]
        total = taps[0:1] * wide[count - 1 : count - 1 + rows]
        for o in range(1, count):
            total = total + taps[o : o + 1] * wide[count - 1 - o : count - 1 - o + rows]
        return total.astype(BF16)

    q_out[...] = one(gq[...], slice(0, LANES), taps_q[...])
    k_out[...] = one(gk[...], slice(LANES, 2 * LANES), taps_k[...])
    for h in range(HEADS):
        place = slice(2 * LANES + h * DIM, 2 * LANES + (h + 1) * DIM)
        v_out[:, head_lanes(h)] = one(gv[:, head_lanes(h)], place, taps_v[:, head_lanes(h)])


def finish_kernel(factor, sums, got, q_out, k_out, v_out, gain_out):
    taps = q_out.shape[0]
    total = (sums[...] + got[...]) * factor
    q_out[...] = total[0:taps, 0:LANES]
    k_out[...] = total[0:taps, LANES : 2 * LANES]
    v_out[...] = total[0:taps, 2 * LANES :]
    gain_out[...] = total[taps : taps + 1, 2 * LANES :]


def far(x):
    return pltpu.with_memory_space_constraint(x, pltpu.HBM)


def held(*xs):
    return [pltpu.with_memory_space_constraint(x, pltpu.VMEM) for x in xs]


def call(kernel, outs, scratch, args, flops, limit=16, loose=(), **specs):
    size = lambda a: a.size * a.dtype.itemsize
    moved = sum(size(a) for a in args) + sum(size(o) for o in outs)
    return pl.pallas_call(
        kernel,
        out_shape=[o if i in loose else pltpu.VMEM(o.shape, o.dtype) for i, o in enumerate(outs)],
        scratch_shapes=scratch,
        compiler_params=pltpu.CompilerParams(vmem_limit_bytes=limit * 2**20),
        cost_estimate=pl.CostEstimate(flops=flops, bytes_accessed=moved, transcendentals=0),
        **specs,
    )(*args)


def exchange(x, distance):
    count = lax.axis_size("seq")
    return lax.ppermute(x, "seq", [(i, i ^ distance) for i in range(count)])


def tie(x, *others):
    return lax.optimization_barrier((x, *others))[0]


def on_side(bit, reverse):
    set_ = lax.rem(lax.div(lax.axis_index("seq"), bit), 2)
    return set_ == (0 if reverse else 1)


def chosen(flag, x):
    return jnp.where(flag, x, jnp.zeros_like(x))


def pair_kernel(keep, near, part, their):
    upper = lax.rem(lax.div(lax.axis_index("seq"), 2), 2)

    def half(which):
        place = pl.ds(which * PART, PART)
        return keep[place].astype(F32) + near[place].astype(F32)

    part[...] = half(upper)
    their[...] = half(1 - upper).astype(BF16)


def step_kernel(total, got, new, send):
    both = total[...] + got[...].astype(F32)
    new[...] = both
    send[...] = both.astype(BF16)


def part_kernel(reverse, part, got_y, *rest):
    *gots, own, give = rest
    before = jnp.zeros(part.shape, F32)
    for i, got in enumerate(gots):
        before = before + chosen(on_side(4 << i, reverse), got[...].astype(F32))
    own[...] = before + chosen(on_side(2, reverse), got_y[...].astype(F32))
    give[...] = (before + chosen(jnp.logical_not(on_side(2, reverse)), part[...])).astype(BF16)


def merge_kernel(reverse, own_part, other_part, keep, near, own, give):
    upper = lax.rem(lax.div(lax.axis_index("seq"), 2), 2)
    side = on_side(1, reverse)
    for part, which in ((own_part, upper), (other_part, 1 - upper)):
        place = pl.ds(which * PART, PART)
        before = part[...].astype(F32)
        own[place] = (before + chosen(side, near[place].astype(F32))).astype(BF16)
        give[place] = (before + chosen(jnp.logical_not(side), keep[place].astype(F32))).astype(BF16)


def beyond(keep, send, reverse, works):
    count = lax.axis_size("seq")
    works = list(works)
    st = jax.ShapeDtypeStruct
    whole, part_shape = keep.shape, (PART, *keep.shape[1:])
    wide, narrow = st(part_shape, F32), st(part_shape, BF16)
    cost = 4 * keep.size

    def under(x):
        return tie(x, works.pop(0)()) if works else x

    near = exchange(send, 1)
    part, their = call(pair_kernel, [wide, narrow], [], (keep, near), cost)
    got_y = exchange(their, 2)
    total, gots, got = part, [], got_y
    bit = 4
    while bit < count:
        total, send = call(step_kernel, [wide, narrow], [], (total, got), cost)
        got = exchange(under(send), bit)
        gots.append(got)
        bit *= 2
    own_part, give_part = call(
        functools.partial(part_kernel, reverse), [wide, narrow], [], (part, got_y, *gots), cost
    )
    other_part = exchange(under(give_part), 2)
    own, give = call(
        functools.partial(merge_kernel, reverse), [st(whole, BF16)] * 2, [], (own_part, other_part, keep, near), cost
    )
    other = exchange(under(give), 1)
    while works:
        other = under(other)
    return own, other


def shards(query_in, key_in, value_in, conv_query, conv_key, conv_value, norm_gain, grad_out):
    rows = query_in.shape[0]
    taps = conv_query.shape[0]
    count = lax.axis_size("seq")
    total_rows = rows * count
    st = jax.ShapeDtypeStruct
    half_state = st((HALF, ROWS, DIM), BF16)
    full_state = pltpu.VMEM((HEADS, ROWS, DIM), BF16)
    wide = pltpu.VMEM((RIM + rows, DIM), F32)
    gain = norm_gain.reshape(HEADS, DIM)
    state_flops = 2 * HEADS * ROWS * DIM * rows
    square_flops = 2 * HALF * rows * rows * DIM

    apart = pl.BlockSpec(memory_space=pltpu.HBM)
    near = pl.BlockSpec(memory_space=pltpu.VMEM)
    ends = call(
        end_kernel,
        [st((RIM, ALL), BF16)],
        [pltpu.SemaphoreType.DMA((3,))],
        (far(query_in), far(key_in), far(value_in)),
        rows,
        in_specs=[apart] * 3,
    )[0]
    rim = lax.ppermute(ends, "seq", [(i, i + 1) for i in range(count - 1)])

    v, k, kt, fk, keep, send = call(
        key_kernel,
        [st((rows, WIDE), BF16), st((rows, LANES), BF16), st((LANES, rows), BF16), st((HEADS, ROWS, rows), BF16),
         half_state, half_state],
        [wide, full_state, pltpu.VMEM((rows, LANES), BF16), pltpu.VMEM((rows, WIDE), BF16),
         pltpu.SemaphoreType.DMA((2,))],
        (far(key_in), far(value_in), rim, conv_key, conv_value),
        state_flops,
        in_specs=[apart, apart, near, near, near],
    )

    made = {}

    def query_work():
        made["q"] = call(
            query_kernel,
            [st((rows, LANES), BF16), st((LANES, rows), BF16), st((HEADS, ROWS, rows), BF16)],
            [wide],
            (query_in, rim, conv_query),
            state_flops,
        )
        return local_work(0)()

    def local_work(first):
        def work():
            made["local", first] = call(
                functools.partial(local_kernel, first),
                [st((rows, HALF * DIM), F32)],
                [],
                held(made["q"][0], k, v),
                2 * HALF * rows * rows * DIM,
            )[0]
            return made["local", first]

        return work

    own, other = beyond(keep, send, False, [query_work, local_work(HALF)])
    q, qt, fq = made["q"]
    output, gs, keep, send, gain_sum = call(
        norm_kernel,
        [st((rows, WIDE), BF16), st((rows, WIDE), BF16), half_state, half_state, st((HEADS, DIM), F32)],
        [full_state, full_state],
        (*held(made["local", 0], made["local", HALF], fq), own, other, grad_out, gain),
        2 * state_flops,
        loose=(0,),
    )
    back = []

    def back_work():
        back.append(
            call(
                functools.partial(back_kernel, len(back) * PART),
                [st((rows, PART * DIM), F32), st((PART * FEAT, rows), F32), st((PART * FEAT, rows), F32)],
                [],
                held(q, k, qt, kt, v, gs),
                4 * PART * rows * rows * DIM,
            )
        )
        return back[-1][0]

    def query_grad_work():
        made["gq"] = call(
            query_grad_kernel,
            [st((rows, LANES), F32), st((taps, LANES), F32)],
            [wide, full_state],
            (query_in, rim, *held(qt, gs), before[0], before[1], *held(*[b[1] for b in back]), conv_query),
            state_flops,
        )
        return made["gq"][0]

    before = (own, other)
    own, other = beyond(keep, send, True, [back_work] * 4 + [query_grad_work])
    gq, sums_q = made["gq"]
    gv, gk, heads, sums = call(
        later_kernel,
        [st((rows, WIDE), F32), st((rows, LANES), F32), st((8, ALL), F32), st((taps + 1, ALL), F32)],
        [wide, full_state],
        (key_in, value_in, rim, *held(kt, fk, v), own, other,
         *held(*[b[0] for b in back], *[b[2] for b in back], gq, sums_q, gain_sum)),
        2 * state_flops,
    )
    follow = lax.ppermute(heads, "seq", [(i + 1, i) for i in range(count - 1)])
    got = exchange(sums, 1)
    bit = 2
    while bit < count:
        sums = sums + got
        if bit == count // 2:
            grad_query, grad_key, grad_value = call(
                signal_kernel,
                [st((rows, LANES), BF16), st((rows, LANES), BF16), st((rows, WIDE), BF16)],
                [pltpu.VMEM((rows + 8, DIM), F32)],
                (*held(gq, gk, gv), follow, conv_query, conv_key, conv_value),
                state_flops,
                loose=(0, 1, 2),
            )
            sums = tie(sums, grad_value)
        got = exchange(sums, bit)
        bit *= 2
    taps_query, taps_key, taps_value, taps_gain = call(
        functools.partial(finish_kernel, total_rows ** (-0.5)),
        [st((taps, LANES), F32), st((taps, LANES), F32), st((taps, WIDE), F32), st((1, WIDE), F32)],
        [],
        (sums, got),
        rows,
        loose=(0, 1, 2, 3),
    )
    return (
        output,
        grad_query,
        grad_key,
        grad_value,
        taps_query,
        taps_key,
        taps_value,
        taps_gain.reshape(WIDE),
    )


def solution(mesh):
    rows = P(("groups", "seq"), None)
    return jax.shard_map(
        shards,
        mesh=mesh,
        in_specs=(rows, rows, rows, P(), P(), P(), P(), rows),
        out_specs=(rows, rows, rows, rows, P("groups", None), P("groups", None), P("groups", None), P("groups")),
        check_vma=False,
    )
```

```python
import functools

import jax
import jax.numpy as jnp
from jax import lax
from jax.experimental import pallas as pl
from jax.experimental.pallas import tpu as pltpu
from jax.sharding import PartitionSpec as P

HEADS = 8
HALF = HEADS // 2
PART = HEADS // 4
FEAT = 16
DIM = 128
EPSILON = 1e-06
LANES = HEADS * FEAT
WIDE = HEADS * DIM
ALL = 2 * LANES + WIDE
ROWS = 160
LIN = 128
TAIL = 144
RIM = 16
STEP = 128
F32 = jnp.float32
BF16 = jnp.bfloat16

NN = (((1,), (0,)), ((), ()))
NT = (((1,), (1,)), ((), ()))
TN = (((0,), (0,)), ((), ()))


def dot(a, b, dims):
    return lax.dot_general(a, b, dims, preferred_element_type=F32)


def head_rows(h):
    return slice(h * FEAT, (h + 1) * FEAT)


def head_lanes(h):
    return slice(h * DIM, (h + 1) * DIM)


def conv(wide_ref, taps, rows):
    margin = taps.shape[0] - 1
    total = taps[0:1] * wide_ref[RIM - margin : RIM - margin + rows]
    for o in range(1, margin + 1):
        total = total + taps[o : o + 1] * wide_ref[RIM - margin + o : RIM - margin + o + rows]
    return total


def tap_sums(grad, wide_ref, taps):
    rows = grad.shape[0]
    start = RIM - (taps - 1)
    return [
        jnp.sum(grad * wide_ref[start + o : start + o + rows], axis=0, keepdims=True)
        for o in range(taps)
    ]


def turned(x, shift):
    return x if shift % FEAT == 0 else pltpu.roll(x, shift % FEAT, 0)


def features(x):
    half = (0.5 / FEAT) ** 0.5
    pieces = [(x * turned(x, FEAT - d) * half).astype(BF16) for d in range(8)]
    pieces.append((x * FEAT ** (-0.25)).astype(BF16))
    rows = lax.broadcasted_iota(jnp.int32, (8, x.shape[1]), 0)
    one = jnp.where(rows == 0, 1.0, 0.0).astype(F32)
    pieces.append(jnp.concatenate([x[:8] * x[8:] * half, one], axis=0).astype(BF16))
    return jnp.concatenate(pieces, axis=0)


def feature_grad(x, state, vector):
    g = dot(state, vector, NT)
    crossed = 2.0 * g[0:FEAT] * x
    for d in range(1, 8):
        part = g[d * FEAT : (d + 1) * FEAT]
        crossed = crossed + part * turned(x, FEAT - d) + turned(part * x, d)
    part = g[TAIL : TAIL + 8]
    crossed = crossed + jnp.concatenate([part * x[8:], part * x[:8]], axis=0)
    return g[LIN:TAIL] * FEAT ** (-0.25) + crossed * (0.5 / FEAT) ** 0.5


def half_index(own):
    core = lax.rem(lax.axis_index("seq"), 2)
    return core if own else 1 - core


def rows_of(half, g):
    return pl.ds(pl.multiple_of((half * HALF + g) * FEAT, FEAT), FEAT)


def lanes_of(half, g, start=0):
    return pl.ds(pl.multiple_of(start + (half * HALF + g) * DIM, DIM), DIM)


def doubled(state_ref, out_ref):
    rows = lax.broadcasted_iota(jnp.int32, (ROWS, DIM), 0)
    pair = ((rows >= FEAT) & (rows < LIN)) | ((rows >= TAIL) & (rows < TAIL + 8))
    weight = jnp.where(pair, 2.0, 1.0).astype(F32)
    for g in range(HALF):
        out_ref[g] = (state_ref[g].astype(F32) * weight).astype(BF16)


def head_mask(h):
    lanes = lax.broadcasted_iota(jnp.int32, (1, LANES), 1)
    return jnp.where(lanes // FEAT == h, 1.0, 0.0).astype(F32).astype(BF16)


def fill(wide, rim, rest):
    wide[0:RIM] = rim.astype(F32)
    wide[RIM : RIM + rest.shape[0]] = rest.astype(F32)


def end_kernel(query, key, value, out, sems):
    start = query.shape[0] - RIM
    copies = [
        pltpu.make_async_copy(ref.at[pl.ds(start, RIM)], out.at[:, pl.ds(lane, ref.shape[1])], sems.at[i])
        for i, (ref, lane) in enumerate(((query, 0), (key, LANES), (value, 2 * LANES)))
    ]
    for copy in copies:
        copy.start()
    for copy in copies:
        copy.wait()


def value_states(half, kt, value, rim, taps_v, v_out, f_out, state_out, wide):
    rows = value.shape[0]
    for g in range(HALF):
        f_out[g] = features(kt[rows_of(half, g)].astype(F32))
    for g in range(HALF):
        fill(wide, rim[:, lanes_of(half, g, 2 * LANES)], value[:, lanes_of(half, g)])
        v_out[:, head_lanes(g)] = conv(wide, taps_v[:, lanes_of(half, g)], rows).astype(BF16)
    for g in range(HALF):
        state_out[g] = dot(f_out[g], v_out[:, head_lanes(g)], NN).astype(BF16)


def first_key_kernel(key, value, rim, taps_k, taps_v, k_out, kt_out, v_out, f_out, state_out, wide):
    rows = key.shape[0]
    fill(wide, rim[:, LANES : 2 * LANES], key[...])
    k = conv(wide, taps_k[...], rows).astype(BF16)
    k_out[...] = k
    kt_out[...] = k.astype(F32).T.astype(BF16)
    value_states(half_index(False), kt_out, value, rim, taps_v, v_out, f_out, state_out, wide)


def second_key_kernel(kt, value, rim, taps_v, v_out, f_out, state_out, wide):
    value_states(half_index(True), kt, value, rim, taps_v, v_out, f_out, state_out, wide)


def query_kernel(query, rim, taps_q, q_out, qt_out, fq_out, wide):
    rows = query.shape[0]
    fill(wide, rim[:, 0:LANES], query[...])
    q = conv(wide, taps_q[...], rows).astype(BF16)
    q_out[...] = q
    qt = q.astype(F32).T
    qt_out[...] = qt.astype(BF16)
    for h in range(HEADS):
        fq_out[h] = features(qt[head_rows(h)])


def local_kernel(own, q_ref, k_ref, v_ref, out):
    rows = q_ref.shape[0]
    half = half_index(own)
    quarter = q_ref[...] * jnp.asarray(FEAT ** (-0.5), BF16)
    for g in range(HALF):
        qs = quarter * head_mask(half * HALF + g)
        for start in range(0, rows, STEP):
            stop = start + STEP
            t = dot(qs[start:stop], k_ref[0:stop], NT)
            w = (0.5 * t + 1.0) * t + 1.0
            at = lax.broadcasted_iota(jnp.int32, (STEP, stop), 0) + start
            w = jnp.where(at >= lax.broadcasted_iota(jnp.int32, (STEP, stop), 1), w, 0.0)
            out[start:stop, head_lanes(g)] = dot(w.astype(BF16), v_ref[0:stop, head_lanes(g)], NN)


def norm_kernel(own, local, fq, prefix, grad, gain, out, gs_out, state_out, gain_out, pre, summed_ref):
    half = half_index(own)
    doubled(prefix, pre)
    for g in range(HALF):
        place = head_lanes(g)
        summed_ref[:, place] = local[:, place] + dot(fq[half * HALF + g], pre[g], TN)
    for g in range(HALF):
        place = head_lanes(g)
        summed = summed_ref[:, place]
        scale = lax.rsqrt(jnp.mean(summed * summed, axis=-1, keepdims=True) + EPSILON)
        normal = summed * scale
        weight = gain[pl.ds(half * HALF + g, 1)]
        out[:, place] = (normal * weight).astype(BF16)
        incoming = grad[:, lanes_of(half, g)].astype(F32)
        gain_out[g : g + 1] = jnp.sum(incoming * normal, axis=0, keepdims=True)
        upstream = incoming * weight
        gs = scale * (upstream - normal * jnp.mean(normal * upstream, axis=-1, keepdims=True))
        gs = gs.astype(BF16)
        gs_out[:, place] = gs
        state_out[g] = dot(fq[half * HALF + g], gs, NN).astype(BF16)


def back_kernel(own, part, q_ref, k_ref, qt_ref, kt_ref, v_ref, gs_ref, gv_out, gq_out, gk_out):
    rows = q_ref.shape[0]
    half = half_index(own)
    quarter = q_ref[...] * jnp.asarray(FEAT ** (-0.5), BF16)
    for i in range(PART):
        g = part * PART + i
        ks = k_ref[...] * head_mask(half * HALF + g)
        qt = qt_ref[rows_of(half, g)]
        kt = kt_ref[rows_of(half, g)]
        for start in range(0, rows, STEP):
            stop = start + STEP
            shape = (STEP, rows - start)
            t = dot(ks[start:stop], quarter[start:], NT)
            seen = lax.broadcasted_iota(jnp.int32, shape, 1) >= lax.broadcasted_iota(jnp.int32, shape, 0)
            w = jnp.where(seen, (0.5 * t + 1.0) * t + 1.0, 0.0).astype(BF16)
            gs = gs_ref[start:, head_lanes(g)]
            gv_out[start:stop, head_lanes(i)] = dot(w, gs, NN)
            gw = dot(v_ref[start:stop, head_lanes(g)], gs, NT)
            s = jnp.where(seen, gw * (FEAT ** (-0.5) + FEAT ** (-0.5) * t), 0.0).astype(BF16)
            part_q = dot(kt[:, start:stop], s, NN)
            if start == 0:
                gq_out[head_rows(i)] = part_q
            else:
                gq_out[head_rows(i), start:] += part_q
            gk_out[head_rows(i), start:stop] = dot(qt[:, start:], s, NT)


def query_grad_kernel(
    query, rim, qt_ref, gs_a, gs_b, pre_a, pre_b, a0, a1, b0, b1, taps_q, g_out, sums, wide, pre, turned_grad
):
    for own, gs, prefix, locals_ in ((True, gs_a, pre_a, (a0, a1)), (False, gs_b, pre_b, (b0, b1))):
        half = half_index(own)
        doubled(prefix, pre)
        for g in range(HALF):
            x = qt_ref[rows_of(half, g)].astype(F32)
            turned_grad[rows_of(half, g)] = locals_[g // PART][head_rows(g % PART)] + feature_grad(
                x, pre[g], gs[:, head_lanes(g)]
            )
    grad = turned_grad[...].T
    g_out[...] = grad
    fill(wide, rim[:, 0:LANES], query[...])
    for o, row in enumerate(tap_sums(grad, wide, taps_q.shape[0])):
        sums[o : o + 1] = row


def later_half(half, value, rim, kt, fk, v, state, locals_v, locals_k, gv_out, gk_put, sums_put, wide, post, taps):
    doubled(state, post)
    for g in range(HALF):
        local = locals_v[g // PART][:, head_lanes(g % PART)]
        gv_out[:, head_lanes(g)] = local + dot(fk[g], post[g], TN)
    for g in range(HALF):
        local = locals_k[g // PART][head_rows(g % PART)]
        x = kt[rows_of(half, g)].astype(F32)
        gk_put(g, local + feature_grad(x, post[g], v[:, head_lanes(g)]))
    for g in range(HALF):
        fill(wide, rim[:, lanes_of(half, g, 2 * LANES)], value[:, lanes_of(half, g)])
        for o, row in enumerate(tap_sums(gv_out[:, head_lanes(g)], wide, taps)):
            sums_put(o, g, row)


def first_later_kernel(value, rim, kt, fk, v, state, v0, v1, k0, k1, gv_out, gk_out, sums, wide, post):
    def gk_put(g, x):
        gk_out[head_rows(g)] = x

    def sums_put(o, g, row):
        sums[o : o + 1, head_lanes(g)] = row

    later_half(
        half_index(False), value, rim, kt, fk, v, state, (v0, v1), (k0, k1), gv_out, gk_put, sums_put, wide, post,
        sums.shape[0],
    )


def second_later_kernel(
    key, value, rim, kt, fk, v, state, v0, v1, k0, k1, gv_b, gk_b, sums_b, gq, sums_q, gain_a, gain_b,
    gv_out, gk_out, head_out, sums, wide, post, turned_grad,
):
    taps = sums_q.shape[0]
    rows = key.shape[0]
    half_a, half_b = half_index(True), half_index(False)

    def gk_put(g, x):
        turned_grad[rows_of(half_a, g)] = x

    def sums_put(o, g, row):
        sums[o : o + 1, lanes_of(half_a, g, 2 * LANES)] = row

    turned_grad[pl.ds(pl.multiple_of(half_b * HALF * FEAT, HALF * FEAT), HALF * FEAT)] = gk_b[...]
    later_half(
        half_a, value, rim, kt, fk, v, state, (v0, v1), (k0, k1), gv_out, gk_put, sums_put, wide, post, taps
    )
    grad = turned_grad[...].T
    gk_out[...] = grad
    fill(wide, rim[:, LANES : 2 * LANES], key[...])
    for o, row in enumerate(tap_sums(grad, wide, taps)):
        sums[o : o + 1, LANES : 2 * LANES] = row
    sums[0:taps, 0:LANES] = sums_q[...]
    sums[taps : taps + 1, 0 : 2 * LANES] = jnp.zeros((1, 2 * LANES), F32)
    head_out[:, 0:LANES] = gq[0:8]
    head_out[:, LANES : 2 * LANES] = grad[0:8]
    for g in range(HALF):
        sums[0:taps, lanes_of(half_b, g, 2 * LANES)] = sums_b[:, head_lanes(g)]
        for half, gain, gv in ((half_a, gain_a, gv_out), (half_b, gain_b, gv_b)):
            sums[taps : taps + 1, lanes_of(half, g, 2 * LANES)] = gain[g : g + 1]
            head_out[:, lanes_of(half, g, 2 * LANES)] = gv[0:8, head_lanes(g)]


def signal_kernel(
    gq, gk, gv_a, gv_b, follow, out_a, out_b, taps_q, taps_k, taps_v, q_out, k_out, v_out, out, wide
):
    rows = gq.shape[0]
    count = taps_q.shape[0]

    def one(grad, after, taps):
        wide[0:rows] = grad
        wide[rows : rows + 8] = after
        total = taps[0:1] * wide[count - 1 : count - 1 + rows]
        for o in range(1, count):
            total = total + taps[o : o + 1] * wide[count - 1 - o : count - 1 - o + rows]
        return total.astype(BF16)

    q_out[...] = one(gq[...], follow[:, 0:LANES], taps_q[...])
    k_out[...] = one(gk[...], follow[:, LANES : 2 * LANES], taps_k[...])
    for own, gv, tokens in ((True, gv_a, out_a), (False, gv_b, out_b)):
        half = half_index(own)
        for g in range(HALF):
            place = lanes_of(half, g)
            out[:, place] = tokens[:, head_lanes(g)]
            v_out[:, place] = one(gv[:, head_lanes(g)], follow[:, lanes_of(half, g, 2 * LANES)], taps_v[:, place])


def finish_kernel(factor, *refs):
    *terms, q_out, k_out, v_out, gain_out = refs
    taps = q_out.shape[0]
    total = terms[0][...]
    for term in terms[1:]:
        total = total + term[...]
    total = total * factor
    q_out[...] = total[0:taps, 0:LANES]
    k_out[...] = total[0:taps, LANES : 2 * LANES]
    v_out[...] = total[0:taps, 2 * LANES :]
    gain_out[...] = total[taps : taps + 1, 2 * LANES :]


def far(x):
    return pltpu.with_memory_space_constraint(x, pltpu.HBM)


def held(*xs):
    return [pltpu.with_memory_space_constraint(x, pltpu.VMEM) for x in xs]


def call(kernel, outs, scratch, args, flops, limit=16, loose=(), **specs):
    size = lambda a: a.size * a.dtype.itemsize
    moved = sum(size(a) for a in args) + sum(size(o) for o in outs)
    return pl.pallas_call(
        kernel,
        out_shape=[o if i in loose else pltpu.VMEM(o.shape, o.dtype) for i, o in enumerate(outs)],
        scratch_shapes=scratch,
        compiler_params=pltpu.CompilerParams(vmem_limit_bytes=limit * 2**20),
        cost_estimate=pl.CostEstimate(flops=flops, bytes_accessed=moved, transcendentals=0),
        **specs,
    )(*args)


def exchange(x, distance):
    count = lax.axis_size("seq")
    return lax.ppermute(x, "seq", [(i, i ^ distance) for i in range(count)])


def tie(x, *others):
    return lax.optimization_barrier((x, *others))[0]


def on_side(bit, reverse):
    set_ = lax.rem(lax.div(lax.axis_index("seq"), bit), 2)
    return set_ == (0 if reverse else 1)


def chosen(flag, x):
    return jnp.where(flag, x, jnp.zeros_like(x))


def pair_kernel(keep, near, part, their):
    upper = lax.rem(lax.div(lax.axis_index("seq"), 2), 2)

    def half(which):
        place = pl.ds(which * PART, PART)
        return keep[place].astype(F32) + near[place].astype(F32)

    part[...] = half(upper)
    their[...] = half(1 - upper).astype(BF16)


def step_kernel(part, *refs):
    *gots, send = refs
    total = part[...]
    for got in gots:
        total = total + got[...].astype(F32)
    send[...] = total.astype(BF16)


def part_kernel(reverse, part, got_y, *rest):
    *gots, own, give = rest
    before = jnp.zeros(part.shape, F32)
    for i, got in enumerate(gots):
        before = before + chosen(on_side(4 << i, reverse), got[...].astype(F32))
    own[...] = before + chosen(on_side(2, reverse), got_y[...].astype(F32))
    give[...] = (before + chosen(jnp.logical_not(on_side(2, reverse)), part[...])).astype(BF16)


def merge_kernel(reverse, own_part, other_part, keep, near, own, give):
    upper = lax.rem(lax.div(lax.axis_index("seq"), 2), 2)
    side = on_side(1, reverse)
    for part, which in ((own_part, upper), (other_part, 1 - upper)):
        place = pl.ds(which * PART, PART)
        before = part[...].astype(F32)
        own[place] = (before + chosen(side, near[place].astype(F32))).astype(BF16)
        give[place] = (before + chosen(jnp.logical_not(side), keep[place].astype(F32))).astype(BF16)


def beyond(keep, send, reverse, works, last):
    count = lax.axis_size("seq")
    works = list(works)
    st = jax.ShapeDtypeStruct
    whole, part_shape = keep.shape, (PART, *keep.shape[1:])
    wide, narrow = st(part_shape, F32), st(part_shape, BF16)
    cost = 4 * keep.size

    def under(x):
        return tie(x, works.pop(0)()) if works else x

    near = exchange(send, 1)
    part, their = call(pair_kernel, [wide, narrow], [], (keep, near), cost)
    got_y = exchange(their, 2)
    gots = []
    bit = 4
    while bit < count:
        send = call(step_kernel, [narrow], [], (part, got_y, *gots), cost)[0]
        gots.append(exchange(under(send), bit))
        bit *= 2
    own_part, give_part = call(
        functools.partial(part_kernel, reverse), [wide, narrow], [], (part, got_y, *gots), cost
    )
    other_part = exchange(under(give_part), 2)
    own, give = call(
        functools.partial(merge_kernel, reverse), [st(whole, BF16)] * 2, [], (own_part, other_part, keep, near), cost
    )
    other = exchange(under(give), 1)
    return own, tie(other, last(own))


def shards(query_in, key_in, value_in, conv_query, conv_key, conv_value, norm_gain, grad_out):
    rows = query_in.shape[0]
    taps = conv_query.shape[0]
    count = lax.axis_size("seq")
    total_rows = rows * count
    st = jax.ShapeDtypeStruct
    half_width = HALF * DIM
    half_state, half_wide = st((HALF, ROWS, DIM), BF16), st((rows, half_width), F32)
    half_narrow, half_features = st((rows, half_width), BF16), st((HALF, ROWS, rows), BF16)
    flat, turned_flat = st((rows, LANES), F32), st((LANES, rows), BF16)
    state_scratch = pltpu.VMEM((HALF, ROWS, DIM), BF16)
    wide = pltpu.VMEM((RIM + rows, DIM), F32)
    gain = norm_gain.reshape(HEADS, DIM)
    state_flops = HEADS * ROWS * DIM * rows
    square_flops = 2 * HALF * rows * rows * DIM

    apart = pl.BlockSpec(memory_space=pltpu.HBM)
    ends = call(
        end_kernel,
        [st((RIM, ALL), BF16)],
        [pltpu.SemaphoreType.DMA((3,))],
        (far(query_in), far(key_in), far(value_in)),
        rows,
        in_specs=[apart] * 3,
    )[0]
    rim = lax.ppermute(ends, "seq", [(i, i + 1) for i in range(count - 1)])

    k, kt, v_b, fk_b, state_b = call(
        first_key_kernel,
        [st((rows, LANES), BF16), turned_flat, half_narrow, half_features, half_state],
        [wide],
        (key_in, value_in, rim, conv_key, conv_value),
        state_flops,
    )
    v_a, fk_a, state_a = call(
        second_key_kernel,
        [half_narrow, half_features, half_state],
        [wide],
        (*held(kt), value_in, rim, conv_value),
        state_flops,
    )
    made = {}

    def local_work(own, v):
        def work():
            if "q" not in made:
                made["q"] = call(
                    query_kernel,
                    [st((rows, LANES), BF16), turned_flat, st((HEADS, ROWS, rows), BF16)],
                    [wide],
                    (query_in, rim, conv_query),
                    state_flops,
                )
            made[own] = call(
                functools.partial(local_kernel, own),
                [half_wide],
                [],
                held(made["q"][0], k, v),
                2 * square_flops,
            )[0]
            return made[own]

        return work

    def norm(own, prefix):
        return call(
            functools.partial(norm_kernel, own),
            [half_narrow, half_narrow, half_state, st((HALF, DIM), F32)],
            [state_scratch, pltpu.VMEM((rows, half_width), F32)],
            (*held(made[own], made["q"][2]), prefix, grad_out, gain),
            2 * state_flops,
        )

    def first_norm(prefix):
        made["norm"] = norm(True, prefix)
        return made["norm"][0]

    pre_a, pre_b = beyond(
        state_a, state_b, False, [local_work(True, v_a), local_work(False, v_b)], first_norm
    )
    q, qt, fq = made["q"]
    out_a, gs_a, state_a, gain_a = made["norm"]
    out_b, gs_b, state_b, gain_b = norm(False, pre_b)
    back = []

    def back_work(own, part, v, gs):
        def work():
            back.append(
                call(
                    functools.partial(back_kernel, own, part),
                    [st((rows, PART * DIM), F32), st((PART * FEAT, rows), F32), st((PART * FEAT, rows), F32)],
                    [],
                    held(q, k, qt, kt, v, gs),
                    2 * square_flops,
                )
            )
            return back[-1][0]

        return work

    def last_work():
        work = back_work(False, 1, v_b, gs_b)()
        made["gq"] = call(
            query_grad_kernel,
            [flat, st((taps, LANES), F32)],
            [wide, state_scratch, pltpu.VMEM((LANES, rows), F32)],
            (query_in, rim, *held(qt, gs_a, gs_b), pre_a, pre_b, *held(*[b[1] for b in back]), conv_query),
            state_flops,
        )
        return made["gq"][0]

    def first_later(state):
        made["later"] = call(
            first_later_kernel,
            [half_wide, st((HALF * FEAT, rows), F32), st((taps, half_width), F32)],
            [wide, state_scratch],
            (value_in, rim, *held(kt, fk_b, v_b), state, *held(back[2][0], back[3][0], back[2][2], back[3][2])),
            2 * state_flops,
        )
        return made["later"][0]

    works = [back_work(True, 0, v_a, gs_a), back_work(True, 1, v_a, gs_a), back_work(False, 0, v_b, gs_b), last_work]
    _, post_a = beyond(state_b, state_a, True, works, first_later)
    gv_b, gk_b, sums_b = made["later"]
    gq, sums_q = made["gq"]
    gv_a, gk, heads, sums = call(
        second_later_kernel,
        [half_wide, flat, st((8, ALL), F32), st((taps + 1, ALL), F32)],
        [wide, state_scratch, pltpu.VMEM((LANES, rows), F32)],
        (key_in, value_in, rim, *held(kt, fk_a, v_a), post_a,
         *held(back[0][0], back[1][0], back[0][2], back[1][2], gv_b, gk_b, sums_b, gq, sums_q, gain_a, gain_b)),
        2 * state_flops,
    )
    follow = lax.ppermute(heads, "seq", [(i + 1, i) for i in range(count - 1)])
    bit = 4
    while bit < count:
        group = (bit, 2 * bit, 3 * bit) if 2 * bit < count else (bit,)
        for got in [exchange(sums, distance) for distance in group]:
            sums = sums + got
        bit *= len(group) + 1
    grad_query, grad_key, grad_value, output = call(
        signal_kernel,
        [st((rows, LANES), BF16), st((rows, LANES), BF16), st((rows, WIDE), BF16), st((rows, WIDE), BF16)],
        [pltpu.VMEM((rows + 8, DIM), F32)],
        (*held(gq, gk, gv_a, gv_b), follow, *held(out_a, out_b), conv_query, conv_key, conv_value),
        2 * state_flops,
        loose=(0, 1, 2, 3),
    )
    taps_query, taps_key, taps_value, taps_gain = call(
        functools.partial(finish_kernel, total_rows ** (-0.5)),
        [st((taps, LANES), F32), st((taps, LANES), F32), st((taps, WIDE), F32), st((1, WIDE), F32)],
        [],
        (tie(sums, grad_value), *[exchange(sums, distance) for distance in (1, 2, 3)]),
        rows,
        loose=(0, 1, 2, 3),
    )
    return (
        output,
        grad_query,
        grad_key,
        grad_value,
        taps_query,
        taps_key,
        taps_value,
        taps_gain.reshape(WIDE),
    )


def solution(mesh):
    rows = P(("groups", "seq"), None)
    return jax.shard_map(
        shards,
        mesh=mesh,
        in_specs=(rows, rows, rows, P(), P(), P(), P(), rows),
        out_specs=(rows, rows, rows, rows, P("groups", None), P("groups", None), P("groups", None), P("groups")),
        check_vma=False,
    )
```

```python
import functools

import jax
import jax.numpy as jnp
from jax import lax
from jax.experimental import pallas as pl
from jax.experimental.pallas import tpu as pltpu
from jax.sharding import PartitionSpec as P

HEADS = 8
HALF = HEADS // 2
PART = HEADS // 4
FEAT = 16
DIM = 128
EPSILON = 1e-06
LANES = HEADS * FEAT
WIDE = HEADS * DIM
ALL = 2 * LANES + WIDE
ROWS = 160
LIN = 128
TAIL = 144
RIM = 16
STEP = 128
F32 = jnp.float32
BF16 = jnp.bfloat16

NN = (((1,), (0,)), ((), ()))
NT = (((1,), (1,)), ((), ()))
TN = (((0,), (0,)), ((), ()))


def dot(a, b, dims):
    return lax.dot_general(a, b, dims, preferred_element_type=F32)


def head_rows(h):
    return slice(h * FEAT, (h + 1) * FEAT)


def head_lanes(h):
    return slice(h * DIM, (h + 1) * DIM)


def conv(wide_ref, taps, rows):
    margin = taps.shape[0] - 1
    total = taps[0:1] * wide_ref[RIM - margin : RIM - margin + rows]
    for o in range(1, margin + 1):
        total = total + taps[o : o + 1] * wide_ref[RIM - margin + o : RIM - margin + o + rows]
    return total


def tap_sums(grad, wide_ref, taps):
    rows = grad.shape[0]
    start = RIM - (taps - 1)
    return [
        jnp.sum(grad * wide_ref[start + o : start + o + rows], axis=0, keepdims=True)
        for o in range(taps)
    ]


def turned(x, shift):
    return x if shift % FEAT == 0 else pltpu.roll(x, shift % FEAT, 0)


def features(x):
    half = (0.5 / FEAT) ** 0.5
    pieces = [(x * turned(x, FEAT - d) * half).astype(BF16) for d in range(8)]
    pieces.append((x * FEAT ** (-0.25)).astype(BF16))
    rows = lax.broadcasted_iota(jnp.int32, (8, x.shape[1]), 0)
    one = jnp.where(rows == 0, 1.0, 0.0).astype(F32)
    pieces.append(jnp.concatenate([x[:8] * x[8:] * half, one], axis=0).astype(BF16))
    return jnp.concatenate(pieces, axis=0)


def feature_grad(x, state, vector):
    g = dot(state, vector, NT)
    crossed = 2.0 * g[0:FEAT] * x
    for d in range(1, 8):
        part = g[d * FEAT : (d + 1) * FEAT]
        crossed = crossed + part * turned(x, FEAT - d) + turned(part * x, d)
    part = g[TAIL : TAIL + 8]
    crossed = crossed + jnp.concatenate([part * x[8:], part * x[:8]], axis=0)
    return g[LIN:TAIL] * FEAT ** (-0.25) + crossed * (0.5 / FEAT) ** 0.5


def half_index(own):
    here, parity, bit = lax.axis_index("seq"), 0, 1
    while bit < lax.axis_size("seq"):
        parity = parity + lax.rem(lax.div(here, bit), 2)
        bit *= 2
    parity = lax.rem(parity, 2)
    return parity if own else 1 - parity


def rows_of(half, g):
    return pl.ds(pl.multiple_of((half * HALF + g) * FEAT, FEAT), FEAT)


def lanes_of(half, g, start=0):
    return pl.ds(pl.multiple_of(start + (half * HALF + g) * DIM, DIM), DIM)


def doubled(state_ref, out_ref):
    rows = lax.broadcasted_iota(jnp.int32, (ROWS, DIM), 0)
    pair = ((rows >= FEAT) & (rows < LIN)) | ((rows >= TAIL) & (rows < TAIL + 8))
    weight = jnp.where(pair, 2.0, 1.0).astype(F32)
    for g in range(HALF):
        out_ref[g] = (state_ref[g].astype(F32) * weight).astype(BF16)


def head_mask(h):
    lanes = lax.broadcasted_iota(jnp.int32, (1, LANES), 1)
    return jnp.where(lanes // FEAT == h, 1.0, 0.0).astype(F32).astype(BF16)


def fill(wide, rim, rest):
    wide[0:RIM] = rim.astype(F32)
    wide[RIM : RIM + rest.shape[0]] = rest.astype(F32)


def end_kernel(query, key, value, out, sems):
    start = query.shape[0] - RIM
    copies = [
        pltpu.make_async_copy(ref.at[pl.ds(start, RIM)], out.at[:, pl.ds(lane, ref.shape[1])], sems.at[i])
        for i, (ref, lane) in enumerate(((query, 0), (key, LANES), (value, 2 * LANES)))
    ]
    for copy in copies:
        copy.start()
    for copy in copies:
        copy.wait()


def value_states(half, kt, value, rim, taps_v, v_out, f_out, state_out, wide):
    rows = value.shape[0]
    for g in range(HALF):
        f_out[g] = features(kt[rows_of(half, g)].astype(F32))
    for g in range(HALF):
        fill(wide, rim[:, lanes_of(half, g, 2 * LANES)], value[:, lanes_of(half, g)])
        v_out[:, head_lanes(g)] = conv(wide, taps_v[:, lanes_of(half, g)], rows).astype(BF16)
    for g in range(HALF):
        state_out[g] = dot(f_out[g], v_out[:, head_lanes(g)], NN).astype(BF16)


def first_key_kernel(key, value, rim, taps_k, taps_v, k_out, kt_out, v_out, f_out, state_out, wide):
    rows = key.shape[0]
    fill(wide, rim[:, LANES : 2 * LANES], key[...])
    k = conv(wide, taps_k[...], rows).astype(BF16)
    k_out[...] = k
    kt_out[...] = k.astype(F32).T.astype(BF16)
    value_states(half_index(False), kt_out, value, rim, taps_v, v_out, f_out, state_out, wide)


def second_key_kernel(kt, value, rim, taps_v, v_out, f_out, state_out, wide):
    value_states(half_index(True), kt, value, rim, taps_v, v_out, f_out, state_out, wide)


def query_kernel(query, rim, taps_q, q_out, qt_out, fq_out, wide):
    rows = query.shape[0]
    fill(wide, rim[:, 0:LANES], query[...])
    q = conv(wide, taps_q[...], rows).astype(BF16)
    q_out[...] = q
    qt = q.astype(F32).T
    qt_out[...] = qt.astype(BF16)
    for h in range(HEADS):
        fq_out[h] = features(qt[head_rows(h)])


def local_kernel(own, q_ref, k_ref, v_ref, out):
    rows = q_ref.shape[0]
    half = half_index(own)
    quarter = q_ref[...] * jnp.asarray(FEAT ** (-0.5), BF16)
    for g in range(HALF):
        qs = quarter * head_mask(half * HALF + g)
        for start in range(0, rows, STEP):
            stop = start + STEP
            t = dot(qs[start:stop], k_ref[0:stop], NT)
            w = (0.5 * t + 1.0) * t + 1.0
            at = lax.broadcasted_iota(jnp.int32, (STEP, stop), 0) + start
            w = jnp.where(at >= lax.broadcasted_iota(jnp.int32, (STEP, stop), 1), w, 0.0)
            out[start:stop, head_lanes(g)] = dot(w.astype(BF16), v_ref[0:stop, head_lanes(g)], NN)


def norm_kernel(own, local, fq, prefix, grad, gain, out, gs_out, state_out, gain_out, pre, summed_ref):
    half = half_index(own)
    doubled(prefix, pre)
    for g in range(HALF):
        place = head_lanes(g)
        summed_ref[:, place] = local[:, place] + dot(fq[half * HALF + g], pre[g], TN)
    for g in range(HALF):
        place = head_lanes(g)
        summed = summed_ref[:, place]
        scale = lax.rsqrt(jnp.mean(summed * summed, axis=-1, keepdims=True) + EPSILON)
        normal = summed * scale
        weight = gain[pl.ds(half * HALF + g, 1)]
        out[:, place] = (normal * weight).astype(BF16)
        incoming = grad[:, lanes_of(half, g)].astype(F32)
        gain_out[g : g + 1] = jnp.sum(incoming * normal, axis=0, keepdims=True)
        upstream = incoming * weight
        gs = scale * (upstream - normal * jnp.mean(normal * upstream, axis=-1, keepdims=True))
        gs = gs.astype(BF16)
        gs_out[:, place] = gs
        state_out[g] = dot(fq[half * HALF + g], gs, NN).astype(BF16)


def back_kernel(own, part, q_ref, k_ref, qt_ref, kt_ref, v_ref, gs_ref, gv_out, gq_out, gk_out):
    rows = q_ref.shape[0]
    half = half_index(own)
    quarter = q_ref[...] * jnp.asarray(FEAT ** (-0.5), BF16)
    for i in range(PART):
        g = part * PART + i
        ks = k_ref[...] * head_mask(half * HALF + g)
        qt = qt_ref[rows_of(half, g)]
        kt = kt_ref[rows_of(half, g)]
        for start in range(0, rows, STEP):
            stop = start + STEP
            shape = (STEP, rows - start)
            t = dot(ks[start:stop], quarter[start:], NT)
            seen = lax.broadcasted_iota(jnp.int32, shape, 1) >= lax.broadcasted_iota(jnp.int32, shape, 0)
            w = jnp.where(seen, (0.5 * t + 1.0) * t + 1.0, 0.0).astype(BF16)
            gs = gs_ref[start:, head_lanes(g)]
            gv_out[start:stop, head_lanes(i)] = dot(w, gs, NN)
            gw = dot(v_ref[start:stop, head_lanes(g)], gs, NT)
            s = jnp.where(seen, gw * (FEAT ** (-0.5) + FEAT ** (-0.5) * t), 0.0).astype(BF16)
            part_q = dot(kt[:, start:stop], s, NN)
            if start == 0:
                gq_out[head_rows(i)] = part_q
            else:
                gq_out[head_rows(i), start:] += part_q
            gk_out[head_rows(i), start:stop] = dot(qt[:, start:], s, NT)


def query_grad_kernel(
    query, rim, qt_ref, gs_a, gs_b, pre_a, pre_b, a0, a1, b0, b1, taps_q, g_out, sums, wide, pre, turned_grad
):
    for own, gs, prefix, locals_ in ((True, gs_a, pre_a, (a0, a1)), (False, gs_b, pre_b, (b0, b1))):
        half = half_index(own)
        doubled(prefix, pre)
        for g in range(HALF):
            x = qt_ref[rows_of(half, g)].astype(F32)
            turned_grad[rows_of(half, g)] = locals_[g // PART][head_rows(g % PART)] + feature_grad(
                x, pre[g], gs[:, head_lanes(g)]
            )
    grad = turned_grad[...].T
    g_out[...] = grad
    fill(wide, rim[:, 0:LANES], query[...])
    for o, row in enumerate(tap_sums(grad, wide, taps_q.shape[0])):
        sums[o : o + 1] = row


def later_half(half, value, rim, kt, fk, v, state, locals_v, locals_k, gv_out, gk_put, sums_put, wide, post, taps):
    doubled(state, post)
    for g in range(HALF):
        local = locals_v[g // PART][:, head_lanes(g % PART)]
        gv_out[:, head_lanes(g)] = local + dot(fk[g], post[g], TN)
    for g in range(HALF):
        local = locals_k[g // PART][head_rows(g % PART)]
        x = kt[rows_of(half, g)].astype(F32)
        gk_put(g, local + feature_grad(x, post[g], v[:, head_lanes(g)]))
    for g in range(HALF):
        fill(wide, rim[:, lanes_of(half, g, 2 * LANES)], value[:, lanes_of(half, g)])
        for o, row in enumerate(tap_sums(gv_out[:, head_lanes(g)], wide, taps)):
            sums_put(o, g, row)


def first_later_kernel(value, rim, kt, fk, v, state, v0, v1, k0, k1, gv_out, gk_out, sums, wide, post):
    def gk_put(g, x):
        gk_out[head_rows(g)] = x

    def sums_put(o, g, row):
        sums[o : o + 1, head_lanes(g)] = row

    later_half(
        half_index(False), value, rim, kt, fk, v, state, (v0, v1), (k0, k1), gv_out, gk_put, sums_put, wide, post,
        sums.shape[0],
    )


def second_later_kernel(
    key, value, rim, kt, fk, v, state, v0, v1, k0, k1, gv_b, gk_b, sums_b, gq, sums_q, gain_a, gain_b,
    gv_out, gk_out, head_out, sums, wide, post, turned_grad,
):
    taps = sums_q.shape[0]
    rows = key.shape[0]
    half_a, half_b = half_index(True), half_index(False)

    def gk_put(g, x):
        turned_grad[rows_of(half_a, g)] = x

    def sums_put(o, g, row):
        sums[o : o + 1, lanes_of(half_a, g, 2 * LANES)] = row

    turned_grad[pl.ds(pl.multiple_of(half_b * HALF * FEAT, HALF * FEAT), HALF * FEAT)] = gk_b[...]
    later_half(
        half_a, value, rim, kt, fk, v, state, (v0, v1), (k0, k1), gv_out, gk_put, sums_put, wide, post, taps
    )
    grad = turned_grad[...].T
    gk_out[...] = grad
    fill(wide, rim[:, LANES : 2 * LANES], key[...])
    for o, row in enumerate(tap_sums(grad, wide, taps)):
        sums[o : o + 1, LANES : 2 * LANES] = row
    sums[0:taps, 0:LANES] = sums_q[...]
    sums[taps : taps + 1, 0 : 2 * LANES] = jnp.zeros((1, 2 * LANES), F32)
    head_out[:, 0:LANES] = gq[0:8]
    head_out[:, LANES : 2 * LANES] = grad[0:8]
    for g in range(HALF):
        sums[0:taps, lanes_of(half_b, g, 2 * LANES)] = sums_b[:, head_lanes(g)]
        for half, gain, gv in ((half_a, gain_a, gv_out), (half_b, gain_b, gv_b)):
            sums[taps : taps + 1, lanes_of(half, g, 2 * LANES)] = gain[g : g + 1]
            head_out[:, lanes_of(half, g, 2 * LANES)] = gv[0:8, head_lanes(g)]


def token_kernel(out_a, out_b, out, sems):
    copies = []
    for i, (own, tokens) in enumerate(((True, out_a), (False, out_b))):
        width = tokens.shape[1]
        place = pl.ds(pl.multiple_of(half_index(own) * width, width), width)
        copies.append(pltpu.make_async_copy(tokens, out.at[:, place], sems.at[i]))
    for copy in copies:
        copy.start()
    for copy in copies:
        copy.wait()


def signal_kernel(
    gq, gk, gv_a, gv_b, follow, taps_q, taps_k, taps_v, q_out, k_out, v_out, wide, q_part, k_part, v_part, sems
):
    rows = gq.shape[0]
    count = taps_q.shape[0]
    copies = []

    def one(grad, after, taps):
        wide[0:rows] = grad
        wide[rows : rows + 8] = after
        total = taps[0:1] * wide[count - 1 : count - 1 + rows]
        for o in range(1, count):
            total = total + taps[o : o + 1] * wide[count - 1 - o : count - 1 - o + rows]
        return total.astype(BF16)

    def move(part, out):
        copies.append(pltpu.make_async_copy(part, out, sems.at[len(copies)]))
        copies[-1].start()

    for i, (own, gv) in enumerate(((True, gv_a), (False, gv_b))):
        half = half_index(own)
        for g in range(HALF):
            place = lanes_of(half, g)
            slot = i * HALF + g
            after = follow[:, lanes_of(half, g, 2 * LANES)]
            v_part[slot] = one(gv[:, head_lanes(g)], after, taps_v[:, place])
            move(v_part.at[slot], v_out.at[:, place])
    q_part[...] = one(gq[...], follow[:, 0:LANES], taps_q[...])
    move(q_part, q_out)
    k_part[...] = one(gk[...], follow[:, LANES : 2 * LANES], taps_k[...])
    move(k_part, k_out)
    for copy in copies:
        copy.wait()


def finish_kernel(factor, *refs):
    *terms, q_out, k_out, v_out, gain_out = refs
    taps = q_out.shape[0]
    total = terms[0][...]
    for term in terms[1:]:
        total = total + term[...]
    total = total * factor
    q_out[...] = total[0:taps, 0:LANES]
    k_out[...] = total[0:taps, LANES : 2 * LANES]
    v_out[...] = total[0:taps, 2 * LANES :]
    gain_out[...] = total[taps : taps + 1, 2 * LANES :]


def far(x):
    return pltpu.with_memory_space_constraint(x, pltpu.HBM)


def held(*xs):
    return [pltpu.with_memory_space_constraint(x, pltpu.VMEM) for x in xs]


def call(kernel, outs, scratch, args, flops, limit=16, loose=(), **specs):
    size = lambda a: a.size * a.dtype.itemsize
    moved = sum(size(a) for a in args) + sum(size(o) for o in outs)
    return pl.pallas_call(
        kernel,
        out_shape=[o if i in loose else pltpu.VMEM(o.shape, o.dtype) for i, o in enumerate(outs)],
        scratch_shapes=scratch,
        compiler_params=pltpu.CompilerParams(vmem_limit_bytes=limit * 2**20),
        cost_estimate=pl.CostEstimate(flops=flops, bytes_accessed=moved, transcendentals=0),
        **specs,
    )(*args)


def exchange(x, distance):
    count = lax.axis_size("seq")
    return lax.ppermute(x, "seq", [(i, i ^ distance) for i in range(count)])


def tie(x, *others):
    return lax.optimization_barrier((x, *others))[0]


def on_side(bit, reverse):
    set_ = lax.rem(lax.div(lax.axis_index("seq"), bit), 2)
    return set_ == (0 if reverse else 1)


def chosen(flag, x):
    return jnp.where(flag, x, jnp.zeros_like(x))


def pair_kernel(keep, near, part, their):
    upper = lax.rem(lax.div(lax.axis_index("seq"), 2), 2)

    def half(which):
        place = pl.ds(which * PART, PART)
        return keep[place].astype(F32) + near[place].astype(F32)

    part[...] = half(upper)
    their[...] = half(1 - upper).astype(BF16)


def step_kernel(part, *refs):
    *gots, send = refs
    total = part[...]
    for got in gots:
        total = total + got[...].astype(F32)
    send[...] = total.astype(BF16)


def part_kernel(reverse, part, got_y, *rest):
    *gots, own, give = rest
    before = jnp.zeros(part.shape, F32)
    for i, got in enumerate(gots):
        before = before + chosen(on_side(4 << i, reverse), got[...].astype(F32))
    own[...] = before + chosen(on_side(2, reverse), got_y[...].astype(F32))
    give[...] = (before + chosen(jnp.logical_not(on_side(2, reverse)), part[...])).astype(BF16)


def merge_kernel(reverse, own_part, other_part, keep, near, own, give):
    upper = lax.rem(lax.div(lax.axis_index("seq"), 2), 2)
    side = on_side(1, reverse)
    for part, which in ((own_part, upper), (other_part, 1 - upper)):
        place = pl.ds(which * PART, PART)
        before = part[...].astype(F32)
        own[place] = (before + chosen(side, near[place].astype(F32))).astype(BF16)
        give[place] = (before + chosen(jnp.logical_not(side), keep[place].astype(F32))).astype(BF16)


def beyond(keep, send, reverse, works, last):
    count = lax.axis_size("seq")
    works = list(works)
    st = jax.ShapeDtypeStruct
    whole, part_shape = keep.shape, (PART, *keep.shape[1:])
    wide, narrow = st(part_shape, F32), st(part_shape, BF16)
    cost = 4 * keep.size

    def under(x):
        return tie(x, *works.pop(0)()) if works else x

    near = exchange(send, 1)
    part, their = call(pair_kernel, [wide, narrow], [], (keep, near), cost)
    got_y = exchange(their, 3)
    gots = []
    bit = 4
    while bit < count:
        send = call(step_kernel, [narrow], [], (part, got_y, *gots), cost)[0]
        gots.append(exchange(under(send), bit + 1))
        bit *= 2
    own_part, give_part = call(
        functools.partial(part_kernel, reverse), [wide, narrow], [], (part, got_y, *gots), cost
    )
    other_part = exchange(under(give_part), 3)
    own, give = call(
        functools.partial(merge_kernel, reverse), [st(whole, BF16)] * 2, [], (own_part, other_part, keep, near), cost
    )
    other = exchange(under(give), 1)
    return own, tie(other, last(own))


def shards(query_in, key_in, value_in, conv_query, conv_key, conv_value, norm_gain, grad_out):
    rows = query_in.shape[0]
    taps = conv_query.shape[0]
    count = lax.axis_size("seq")
    total_rows = rows * count
    st = jax.ShapeDtypeStruct
    half_width = HALF * DIM
    half_state, half_wide = st((HALF, ROWS, DIM), BF16), st((rows, half_width), F32)
    half_narrow, half_features = st((rows, half_width), BF16), st((HALF, ROWS, rows), BF16)
    flat, turned_flat = st((rows, LANES), F32), st((LANES, rows), BF16)
    state_scratch = pltpu.VMEM((HALF, ROWS, DIM), BF16)
    wide = pltpu.VMEM((RIM + rows, DIM), F32)
    gain = norm_gain.reshape(HEADS, DIM)
    state_flops = HEADS * ROWS * DIM * rows
    square_flops = 2 * HALF * rows * rows * DIM

    apart = pl.BlockSpec(memory_space=pltpu.HBM)
    ends = call(
        end_kernel,
        [st((RIM, ALL), BF16)],
        [pltpu.SemaphoreType.DMA((3,))],
        (far(query_in), far(key_in), far(value_in)),
        rows,
        in_specs=[apart] * 3,
    )[0]
    rim = lax.ppermute(ends, "seq", [(i, i + 1) for i in range(count - 1)])

    k, kt, v_b, fk_b, state_b = call(
        first_key_kernel,
        [st((rows, LANES), BF16), turned_flat, half_narrow, half_features, half_state],
        [wide],
        (key_in, value_in, rim, conv_key, conv_value),
        state_flops,
    )
    v_a, fk_a, state_a = call(
        second_key_kernel,
        [half_narrow, half_features, half_state],
        [wide],
        (*held(kt), value_in, rim, conv_value),
        state_flops,
    )
    made = {}

    def local_work(own, v):
        def work():
            if "q" not in made:
                made["q"] = call(
                    query_kernel,
                    [st((rows, LANES), BF16), turned_flat, st((HEADS, ROWS, rows), BF16)],
                    [wide],
                    (query_in, rim, conv_query),
                    state_flops,
                )
            made[own] = call(
                functools.partial(local_kernel, own),
                [half_wide],
                [],
                held(made["q"][0], k, v),
                2 * square_flops,
            )[0]
            return (made[own],)

        return work

    def norm(own, prefix):
        return call(
            functools.partial(norm_kernel, own),
            [half_narrow, half_narrow, half_state, st((HALF, DIM), F32)],
            [state_scratch, pltpu.VMEM((rows, half_width), F32)],
            (*held(made[own], made["q"][2]), prefix, grad_out, gain),
            2 * state_flops,
        )

    def first_norm(prefix):
        made["norm"] = norm(True, prefix)
        return made["norm"][0]

    pre_a, pre_b = beyond(
        state_a, state_b, False, [local_work(True, v_a), local_work(False, v_b)], first_norm
    )
    q, qt, fq = made["q"]
    out_a, gs_a, state_a, gain_a = made["norm"]
    out_b, gs_b, state_b, gain_b = norm(False, pre_b)
    back = []

    def first_back():
        made["out"] = call(
            token_kernel,
            [st((rows, WIDE), BF16)],
            [pltpu.SemaphoreType.DMA((2,))],
            held(out_a, out_b),
            rows,
            loose=(0,),
            out_specs=[apart],
        )[0]
        return (*back_work(True, 0, v_a, gs_a)(), made["out"])

    def back_work(own, part, v, gs):
        def work():
            back.append(
                call(
                    functools.partial(back_kernel, own, part),
                    [st((rows, PART * DIM), F32), st((PART * FEAT, rows), F32), st((PART * FEAT, rows), F32)],
                    [],
                    held(q, k, qt, kt, v, gs),
                    2 * square_flops,
                )
            )
            return (back[-1][0],)

        return work

    def last_work():
        work = back_work(False, 1, v_b, gs_b)()[0]
        made["gq"] = call(
            query_grad_kernel,
            [flat, st((taps, LANES), F32)],
            [wide, state_scratch, pltpu.VMEM((LANES, rows), F32)],
            (query_in, rim, *held(qt, gs_a, gs_b), pre_a, pre_b, *held(*[b[1] for b in back]), conv_query),
            state_flops,
        )
        return (work, made["gq"][0])

    def first_later(state):
        made["later"] = call(
            first_later_kernel,
            [half_wide, st((HALF * FEAT, rows), F32), st((taps, half_width), F32)],
            [wide, state_scratch],
            (value_in, rim, *held(kt, fk_b, v_b), state, *held(back[2][0], back[3][0], back[2][2], back[3][2])),
            2 * state_flops,
        )
        return made["later"][0]

    works = [first_back, back_work(True, 1, v_a, gs_a), back_work(False, 0, v_b, gs_b), last_work]
    _, post_a = beyond(state_b, state_a, True, works, first_later)
    gv_b, gk_b, sums_b = made["later"]
    gq, sums_q = made["gq"]
    gv_a, gk, heads, sums = call(
        second_later_kernel,
        [half_wide, flat, st((8, ALL), F32), st((taps + 1, ALL), F32)],
        [wide, state_scratch, pltpu.VMEM((LANES, rows), F32)],
        (key_in, value_in, rim, *held(kt, fk_a, v_a), post_a,
         *held(back[0][0], back[1][0], back[0][2], back[1][2], gv_b, gk_b, sums_b, gq, sums_q, gain_a, gain_b)),
        2 * state_flops,
    )
    follow = lax.ppermute(heads, "seq", [(i + 1, i) for i in range(count - 1)])
    bit = 4
    while bit < count:
        group = (bit + 1, 2 * bit + 1, 3 * bit) if 2 * bit < count else (bit + 1,)
        for got in [exchange(sums, distance) for distance in group]:
            sums = sums + got
        bit *= len(group) + 1
    flat_narrow = st((rows, LANES), BF16)
    grad_query, grad_key, grad_value = call(
        signal_kernel,
        [flat_narrow, flat_narrow, st((rows, WIDE), BF16)],
        [pltpu.VMEM((rows + 8, DIM), F32), pltpu.VMEM((rows, LANES), BF16), pltpu.VMEM((rows, LANES), BF16),
         pltpu.VMEM((HEADS, rows, DIM), BF16), pltpu.SemaphoreType.DMA((HEADS + 2,))],
        (*held(gq, gk, gv_a, gv_b), follow, conv_query, conv_key, conv_value),
        2 * state_flops,
        loose=(0, 1, 2),
        out_specs=[apart] * 3,
    )
    taps_query, taps_key, taps_value, taps_gain = call(
        functools.partial(finish_kernel, total_rows ** (-0.5)),
        [st((taps, LANES), F32), st((taps, LANES), F32), st((taps, WIDE), F32), st((1, WIDE), F32)],
        [],
        (tie(sums, grad_value), *[exchange(sums, distance) for distance in (1, 2, 3)]),
        rows,
        loose=(0, 1, 2, 3),
    )
    return (
        made["out"],
        grad_query,
        grad_key,
        grad_value,
        taps_query,
        taps_key,
        taps_value,
        taps_gain.reshape(WIDE),
    )


def solution(mesh):
    rows = P(("groups", "seq"), None)
    return jax.shard_map(
        shards,
        mesh=mesh,
        in_specs=(rows, rows, rows, P(), P(), P(), P(), rows),
        out_specs=(rows, rows, rows, rows, P("groups", None), P("groups", None), P("groups", None), P("groups")),
        check_vma=False,
    )
```

```python
import functools

import jax
import jax.numpy as jnp
from jax import lax
from jax.experimental import pallas as pl
from jax.experimental.pallas import tpu as pltpu
from jax.sharding import PartitionSpec as P

HEADS = 8
HALF = HEADS // 2
PART = HEADS // 4
FEAT = 16
DIM = 128
EPSILON = 1e-06
LANES = HEADS * FEAT
WIDE = HEADS * DIM
ALL = 2 * LANES + WIDE
ROWS = 160
LIN = 128
TAIL = 144
RIM = 16
STEP = 128
F32 = jnp.float32
BF16 = jnp.bfloat16

NN = (((1,), (0,)), ((), ()))
NT = (((1,), (1,)), ((), ()))
TN = (((0,), (0,)), ((), ()))


def dot(a, b, dims):
    return lax.dot_general(a, b, dims, preferred_element_type=F32)


def head_rows(h):
    return slice(h * FEAT, (h + 1) * FEAT)


def head_lanes(h):
    return slice(h * DIM, (h + 1) * DIM)


def conv(wide_ref, taps, rows):
    margin = taps.shape[0] - 1
    total = taps[0:1] * wide_ref[RIM - margin : RIM - margin + rows]
    for o in range(1, margin + 1):
        total = total + taps[o : o + 1] * wide_ref[RIM - margin + o : RIM - margin + o + rows]
    return total


def tap_sums(grad, wide_ref, taps):
    rows = grad.shape[0]
    start = RIM - (taps - 1)
    return [
        jnp.sum(grad * wide_ref[start + o : start + o + rows], axis=0, keepdims=True)
        for o in range(taps)
    ]


def turned(x, shift):
    return x if shift % FEAT == 0 else pltpu.roll(x, shift % FEAT, 0)


def features(x):
    half = (0.5 / FEAT) ** 0.5
    pieces = [(x * turned(x, FEAT - d) * half).astype(BF16) for d in range(8)]
    pieces.append((x * FEAT ** (-0.25)).astype(BF16))
    rows = lax.broadcasted_iota(jnp.int32, (8, x.shape[1]), 0)
    one = jnp.where(rows == 0, 1.0, 0.0).astype(F32)
    pieces.append(jnp.concatenate([x[:8] * x[8:] * half, one], axis=0).astype(BF16))
    return jnp.concatenate(pieces, axis=0)


def feature_grad(x, state, vector):
    g = dot(state, vector, NT)
    crossed = 2.0 * g[0:FEAT] * x
    for d in range(1, 8):
        part = g[d * FEAT : (d + 1) * FEAT]
        crossed = crossed + part * turned(x, FEAT - d) + turned(part * x, d)
    part = g[TAIL : TAIL + 8]
    crossed = crossed + jnp.concatenate([part * x[8:], part * x[:8]], axis=0)
    return g[LIN:TAIL] * FEAT ** (-0.25) + crossed * (0.5 / FEAT) ** 0.5


def half_index(own):
    core = lax.rem(lax.axis_index("seq"), 2)
    return core if own else 1 - core


def rows_of(half, g):
    return pl.ds(pl.multiple_of((half * HALF + g) * FEAT, FEAT), FEAT)


def lanes_of(half, g, start=0):
    return pl.ds(pl.multiple_of(start + (half * HALF + g) * DIM, DIM), DIM)


def doubled(state_ref, out_ref):
    rows = lax.broadcasted_iota(jnp.int32, (ROWS, DIM), 0)
    pair = ((rows >= FEAT) & (rows < LIN)) | ((rows >= TAIL) & (rows < TAIL + 8))
    weight = jnp.where(pair, 2.0, 1.0).astype(F32)
    for g in range(HALF):
        out_ref[g] = (state_ref[g].astype(F32) * weight).astype(BF16)


def head_mask(h):
    lanes = lax.broadcasted_iota(jnp.int32, (1, LANES), 1)
    return jnp.where(lanes // FEAT == h, 1.0, 0.0).astype(F32).astype(BF16)


def fill(wide, rim, rest):
    wide[0:RIM] = rim.astype(F32)
    wide[RIM : RIM + rest.shape[0]] = rest.astype(F32)


def end_kernel(query, key, value, out, sems):
    start = query.shape[0] - RIM
    copies = [
        pltpu.make_async_copy(ref.at[pl.ds(start, RIM)], out.at[:, pl.ds(lane, ref.shape[1])], sems.at[i])
        for i, (ref, lane) in enumerate(((query, 0), (key, LANES), (value, 2 * LANES)))
    ]
    for copy in copies:
        copy.start()
    for copy in copies:
        copy.wait()


def value_states(half, kt, value, rim, taps_v, v_out, f_out, state_out, wide):
    rows = value.shape[0]
    for g in range(HALF):
        f_out[g] = features(kt[rows_of(half, g)].astype(F32))
    for g in range(HALF):
        fill(wide, rim[:, lanes_of(half, g, 2 * LANES)], value[:, lanes_of(half, g)])
        v_out[:, head_lanes(g)] = conv(wide, taps_v[:, lanes_of(half, g)], rows).astype(BF16)
    for g in range(HALF):
        state_out[g] = dot(f_out[g], v_out[:, head_lanes(g)], NN).astype(BF16)


def first_key_kernel(key, value, rim, taps_k, taps_v, k_out, kt_out, v_out, f_out, state_out, wide):
    rows = key.shape[0]
    fill(wide, rim[:, LANES : 2 * LANES], key[...])
    k = conv(wide, taps_k[...], rows).astype(BF16)
    k_out[...] = k
    kt_out[...] = k.astype(F32).T.astype(BF16)
    value_states(half_index(False), kt_out, value, rim, taps_v, v_out, f_out, state_out, wide)


def second_key_kernel(kt, value, rim, taps_v, v_out, f_out, state_out, wide):
    value_states(half_index(True), kt, value, rim, taps_v, v_out, f_out, state_out, wide)


def query_kernel(query, rim, taps_q, q_out, qt_out, fq_out, wide):
    rows = query.shape[0]
    fill(wide, rim[:, 0:LANES], query[...])
    q = conv(wide, taps_q[...], rows).astype(BF16)
    q_out[...] = q
    qt = q.astype(F32).T
    qt_out[...] = qt.astype(BF16)
    for h in range(HEADS):
        fq_out[h] = features(qt[head_rows(h)])


def local_kernel(own, q_ref, k_ref, v_ref, out):
    rows = q_ref.shape[0]
    half = half_index(own)
    quarter = q_ref[...] * jnp.asarray(FEAT ** (-0.5), BF16)
    for g in range(HALF):
        qs = quarter * head_mask(half * HALF + g)
        for start in range(0, rows, STEP):
            stop = start + STEP
            t = dot(qs[start:stop], k_ref[0:stop], NT)
            w = (0.5 * t + 1.0) * t + 1.0
            at = lax.broadcasted_iota(jnp.int32, (STEP, stop), 0) + start
            w = jnp.where(at >= lax.broadcasted_iota(jnp.int32, (STEP, stop), 1), w, 0.0)
            out[start:stop, head_lanes(g)] = dot(w.astype(BF16), v_ref[0:stop, head_lanes(g)], NN)


def norm_kernel(own, local, fq, prefix, grad, gain, *refs):
    *others, out, gs_out, state_out, gain_out, pre, summed_ref = refs
    half = half_index(own)
    doubled(prefix, pre)
    for other in others:
        for g in range(HALF):
            out[:, lanes_of(1 - half, g)] = other[:, head_lanes(g)]
    for g in range(HALF):
        place = head_lanes(g)
        summed_ref[:, place] = local[:, place] + dot(fq[half * HALF + g], pre[g], TN)
    for g in range(HALF):
        place = head_lanes(g)
        summed = summed_ref[:, place]
        scale = lax.rsqrt(jnp.mean(summed * summed, axis=-1, keepdims=True) + EPSILON)
        normal = summed * scale
        weight = gain[pl.ds(half * HALF + g, 1)]
        out[:, place if own else lanes_of(half, g)] = (normal * weight).astype(BF16)
        incoming = grad[:, lanes_of(half, g)].astype(F32)
        gain_out[g : g + 1] = jnp.sum(incoming * normal, axis=0, keepdims=True)
        upstream = incoming * weight
        gs = scale * (upstream - normal * jnp.mean(normal * upstream, axis=-1, keepdims=True))
        gs = gs.astype(BF16)
        gs_out[:, place] = gs
        state_out[g] = dot(fq[half * HALF + g], gs, NN).astype(BF16)


def first_back_kernel(q_ref, k_ref, qt_ref, kt_ref, v_ref, gs_ref, tokens, gv_out, gq_out, gk_out, out, sem):
    copy = pltpu.make_async_copy(tokens, out, sem)
    copy.start()
    back_kernel(True, 0, q_ref, k_ref, qt_ref, kt_ref, v_ref, gs_ref, gv_out, gq_out, gk_out)
    copy.wait()


def back_kernel(own, part, q_ref, k_ref, qt_ref, kt_ref, v_ref, gs_ref, gv_out, gq_out, gk_out):
    rows = q_ref.shape[0]
    half = half_index(own)
    quarter = q_ref[...] * jnp.asarray(FEAT ** (-0.5), BF16)
    for i in range(PART):
        g = part * PART + i
        ks = k_ref[...] * head_mask(half * HALF + g)
        qt = qt_ref[rows_of(half, g)]
        kt = kt_ref[rows_of(half, g)]
        for start in range(0, rows, STEP):
            stop = start + STEP
            shape = (STEP, rows - start)
            t = dot(ks[start:stop], quarter[start:], NT)
            seen = lax.broadcasted_iota(jnp.int32, shape, 1) >= lax.broadcasted_iota(jnp.int32, shape, 0)
            w = jnp.where(seen, (0.5 * t + 1.0) * t + 1.0, 0.0).astype(BF16)
            gs = gs_ref[start:, head_lanes(g)]
            gv_out[start:stop, head_lanes(i)] = dot(w, gs, NN)
            gw = dot(v_ref[start:stop, head_lanes(g)], gs, NT)
            s = jnp.where(seen, gw * (FEAT ** (-0.5) + FEAT ** (-0.5) * t), 0.0).astype(BF16)
            part_q = dot(kt[:, start:stop], s, NN)
            if start == 0:
                gq_out[head_rows(i)] = part_q
            else:
                gq_out[head_rows(i), start:] += part_q
            gk_out[head_rows(i), start:stop] = dot(qt[:, start:], s, NT)


def query_grad_kernel(
    query, rim, qt_ref, gs_a, gs_b, pre_a, pre_b, a0, a1, b0, b1, taps_q, g_out, sums, wide, pre, turned_grad
):
    for own, gs, prefix, locals_ in ((True, gs_a, pre_a, (a0, a1)), (False, gs_b, pre_b, (b0, b1))):
        half = half_index(own)
        doubled(prefix, pre)
        for g in range(HALF):
            x = qt_ref[rows_of(half, g)].astype(F32)
            turned_grad[rows_of(half, g)] = locals_[g // PART][head_rows(g % PART)] + feature_grad(
                x, pre[g], gs[:, head_lanes(g)]
            )
    grad = turned_grad[...].T
    g_out[...] = grad
    fill(wide, rim[:, 0:LANES], query[...])
    for o, row in enumerate(tap_sums(grad, wide, taps_q.shape[0])):
        sums[o : o + 1] = row


def later_half(half, value, rim, kt, fk, v, state, locals_v, locals_k, gv_out, gk_put, sums_put, wide, post, taps):
    doubled(state, post)
    for g in range(HALF):
        local = locals_v[g // PART][:, head_lanes(g % PART)]
        gv_out[:, head_lanes(g)] = local + dot(fk[g], post[g], TN)
    for g in range(HALF):
        local = locals_k[g // PART][head_rows(g % PART)]
        x = kt[rows_of(half, g)].astype(F32)
        gk_put(g, local + feature_grad(x, post[g], v[:, head_lanes(g)]))
    for g in range(HALF):
        fill(wide, rim[:, lanes_of(half, g, 2 * LANES)], value[:, lanes_of(half, g)])
        for o, row in enumerate(tap_sums(gv_out[:, head_lanes(g)], wide, taps)):
            sums_put(o, g, row)


def first_later_kernel(value, rim, kt, fk, v, state, v0, v1, k0, k1, gv_out, gk_out, sums, wide, post):
    def gk_put(g, x):
        gk_out[head_rows(g)] = x

    def sums_put(o, g, row):
        sums[o : o + 1, head_lanes(g)] = row

    later_half(
        half_index(False), value, rim, kt, fk, v, state, (v0, v1), (k0, k1), gv_out, gk_put, sums_put, wide, post,
        sums.shape[0],
    )


def second_later_kernel(
    key, value, rim, kt, fk, v, state, v0, v1, k0, k1, gv_b, gk_b, sums_b, gq, sums_q, gain_a, gain_b,
    gv_out, gk_out, sums, wide, post, turned_grad,
):
    taps = sums_q.shape[0]
    rows = key.shape[0]
    half_a, half_b = half_index(True), half_index(False)

    def gk_put(g, x):
        turned_grad[rows_of(half_a, g)] = x

    def sums_put(o, g, row):
        sums[o : o + 1, lanes_of(half_a, g, 2 * LANES)] = row

    turned_grad[pl.ds(pl.multiple_of(half_b * HALF * FEAT, HALF * FEAT), HALF * FEAT)] = gk_b[...]
    later_half(
        half_a, value, rim, kt, fk, v, state, (v0, v1), (k0, k1), gv_out, gk_put, sums_put, wide, post, taps
    )
    grad = turned_grad[...].T
    gk_out[...] = grad
    fill(wide, rim[:, LANES : 2 * LANES], key[...])
    for o, row in enumerate(tap_sums(grad, wide, taps)):
        sums[o : o + 1, LANES : 2 * LANES] = row
    sums[0:taps, 0:LANES] = sums_q[...]
    sums[taps : taps + 1, 0 : 2 * LANES] = jnp.zeros((1, 2 * LANES), F32)
    heads = slice(taps + 1, 2 * taps)
    sums[heads, 0:LANES] = gq[0 : taps - 1]
    sums[heads, LANES : 2 * LANES] = grad[0 : taps - 1]
    sums[2 * taps :] = jnp.zeros((sums.shape[0] - 2 * taps, ALL), F32)
    for g in range(HALF):
        sums[0:taps, lanes_of(half_b, g, 2 * LANES)] = sums_b[:, head_lanes(g)]
        for half, gain, gv in ((half_a, gain_a, gv_out), (half_b, gain_b, gv_b)):
            sums[taps : taps + 1, lanes_of(half, g, 2 * LANES)] = gain[g : g + 1]
            sums[heads, lanes_of(half, g, 2 * LANES)] = gv[0 : taps - 1, head_lanes(g)]


def signal_rows(wide, taps, rows):
    count = taps.shape[0]
    total = taps[0:1] * wide[count - 1 : count - 1 + rows]
    for o in range(1, count):
        total = total + taps[o : o + 1] * wide[count - 1 - o : count - 1 - o + rows]
    return total.astype(BF16)


def signal_kernel(
    gq, gk, gv_a, gv_b, taps_q, taps_k, taps_v, q_out, k_out, v_out, wide, q_part, k_part, v_part, sems
):
    rows = gq.shape[0]
    copies = []
    wide[rows:] = jnp.zeros((wide.shape[0] - rows, DIM), F32)

    def one(grad, taps):
        wide[0:rows] = grad
        return signal_rows(wide, taps, rows)

    def move(part, out):
        copies.append(pltpu.make_async_copy(part, out, sems.at[len(copies)]))
        copies[-1].start()

    for i, (own, gv) in enumerate(((True, gv_a), (False, gv_b))):
        half = half_index(own)
        for g in range(HALF):
            place = lanes_of(half, g)
            slot = i * HALF + g
            v_part[slot] = one(gv[:, head_lanes(g)], taps_v[:, place])
            move(v_part.at[slot], v_out.at[:, place])
    q_part[...] = one(gq[...], taps_q[...])
    move(q_part, q_out)
    k_part[...] = one(gk[...], taps_k[...])
    move(k_part, k_out)
    for copy in copies:
        copy.wait()


def digit(bit, radix):
    return lax.rem(lax.div(lax.axis_index("seq"), bit), radix)


def combine_kernel(bit, radix, taps, final, with_own, with_next, *refs):
    *gots, own_out, next_out = refs
    sums, heads = slice(0, taps + 1), slice(taps + 1, 2 * taps)
    here = digit(bit, radix)
    total = with_own[sums]
    for got in gots:
        total = total + got[sums]
    passed = with_next[heads]
    open_ = lax.rem(lax.div(lax.axis_index("seq"), 4), max(bit // 4, 1)) == bit // 4 - 1 if bit > 4 else None
    taken = passed
    for d in range(radix):
        source = d ^ (d + 1) if d + 1 < radix else d
        taken = jnp.where(here == d, gots[source - 1][heads], taken)
    passed = taken if open_ is None else jnp.where(open_, taken, passed)
    if final:
        passed = jnp.where(digit(1, 4) == 0, passed, with_own[heads])
    rest = jnp.zeros((own_out.shape[0] - 2 * taps, ALL), F32)
    for ref, rows in ((own_out, with_own[heads]), (next_out, passed)):
        ref[sums] = total
        ref[heads] = rows
        ref[2 * taps :] = rest


def finish_kernel(
    factor, last, sums, got_1, got_2, got_3, gq, gk, gv_a, gv_b, taps_q, taps_k, taps_v, q_in, k_in, v_in,
    q_out, k_out, v_out, q_sums, k_sums, v_sums, gain_sums, wide, q_part, k_part, v_part, sems,
):
    taps = q_sums.shape[0]
    here = lax.axis_index("seq")
    heads = slice(taps + 1, 2 * taps)
    margin = taps - 1
    start = gq.shape[0] - RIM
    wide[RIM:] = jnp.zeros((wide.shape[0] - RIM, DIM), F32)
    even = lax.rem(here, 2) == 0

    def one(grad, place, taps_ref):
        follow = jnp.where(even, got_1[heads, place], got_3[heads, place])
        wide[0:RIM] = grad
        wide[RIM : RIM + margin] = jnp.where(here == last, jnp.zeros_like(follow), follow)
        return signal_rows(wide, taps_ref, RIM)

    q_part[...] = one(gq[start:], slice(0, LANES), taps_q[...])
    k_part[...] = one(gk[start:], slice(LANES, 2 * LANES), taps_k[...])
    for own, gv in ((True, gv_a), (False, gv_b)):
        half = half_index(own)
        for g in range(HALF):
            place = lanes_of(half, g)
            v_part[:, place] = one(gv[start:, head_lanes(g)], lanes_of(half, g, 2 * LANES), taps_v[:, place])
    copies = [
        pltpu.make_async_copy(part, out.at[pl.ds(start, RIM)], sems.at[i])
        for i, (part, out) in enumerate(((q_part, q_out), (k_part, k_out), (v_part, v_out)))
    ]
    for copy in copies:
        copy.start()
    rows = slice(0, taps + 1)
    total = (sums[rows] + got_1[rows] + got_2[rows] + got_3[rows]) * factor
    q_sums[...] = total[0:taps, 0:LANES]
    k_sums[...] = total[0:taps, LANES : 2 * LANES]
    v_sums[...] = total[0:taps, 2 * LANES :]
    gain_sums[...] = total[taps : taps + 1, 2 * LANES :]
    for copy in copies:
        copy.wait()


def far(x):
    return pltpu.with_memory_space_constraint(x, pltpu.HBM)


def held(*xs):
    return [pltpu.with_memory_space_constraint(x, pltpu.VMEM) for x in xs]


def call(kernel, outs, scratch, args, flops, limit=16, loose=(), **specs):
    size = lambda a: a.size * a.dtype.itemsize
    moved = sum(size(a) for a in args) + sum(size(o) for o in outs)
    return pl.pallas_call(
        kernel,
        out_shape=[o if i in loose else pltpu.VMEM(o.shape, o.dtype) for i, o in enumerate(outs)],
        scratch_shapes=scratch,
        compiler_params=pltpu.CompilerParams(vmem_limit_bytes=limit * 2**20),
        cost_estimate=pl.CostEstimate(flops=flops, bytes_accessed=moved, transcendentals=0),
        **specs,
    )(*args)


def exchange(x, distance):
    count = lax.axis_size("seq")
    return lax.ppermute(x, "seq", [(i, i ^ distance) for i in range(count)])


def tie(x, *others):
    return lax.optimization_barrier((x, *others))[0]


def on_side(bit, reverse):
    set_ = lax.rem(lax.div(lax.axis_index("seq"), bit), 2)
    return set_ == (0 if reverse else 1)


def chosen(flag, x):
    return jnp.where(flag, x, jnp.zeros_like(x))


def pair_kernel(keep, near, part, their):
    upper = lax.rem(lax.div(lax.axis_index("seq"), 2), 2)

    def half(which):
        place = pl.ds(which * PART, PART)
        return keep[place].astype(F32) + near[place].astype(F32)

    part[...] = half(upper)
    their[...] = half(1 - upper).astype(BF16)


def step_kernel(part, *refs):
    *gots, send = refs
    total = part[...]
    for got in gots:
        total = total + got[...].astype(F32)
    send[...] = total.astype(BF16)


def part_kernel(reverse, part, got_y, *rest):
    *gots, own, give = rest
    before = jnp.zeros(part.shape, F32)
    for i, got in enumerate(gots):
        before = before + chosen(on_side(4 << i, reverse), got[...].astype(F32))
    own[...] = before + chosen(on_side(2, reverse), got_y[...].astype(F32))
    give[...] = (before + chosen(jnp.logical_not(on_side(2, reverse)), part[...])).astype(BF16)


def merge_kernel(reverse, own_part, other_part, keep, near, own, give):
    upper = lax.rem(lax.div(lax.axis_index("seq"), 2), 2)
    side = on_side(1, reverse)
    for part, which in ((own_part, upper), (other_part, 1 - upper)):
        place = pl.ds(which * PART, PART)
        before = part[...].astype(F32)
        own[place] = (before + chosen(side, near[place].astype(F32))).astype(BF16)
        give[place] = (before + chosen(jnp.logical_not(side), keep[place].astype(F32))).astype(BF16)


def beyond(keep, send, reverse, works, last):
    count = lax.axis_size("seq")
    works = list(works)
    st = jax.ShapeDtypeStruct
    whole, part_shape = keep.shape, (PART, *keep.shape[1:])
    wide, narrow = st(part_shape, F32), st(part_shape, BF16)
    cost = 4 * keep.size

    def under(x):
        return tie(x, *works.pop(0)()) if works else x

    near = exchange(send, 1)
    part, their = call(pair_kernel, [wide, narrow], [], (keep, near), cost)
    got_y = exchange(their, 2)
    gots = []
    bit = 4
    while bit < count:
        send = call(step_kernel, [narrow], [], (part, got_y, *gots), cost)[0]
        gots.append(exchange(under(send), bit))
        bit *= 2
    own_part, give_part = call(
        functools.partial(part_kernel, reverse), [wide, narrow], [], (part, got_y, *gots), cost
    )
    other_part = exchange(under(give_part), 2)
    own, give = call(
        functools.partial(merge_kernel, reverse), [st(whole, BF16)] * 2, [], (own_part, other_part, keep, near), cost
    )
    other = exchange(under(give), 1)
    return own, tie(other, last(own))


def shards(query_in, key_in, value_in, conv_query, conv_key, conv_value, norm_gain, grad_out):
    rows = query_in.shape[0]
    taps = conv_query.shape[0]
    count = lax.axis_size("seq")
    total_rows = rows * count
    st = jax.ShapeDtypeStruct
    half_width = HALF * DIM
    half_state, half_wide = st((HALF, ROWS, DIM), BF16), st((rows, half_width), F32)
    half_narrow, half_features = st((rows, half_width), BF16), st((HALF, ROWS, rows), BF16)
    flat, turned_flat = st((rows, LANES), F32), st((LANES, rows), BF16)
    state_scratch = pltpu.VMEM((HALF, ROWS, DIM), BF16)
    wide = pltpu.VMEM((RIM + rows, DIM), F32)
    gain = norm_gain.reshape(HEADS, DIM)
    state_flops = HEADS * ROWS * DIM * rows
    square_flops = 2 * HALF * rows * rows * DIM

    apart = pl.BlockSpec(memory_space=pltpu.HBM)
    near = pl.BlockSpec(memory_space=pltpu.VMEM)
    ends = call(
        end_kernel,
        [st((RIM, ALL), BF16)],
        [pltpu.SemaphoreType.DMA((3,))],
        (far(query_in), far(key_in), far(value_in)),
        rows,
        in_specs=[apart] * 3,
    )[0]
    rim = lax.ppermute(ends, "seq", [(i, i + 1) for i in range(count - 1)])

    k, kt, v_b, fk_b, state_b = call(
        first_key_kernel,
        [st((rows, LANES), BF16), turned_flat, half_narrow, half_features, half_state],
        [wide],
        (key_in, value_in, rim, conv_key, conv_value),
        state_flops,
    )
    v_a, fk_a, state_a = call(
        second_key_kernel,
        [half_narrow, half_features, half_state],
        [wide],
        (*held(kt), value_in, rim, conv_value),
        state_flops,
    )
    made = {}

    def local_work(own, v):
        def work():
            if "q" not in made:
                made["q"] = call(
                    query_kernel,
                    [st((rows, LANES), BF16), turned_flat, st((HEADS, ROWS, rows), BF16)],
                    [wide],
                    (query_in, rim, conv_query),
                    state_flops,
                )
            made[own] = call(
                functools.partial(local_kernel, own),
                [half_wide],
                [],
                held(made["q"][0], k, v),
                2 * square_flops,
            )[0]
            return (made[own],)

        return work

    def norm(own, prefix, *others):
        return call(
            functools.partial(norm_kernel, own),
            [half_narrow if own else st((rows, WIDE), BF16), half_narrow, half_state, st((HALF, DIM), F32)],
            [state_scratch, pltpu.VMEM((rows, half_width), F32)],
            (*held(made[own], made["q"][2]), prefix, grad_out, gain, *held(*others)),
            2 * state_flops,
        )

    def first_norm(prefix):
        made["norm"] = norm(True, prefix)
        return made["norm"][0]

    pre_a, pre_b = beyond(
        state_a, state_b, False, [local_work(True, v_a), local_work(False, v_b)], first_norm
    )
    q, qt, fq = made["q"]
    out_a, gs_a, state_a, gain_a = made["norm"]
    tokens, gs_b, state_b, gain_b = norm(False, pre_b, out_a)
    back = []

    def first_back():
        *parts, made["out"] = call(
            first_back_kernel,
            [st((rows, PART * DIM), F32), st((PART * FEAT, rows), F32), st((PART * FEAT, rows), F32),
             st((rows, WIDE), BF16)],
            [pltpu.SemaphoreType.DMA],
            held(q, k, qt, kt, v_a, gs_a, tokens),
            2 * square_flops,
            loose=(3,),
            out_specs=[near] * 3 + [apart],
        )
        back.append(parts)
        return (parts[0],)

    def back_work(own, part, v, gs):
        def work():
            back.append(
                call(
                    functools.partial(back_kernel, own, part),
                    [st((rows, PART * DIM), F32), st((PART * FEAT, rows), F32), st((PART * FEAT, rows), F32)],
                    [],
                    held(q, k, qt, kt, v, gs),
                    2 * square_flops,
                )
            )
            return (back[-1][0],)

        return work

    def last_work():
        work = back_work(False, 1, v_b, gs_b)()[0]
        made["gq"] = call(
            query_grad_kernel,
            [flat, st((taps, LANES), F32)],
            [wide, state_scratch, pltpu.VMEM((LANES, rows), F32)],
            (query_in, rim, *held(qt, gs_a, gs_b), pre_a, pre_b, *held(*[b[1] for b in back]), conv_query),
            state_flops,
        )
        return (work, made["gq"][0])

    def first_later(state):
        made["later"] = call(
            first_later_kernel,
            [half_wide, st((HALF * FEAT, rows), F32), st((taps, half_width), F32)],
            [wide, state_scratch],
            (value_in, rim, *held(kt, fk_b, v_b), state, *held(back[2][0], back[3][0], back[2][2], back[3][2])),
            2 * state_flops,
        )
        return made["later"][0]

    works = [first_back, back_work(True, 1, v_a, gs_a), back_work(False, 0, v_b, gs_b), last_work]
    _, post_a = beyond(state_b, state_a, True, works, first_later)
    gv_b, gk_b, sums_b = made["later"]
    gq, sums_q = made["gq"]
    pack = st((-(-2 * taps // 8) * 8, ALL), F32)
    gv_a, gk, sums = call(
        second_later_kernel,
        [half_wide, flat, pack],
        [wide, state_scratch, pltpu.VMEM((LANES, rows), F32)],
        (key_in, value_in, rim, *held(kt, fk_a, v_a), post_a,
         *held(back[0][0], back[1][0], back[0][2], back[1][2], gv_b, gk_b, sums_b, gq, sums_q, gain_a, gain_b)),
        2 * state_flops,
    )
    sums_next, bit = sums, 4
    while bit < count:
        radix = 4 if 4 * bit <= count else 2
        gots = [exchange(sums_next, bit * j) for j in range(1, radix)]
        sums, sums_next = call(
            functools.partial(combine_kernel, bit, radix, taps, bit * radix == count),
            [pack, pack],
            [],
            (sums, sums_next, *gots),
            rows,
        )
        bit *= radix
    flat_narrow, wide_narrow = st((rows, LANES), BF16), st((rows, WIDE), BF16)
    grads = call(
        signal_kernel,
        [flat_narrow, flat_narrow, wide_narrow],
        [pltpu.VMEM((rows + 8, DIM), F32), pltpu.VMEM((rows, LANES), BF16), pltpu.VMEM((rows, LANES), BF16),
         pltpu.VMEM((HEADS, rows, DIM), BF16), pltpu.SemaphoreType.DMA((HEADS + 2,))],
        (*held(gq, gk, gv_a, gv_b), conv_query, conv_key, conv_value),
        2 * state_flops,
        loose=(0, 1, 2),
        out_specs=[apart] * 3,
    )
    gots = [exchange(sums_next if j == 3 else sums, j) for j in range(1, 4)]
    grad_query, grad_key, grad_value, taps_query, taps_key, taps_value, taps_gain = call(
        functools.partial(finish_kernel, total_rows ** (-0.5), count - 1),
        [flat_narrow, flat_narrow, wide_narrow,
         st((taps, LANES), F32), st((taps, LANES), F32), st((taps, WIDE), F32), st((1, WIDE), F32)],
        [pltpu.VMEM((RIM + 8, DIM), F32), pltpu.VMEM((RIM, LANES), BF16), pltpu.VMEM((RIM, LANES), BF16),
         pltpu.VMEM((RIM, WIDE), BF16), pltpu.SemaphoreType.DMA((3,))],
        (sums, *gots, *held(gq, gk, gv_a, gv_b), conv_query, conv_key, conv_value, *[far(g) for g in grads]),
        rows,
        loose=range(7),
        in_specs=[near] * 11 + [apart] * 3,
        out_specs=[apart] * 3 + [near] * 4,
        input_output_aliases={11: 0, 12: 1, 13: 2},
    )
    return (
        made["out"],
        grad_query,
        grad_key,
        grad_value,
        taps_query,
        taps_key,
        taps_value,
        taps_gain.reshape(WIDE),
    )


def solution(mesh):
    rows = P(("groups", "seq"), None)
    return jax.shard_map(
        shards,
        mesh=mesh,
        in_specs=(rows, rows, rows, P(), P(), P(), P(), rows),
        out_specs=(rows, rows, rows, rows, P("groups", None), P("groups", None), P("groups", None), P("groups")),
        check_vma=False,
    )
```

```python
import functools

import jax
import jax.numpy as jnp
from jax import lax
from jax.experimental import pallas as pl
from jax.experimental.pallas import tpu as pltpu
from jax.sharding import PartitionSpec as P

HEADS = 8
HALF = HEADS // 2
PART = HEADS // 4
FEAT = 16
DIM = 128
EPSILON = 1e-06
LANES = HEADS * FEAT
WIDE = HEADS * DIM
ALL = 2 * LANES + WIDE
ROWS = 160
LIN = 128
TAIL = 144
RIM = 16
STEP = 128
F32 = jnp.float32
BF16 = jnp.bfloat16

NN = (((1,), (0,)), ((), ()))
NT = (((1,), (1,)), ((), ()))
TN = (((0,), (0,)), ((), ()))


def dot(a, b, dims):
    return lax.dot_general(a, b, dims, preferred_element_type=F32)


def head_rows(h):
    return slice(h * FEAT, (h + 1) * FEAT)


def head_lanes(h):
    return slice(h * DIM, (h + 1) * DIM)


def conv(wide_ref, taps, rows):
    margin = taps.shape[0] - 1
    total = taps[0:1] * wide_ref[RIM - margin : RIM - margin + rows]
    for o in range(1, margin + 1):
        total = total + taps[o : o + 1] * wide_ref[RIM - margin + o : RIM - margin + o + rows]
    return total


def tap_sums(grad, wide_ref, taps):
    rows = grad.shape[0]
    start = RIM - (taps - 1)
    return [
        jnp.sum(grad * wide_ref[start + o : start + o + rows], axis=0, keepdims=True)
        for o in range(taps)
    ]


def turned(x, shift):
    return x if shift % FEAT == 0 else pltpu.roll(x, shift % FEAT, 0)


def features(x):
    half = (0.5 / FEAT) ** 0.5
    pieces = [(x * turned(x, FEAT - d) * half).astype(BF16) for d in range(8)]
    pieces.append((x * FEAT ** (-0.25)).astype(BF16))
    rows = lax.broadcasted_iota(jnp.int32, (8, x.shape[1]), 0)
    one = jnp.where(rows == 0, 1.0, 0.0).astype(F32)
    pieces.append(jnp.concatenate([x[:8] * x[8:] * half, one], axis=0).astype(BF16))
    return jnp.concatenate(pieces, axis=0)


def feature_grad(x, state, vector):
    g = dot(state, vector, NT)
    crossed = 2.0 * g[0:FEAT] * x
    for d in range(1, 8):
        part = g[d * FEAT : (d + 1) * FEAT]
        crossed = crossed + part * turned(x, FEAT - d) + turned(part * x, d)
    part = g[TAIL : TAIL + 8]
    crossed = crossed + jnp.concatenate([part * x[8:], part * x[:8]], axis=0)
    return g[LIN:TAIL] * FEAT ** (-0.25) + crossed * (0.5 / FEAT) ** 0.5


def half_index(own):
    core = lax.rem(lax.axis_index("seq"), 2)
    return core if own else 1 - core


def rows_of(half, g):
    return pl.ds(pl.multiple_of((half * HALF + g) * FEAT, FEAT), FEAT)


def lanes_of(half, g, start=0):
    return pl.ds(pl.multiple_of(start + (half * HALF + g) * DIM, DIM), DIM)


def doubled(state_ref, out_ref):
    rows = lax.broadcasted_iota(jnp.int32, (ROWS, DIM), 0)
    pair = ((rows >= FEAT) & (rows < LIN)) | ((rows >= TAIL) & (rows < TAIL + 8))
    weight = jnp.where(pair, 2.0, 1.0).astype(F32)
    for g in range(HALF):
        out_ref[g] = (state_ref[g].astype(F32) * weight).astype(BF16)


def head_mask(h):
    lanes = lax.broadcasted_iota(jnp.int32, (1, LANES), 1)
    return jnp.where(lanes // FEAT == h, 1.0, 0.0).astype(F32).astype(BF16)


def fill(wide, rim, rest):
    wide[0:RIM] = rim.astype(F32)
    wide[RIM : RIM + rest.shape[0]] = rest.astype(F32)


def end_kernel(query, key, value, out, sems):
    start = query.shape[0] - RIM
    copies = [
        pltpu.make_async_copy(ref.at[pl.ds(start, RIM)], out.at[:, pl.ds(lane, ref.shape[1])], sems.at[i])
        for i, (ref, lane) in enumerate(((query, 0), (key, LANES), (value, 2 * LANES)))
    ]
    for copy in copies:
        copy.start()
    for copy in copies:
        copy.wait()


def value_states(half, kt, value, rim, taps_v, v_out, f_out, state_out, wide):
    rows = value.shape[0]
    for g in range(HALF):
        f_out[g] = features(kt[rows_of(half, g)].astype(F32))
    for g in range(HALF):
        fill(wide, rim[:, lanes_of(half, g, 2 * LANES)], value[:, lanes_of(half, g)])
        v_out[:, head_lanes(g)] = conv(wide, taps_v[:, lanes_of(half, g)], rows).astype(BF16)
    for g in range(HALF):
        state_out[g] = dot(f_out[g], v_out[:, head_lanes(g)], NN).astype(BF16)


def first_key_kernel(key, value, rim, taps_k, taps_v, k_out, kt_out, v_out, f_out, state_out, wide):
    rows = key.shape[0]
    fill(wide, rim[:, LANES : 2 * LANES], key[...])
    k = conv(wide, taps_k[...], rows).astype(BF16)
    k_out[...] = k
    kt_out[...] = k.astype(F32).T.astype(BF16)
    value_states(half_index(False), kt_out, value, rim, taps_v, v_out, f_out, state_out, wide)


def second_key_kernel(kt, value, rim, taps_v, v_out, f_out, state_out, wide):
    value_states(half_index(True), kt, value, rim, taps_v, v_out, f_out, state_out, wide)


def query_kernel(query, rim, taps_q, q_out, qt_out, fq_out, wide):
    rows = query.shape[0]
    fill(wide, rim[:, 0:LANES], query[...])
    q = conv(wide, taps_q[...], rows).astype(BF16)
    q_out[...] = q
    qt = q.astype(F32).T
    qt_out[...] = qt.astype(BF16)
    for h in range(HEADS):
        fq_out[h] = features(qt[head_rows(h)])


def local_kernel(own, q_ref, k_ref, v_ref, out):
    rows = q_ref.shape[0]
    half = half_index(own)
    quarter = q_ref[...] * jnp.asarray(FEAT ** (-0.5), BF16)
    for g in range(HALF):
        qs = quarter * head_mask(half * HALF + g)
        for start in range(0, rows, STEP):
            stop = start + STEP
            t = dot(qs[start:stop], k_ref[0:stop], NT)
            w = (0.5 * t + 1.0) * t + 1.0
            at = lax.broadcasted_iota(jnp.int32, (STEP, stop), 0) + start
            w = jnp.where(at >= lax.broadcasted_iota(jnp.int32, (STEP, stop), 1), w, 0.0)
            out[start:stop, head_lanes(g)] = dot(w.astype(BF16), v_ref[0:stop, head_lanes(g)], NN)


def norm_kernel(own, local, fq, prefix, grad, gain, *refs):
    *others, out, gs_out, state_out, gain_out, pre, summed_ref = refs
    half = half_index(own)
    doubled(prefix, pre)
    for other in others:
        for g in range(HALF):
            out[:, lanes_of(1 - half, g)] = other[:, head_lanes(g)]
    for g in range(HALF):
        place = head_lanes(g)
        summed_ref[:, place] = local[:, place] + dot(fq[half * HALF + g], pre[g], TN)
    for g in range(HALF):
        place = head_lanes(g)
        summed = summed_ref[:, place]
        scale = lax.rsqrt(jnp.mean(summed * summed, axis=-1, keepdims=True) + EPSILON)
        normal = summed * scale
        weight = gain[pl.ds(half * HALF + g, 1)]
        out[:, place if own else lanes_of(half, g)] = (normal * weight).astype(BF16)
        incoming = grad[:, lanes_of(half, g)].astype(F32)
        gain_out[g : g + 1] = jnp.sum(incoming * normal, axis=0, keepdims=True)
        upstream = incoming * weight
        gs = scale * (upstream - normal * jnp.mean(normal * upstream, axis=-1, keepdims=True))
        gs = gs.astype(BF16)
        gs_out[:, place] = gs
        state_out[g] = dot(fq[half * HALF + g], gs, NN).astype(BF16)


def first_back_kernel(q_ref, k_ref, qt_ref, kt_ref, v_ref, gs_ref, tokens, gv_out, gq_out, gk_out, out, sem):
    copy = pltpu.make_async_copy(tokens, out, sem)
    copy.start()
    back_kernel(True, 0, q_ref, k_ref, qt_ref, kt_ref, v_ref, gs_ref, gv_out, gq_out, gk_out)
    copy.wait()


def back_kernel(own, part, q_ref, k_ref, qt_ref, kt_ref, v_ref, gs_ref, gv_out, gq_out, gk_out):
    rows = q_ref.shape[0]
    half = half_index(own)
    quarter = q_ref[...] * jnp.asarray(FEAT ** (-0.5), BF16)
    for i in range(PART):
        g = part * PART + i
        ks = k_ref[...] * head_mask(half * HALF + g)
        qt = qt_ref[rows_of(half, g)]
        kt = kt_ref[rows_of(half, g)]
        for start in range(0, rows, STEP):
            stop = start + STEP
            shape = (STEP, rows - start)
            t = dot(ks[start:stop], quarter[start:], NT)
            seen = lax.broadcasted_iota(jnp.int32, shape, 1) >= lax.broadcasted_iota(jnp.int32, shape, 0)
            w = jnp.where(seen, (0.5 * t + 1.0) * t + 1.0, 0.0).astype(BF16)
            gs = gs_ref[start:, head_lanes(g)]
            gv_out[start:stop, head_lanes(i)] = dot(w, gs, NN)
            gw = dot(v_ref[start:stop, head_lanes(g)], gs, NT)
            s = jnp.where(seen, gw * (FEAT ** (-0.5) + FEAT ** (-0.5) * t), 0.0).astype(BF16)
            part_q = dot(kt[:, start:stop], s, NN)
            if start == 0:
                gq_out[head_rows(i)] = part_q
            else:
                gq_out[head_rows(i), start:] += part_q
            gk_out[head_rows(i), start:stop] = dot(qt[:, start:], s, NT)


def query_grad_kernel(
    query, rim, qt_ref, gs_a, gs_b, pre_a, pre_b, a0, a1, b0, b1, taps_q, g_out, sums, wide, pre, turned_grad
):
    for own, gs, prefix, locals_ in ((True, gs_a, pre_a, (a0, a1)), (False, gs_b, pre_b, (b0, b1))):
        half = half_index(own)
        doubled(prefix, pre)
        for g in range(HALF):
            x = qt_ref[rows_of(half, g)].astype(F32)
            turned_grad[rows_of(half, g)] = locals_[g // PART][head_rows(g % PART)] + feature_grad(
                x, pre[g], gs[:, head_lanes(g)]
            )
    grad = turned_grad[...].T
    g_out[...] = grad
    fill(wide, rim[:, 0:LANES], query[...])
    for o, row in enumerate(tap_sums(grad, wide, taps_q.shape[0])):
        sums[o : o + 1] = row


def later_half(half, value, rim, kt, fk, v, state, locals_v, locals_k, gv_out, gk_put, sums_put, wide, post, taps):
    doubled(state, post)
    for g in range(HALF):
        local = locals_v[g // PART][:, head_lanes(g % PART)]
        gv_out[:, head_lanes(g)] = local + dot(fk[g], post[g], TN)
    for g in range(HALF):
        local = locals_k[g // PART][head_rows(g % PART)]
        x = kt[rows_of(half, g)].astype(F32)
        gk_put(g, local + feature_grad(x, post[g], v[:, head_lanes(g)]))
    for g in range(HALF):
        fill(wide, rim[:, lanes_of(half, g, 2 * LANES)], value[:, lanes_of(half, g)])
        for o, row in enumerate(tap_sums(gv_out[:, head_lanes(g)], wide, taps)):
            sums_put(o, g, row)


def first_later_kernel(value, rim, kt, fk, v, state, v0, v1, k0, k1, gv_out, gk_out, sums, wide, post):
    def gk_put(g, x):
        gk_out[head_rows(g)] = x

    def sums_put(o, g, row):
        sums[o : o + 1, head_lanes(g)] = row

    later_half(
        half_index(False), value, rim, kt, fk, v, state, (v0, v1), (k0, k1), gv_out, gk_put, sums_put, wide, post,
        sums.shape[0],
    )


def second_later_kernel(
    key, value, rim, kt, fk, v, state, v0, v1, k0, k1, gv_b, gk_b, sums_b, gq, sums_q, gain_a, gain_b,
    gv_out, gk_out, head_out, sums, wide, post, turned_grad,
):
    taps = sums_q.shape[0]
    rows = key.shape[0]
    half_a, half_b = half_index(True), half_index(False)

    def gk_put(g, x):
        turned_grad[rows_of(half_a, g)] = x

    def sums_put(o, g, row):
        sums[o : o + 1, lanes_of(half_a, g, 2 * LANES)] = row

    turned_grad[pl.ds(pl.multiple_of(half_b * HALF * FEAT, HALF * FEAT), HALF * FEAT)] = gk_b[...]
    later_half(
        half_a, value, rim, kt, fk, v, state, (v0, v1), (k0, k1), gv_out, gk_put, sums_put, wide, post, taps
    )
    grad = turned_grad[...].T
    gk_out[...] = grad
    fill(wide, rim[:, LANES : 2 * LANES], key[...])
    for o, row in enumerate(tap_sums(grad, wide, taps)):
        sums[o : o + 1, LANES : 2 * LANES] = row
    sums[0:taps, 0:LANES] = sums_q[...]
    sums[taps : taps + 1, 0 : 2 * LANES] = jnp.zeros((1, 2 * LANES), F32)
    head_out[:, 0:LANES] = gq[0:8]
    head_out[:, LANES : 2 * LANES] = grad[0:8]
    for g in range(HALF):
        sums[0:taps, lanes_of(half_b, g, 2 * LANES)] = sums_b[:, head_lanes(g)]
        for half, gain, gv in ((half_a, gain_a, gv_out), (half_b, gain_b, gv_b)):
            sums[taps : taps + 1, lanes_of(half, g, 2 * LANES)] = gain[g : g + 1]
            head_out[:, lanes_of(half, g, 2 * LANES)] = gv[0:8, head_lanes(g)]


def signal_kernel(
    gq, gk, gv_a, gv_b, follow, taps_q, taps_k, taps_v, q_out, k_out, v_out, wide, q_part, k_part, v_part, sems
):
    rows = gq.shape[0]
    count = taps_q.shape[0]
    copies = []

    def one(grad, after, taps):
        wide[0:rows] = grad
        wide[rows : rows + 8] = after
        total = taps[0:1] * wide[count - 1 : count - 1 + rows]
        for o in range(1, count):
            total = total + taps[o : o + 1] * wide[count - 1 - o : count - 1 - o + rows]
        return total.astype(BF16)

    def move(part, out):
        copies.append(pltpu.make_async_copy(part, out, sems.at[len(copies)]))
        copies[-1].start()

    for i, (own, gv) in enumerate(((True, gv_a), (False, gv_b))):
        half = half_index(own)
        for g in range(HALF):
            place = lanes_of(half, g)
            slot = i * HALF + g
            after = follow[:, lanes_of(half, g, 2 * LANES)]
            v_part[slot] = one(gv[:, head_lanes(g)], after, taps_v[:, place])
            move(v_part.at[slot], v_out.at[:, place])
    q_part[...] = one(gq[...], follow[:, 0:LANES], taps_q[...])
    move(q_part, q_out)
    k_part[...] = one(gk[...], follow[:, LANES : 2 * LANES], taps_k[...])
    move(k_part, k_out)
    for copy in copies:
        copy.wait()


def finish_kernel(factor, *refs):
    *terms, q_out, k_out, v_out, gain_out = refs
    taps = q_out.shape[0]
    total = terms[0][...]
    for term in terms[1:]:
        total = total + term[...]
    total = total * factor
    q_out[...] = total[0:taps, 0:LANES]
    k_out[...] = total[0:taps, LANES : 2 * LANES]
    v_out[...] = total[0:taps, 2 * LANES :]
    gain_out[...] = total[taps : taps + 1, 2 * LANES :]


def far(x):
    return pltpu.with_memory_space_constraint(x, pltpu.HBM)


def held(*xs):
    return [pltpu.with_memory_space_constraint(x, pltpu.VMEM) for x in xs]


def call(kernel, outs, scratch, args, flops, limit=16, loose=(), **specs):
    size = lambda a: a.size * a.dtype.itemsize
    moved = sum(size(a) for a in args) + sum(size(o) for o in outs)
    return pl.pallas_call(
        kernel,
        out_shape=[o if i in loose else pltpu.VMEM(o.shape, o.dtype) for i, o in enumerate(outs)],
        scratch_shapes=scratch,
        compiler_params=pltpu.CompilerParams(vmem_limit_bytes=limit * 2**20),
        cost_estimate=pl.CostEstimate(flops=flops, bytes_accessed=moved, transcendentals=0),
        **specs,
    )(*args)


def exchange(x, distance):
    count = lax.axis_size("seq")
    return lax.ppermute(x, "seq", [(i, i ^ distance) for i in range(count)])


def tie(x, *others):
    return lax.optimization_barrier((x, *others))[0]


def on_side(bit, reverse):
    set_ = lax.rem(lax.div(lax.axis_index("seq"), bit), 2)
    return set_ == (0 if reverse else 1)


def chosen(flag, x):
    return jnp.where(flag, x, jnp.zeros_like(x))


def pair_kernel(keep, near, part, their):
    upper = lax.rem(lax.div(lax.axis_index("seq"), 2), 2)

    def half(which):
        place = pl.ds(which * PART, PART)
        return keep[place].astype(F32) + near[place].astype(F32)

    part[...] = half(upper)
    their[...] = half(1 - upper).astype(BF16)


def step_kernel(part, *refs):
    *gots, send = refs
    total = part[...]
    for got in gots:
        total = total + got[...].astype(F32)
    send[...] = total.astype(BF16)


def part_kernel(reverse, part, got_y, *rest):
    *gots, own, give = rest
    before = jnp.zeros(part.shape, F32)
    for i, got in enumerate(gots):
        before = before + chosen(on_side(4 << i, reverse), got[...].astype(F32))
    own[...] = before + chosen(on_side(2, reverse), got_y[...].astype(F32))
    give[...] = (before + chosen(jnp.logical_not(on_side(2, reverse)), part[...])).astype(BF16)


def merge_kernel(reverse, own_part, other_part, keep, near, own, give):
    upper = lax.rem(lax.div(lax.axis_index("seq"), 2), 2)
    side = on_side(1, reverse)
    for part, which in ((own_part, upper), (other_part, 1 - upper)):
        place = pl.ds(which * PART, PART)
        before = part[...].astype(F32)
        own[place] = (before + chosen(side, near[place].astype(F32))).astype(BF16)
        give[place] = (before + chosen(jnp.logical_not(side), keep[place].astype(F32))).astype(BF16)


def beyond(keep, send, reverse, works, last):
    count = lax.axis_size("seq")
    works = list(works)
    st = jax.ShapeDtypeStruct
    whole, part_shape = keep.shape, (PART, *keep.shape[1:])
    wide, narrow = st(part_shape, F32), st(part_shape, BF16)
    cost = 4 * keep.size

    def under(x):
        return tie(x, *works.pop(0)()) if works else x

    near = exchange(send, 1)
    part, their = call(pair_kernel, [wide, narrow], [], (keep, near), cost)
    got_y = exchange(their, 2)
    gots = []
    bit = 4
    while bit < count:
        send = call(step_kernel, [narrow], [], (part, got_y, *gots), cost)[0]
        gots.append(exchange(under(send), bit))
        bit *= 2
    own_part, give_part = call(
        functools.partial(part_kernel, reverse), [wide, narrow], [], (part, got_y, *gots), cost
    )
    other_part = exchange(under(give_part), 2)
    own, give = call(
        functools.partial(merge_kernel, reverse), [st(whole, BF16)] * 2, [], (own_part, other_part, keep, near), cost
    )
    other = exchange(under(give), 1)
    return own, tie(other, last(own))


def shards(query_in, key_in, value_in, conv_query, conv_key, conv_value, norm_gain, grad_out):
    rows = query_in.shape[0]
    taps = conv_query.shape[0]
    count = lax.axis_size("seq")
    total_rows = rows * count
    st = jax.ShapeDtypeStruct
    half_width = HALF * DIM
    half_state, half_wide = st((HALF, ROWS, DIM), BF16), st((rows, half_width), F32)
    half_narrow, half_features = st((rows, half_width), BF16), st((HALF, ROWS, rows), BF16)
    flat, turned_flat = st((rows, LANES), F32), st((LANES, rows), BF16)
    state_scratch = pltpu.VMEM((HALF, ROWS, DIM), BF16)
    wide = pltpu.VMEM((RIM + rows, DIM), F32)
    gain = norm_gain.reshape(HEADS, DIM)
    state_flops = HEADS * ROWS * DIM * rows
    square_flops = 2 * HALF * rows * rows * DIM

    apart = pl.BlockSpec(memory_space=pltpu.HBM)
    near = pl.BlockSpec(memory_space=pltpu.VMEM)
    ends = call(
        end_kernel,
        [st((RIM, ALL), BF16)],
        [pltpu.SemaphoreType.DMA((3,))],
        (far(query_in), far(key_in), far(value_in)),
        rows,
        in_specs=[apart] * 3,
    )[0]
    rim = lax.ppermute(ends, "seq", [(i, i + 1) for i in range(count - 1)])

    k, kt, v_b, fk_b, state_b = call(
        first_key_kernel,
        [st((rows, LANES), BF16), turned_flat, half_narrow, half_features, half_state],
        [wide],
        (key_in, value_in, rim, conv_key, conv_value),
        state_flops,
    )
    v_a, fk_a, state_a = call(
        second_key_kernel,
        [half_narrow, half_features, half_state],
        [wide],
        (*held(kt), value_in, rim, conv_value),
        state_flops,
    )
    made = {}

    def local_work(own, v):
        def work():
            if "q" not in made:
                made["q"] = call(
                    query_kernel,
                    [st((rows, LANES), BF16), turned_flat, st((HEADS, ROWS, rows), BF16)],
                    [wide],
                    (query_in, rim, conv_query),
                    state_flops,
                )
            made[own] = call(
                functools.partial(local_kernel, own),
                [half_wide],
                [],
                held(made["q"][0], k, v),
                2 * square_flops,
            )[0]
            return (made[own],)

        return work

    def norm(own, prefix, *others):
        return call(
            functools.partial(norm_kernel, own),
            [half_narrow if own else st((rows, WIDE), BF16), half_narrow, half_state, st((HALF, DIM), F32)],
            [state_scratch, pltpu.VMEM((rows, half_width), F32)],
            (*held(made[own], made["q"][2]), prefix, grad_out, gain, *held(*others)),
            2 * state_flops,
        )

    def first_norm(prefix):
        made["norm"] = norm(True, prefix)
        return made["norm"][0]

    pre_a, pre_b = beyond(
        state_a, state_b, False, [local_work(True, v_a), local_work(False, v_b)], first_norm
    )
    q, qt, fq = made["q"]
    out_a, gs_a, state_a, gain_a = made["norm"]
    tokens, gs_b, state_b, gain_b = norm(False, pre_b, out_a)
    back = []

    def first_back():
        *parts, made["out"] = call(
            first_back_kernel,
            [st((rows, PART * DIM), F32), st((PART * FEAT, rows), F32), st((PART * FEAT, rows), F32),
             st((rows, WIDE), BF16)],
            [pltpu.SemaphoreType.DMA],
            held(q, k, qt, kt, v_a, gs_a, tokens),
            2 * square_flops,
            loose=(3,),
            out_specs=[near] * 3 + [apart],
        )
        back.append(parts)
        return (parts[0],)

    def back_work(own, part, v, gs):
        def work():
            back.append(
                call(
                    functools.partial(back_kernel, own, part),
                    [st((rows, PART * DIM), F32), st((PART * FEAT, rows), F32), st((PART * FEAT, rows), F32)],
                    [],
                    held(q, k, qt, kt, v, gs),
                    2 * square_flops,
                )
            )
            return (back[-1][0],)

        return work

    def last_work():
        work = back_work(False, 1, v_b, gs_b)()[0]
        made["gq"] = call(
            query_grad_kernel,
            [flat, st((taps, LANES), F32)],
            [wide, state_scratch, pltpu.VMEM((LANES, rows), F32)],
            (query_in, rim, *held(qt, gs_a, gs_b), pre_a, pre_b, *held(*[b[1] for b in back]), conv_query),
            state_flops,
        )
        return (work, made["gq"][0])

    def first_later(state):
        made["later"] = call(
            first_later_kernel,
            [half_wide, st((HALF * FEAT, rows), F32), st((taps, half_width), F32)],
            [wide, state_scratch],
            (value_in, rim, *held(kt, fk_b, v_b), state, *held(back[2][0], back[3][0], back[2][2], back[3][2])),
            2 * state_flops,
        )
        return made["later"][0]

    works = [first_back, back_work(True, 1, v_a, gs_a), back_work(False, 0, v_b, gs_b), last_work]
    _, post_a = beyond(state_b, state_a, True, works, first_later)
    gv_b, gk_b, sums_b = made["later"]
    gq, sums_q = made["gq"]
    gv_a, gk, heads, sums = call(
        second_later_kernel,
        [half_wide, flat, st((8, ALL), F32), st((taps + 1, ALL), F32)],
        [wide, state_scratch, pltpu.VMEM((LANES, rows), F32)],
        (key_in, value_in, rim, *held(kt, fk_a, v_a), post_a,
         *held(back[0][0], back[1][0], back[0][2], back[1][2], gv_b, gk_b, sums_b, gq, sums_q, gain_a, gain_b)),
        2 * state_flops,
    )
    follow = lax.ppermute(heads, "seq", [(i + 1, i) for i in range(count - 1)])
    bit = 4
    while bit < count:
        group = (bit, 2 * bit, 3 * bit) if 2 * bit < count else (bit,)
        for got in [exchange(sums, distance) for distance in group]:
            sums = sums + got
        bit *= len(group) + 1
    flat_narrow = st((rows, LANES), BF16)
    grad_query, grad_key, grad_value = call(
        signal_kernel,
        [flat_narrow, flat_narrow, st((rows, WIDE), BF16)],
        [pltpu.VMEM((rows + 8, DIM), F32), pltpu.VMEM((rows, LANES), BF16), pltpu.VMEM((rows, LANES), BF16),
         pltpu.VMEM((HEADS, rows, DIM), BF16), pltpu.SemaphoreType.DMA((HEADS + 2,))],
        (*held(gq, gk, gv_a, gv_b), follow, conv_query, conv_key, conv_value),
        2 * state_flops,
        loose=(0, 1, 2),
        out_specs=[apart] * 3,
    )
    taps_query, taps_key, taps_value, taps_gain = call(
        functools.partial(finish_kernel, total_rows ** (-0.5)),
        [st((taps, LANES), F32), st((taps, LANES), F32), st((taps, WIDE), F32), st((1, WIDE), F32)],
        [],
        (tie(sums, grad_value), *[exchange(sums, distance) for distance in (1, 2, 3)]),
        rows,
        loose=(0, 1, 2, 3),
    )
    return (
        made["out"],
        grad_query,
        grad_key,
        grad_value,
        taps_query,
        taps_key,
        taps_value,
        taps_gain.reshape(WIDE),
    )


def solution(mesh):
    rows = P(("groups", "seq"), None)
    return jax.shard_map(
        shards,
        mesh=mesh,
        in_specs=(rows, rows, rows, P(), P(), P(), P(), rows),
        out_specs=(rows, rows, rows, rows, P("groups", None), P("groups", None), P("groups", None), P("groups")),
        check_vma=False,
    )
```

```python
import functools

import jax
import jax.numpy as jnp
from jax import lax
from jax.experimental import pallas as pl
from jax.experimental.pallas import tpu as pltpu
from jax.sharding import PartitionSpec as P

HEADS = 8
HALF = HEADS // 2
PART = HEADS // 4
FEAT = 16
DIM = 128
EPSILON = 1e-06
LANES = HEADS * FEAT
WIDE = HEADS * DIM
ALL = 2 * LANES + WIDE
ROWS = 160
LIN = 128
TAIL = 144
RIM = 16
STEP = 128
CUT = 128
F32 = jnp.float32
BF16 = jnp.bfloat16

NN = (((1,), (0,)), ((), ()))
NT = (((1,), (1,)), ((), ()))
TN = (((0,), (0,)), ((), ()))


def dot(a, b, dims):
    return lax.dot_general(a, b, dims, preferred_element_type=F32)


def head_rows(h):
    return slice(h * FEAT, (h + 1) * FEAT)


def head_lanes(h):
    return slice(h * DIM, (h + 1) * DIM)


def conv(wide_ref, taps, rows):
    margin = taps.shape[0] - 1
    total = taps[0:1] * wide_ref[RIM - margin : RIM - margin + rows]
    for o in range(1, margin + 1):
        total = total + taps[o : o + 1] * wide_ref[RIM - margin + o : RIM - margin + o + rows]
    return total


def tap_sums(grad, wide_ref, taps):
    rows = grad.shape[0]
    start = RIM - (taps - 1)
    return [
        jnp.sum(grad * wide_ref[start + o : start + o + rows], axis=0, keepdims=True)
        for o in range(taps)
    ]


def turned(x, shift):
    return x if shift % FEAT == 0 else pltpu.roll(x, shift % FEAT, 0)


def features(x):
    half = (0.5 / FEAT) ** 0.5
    pieces = [(x * turned(x, FEAT - d) * half).astype(BF16) for d in range(8)]
    pieces.append((x * FEAT ** (-0.25)).astype(BF16))
    rows = lax.broadcasted_iota(jnp.int32, (8, x.shape[1]), 0)
    one = jnp.where(rows == 0, 1.0, 0.0).astype(F32)
    pieces.append(jnp.concatenate([x[:8] * x[8:] * half, one], axis=0).astype(BF16))
    return jnp.concatenate(pieces, axis=0)


def feature_grad(x, state, vector):
    g = dot(state, vector, NT)
    crossed = 2.0 * g[0:FEAT] * x
    for d in range(1, 8):
        part = g[d * FEAT : (d + 1) * FEAT]
        crossed = crossed + part * turned(x, FEAT - d) + turned(part * x, d)
    part = g[TAIL : TAIL + 8]
    crossed = crossed + jnp.concatenate([part * x[8:], part * x[:8]], axis=0)
    return g[LIN:TAIL] * FEAT ** (-0.25) + crossed * (0.5 / FEAT) ** 0.5


def half_index(own):
    core = lax.rem(lax.axis_index("seq"), 2)
    return core if own else 1 - core


def rows_of(half, g):
    return pl.ds(pl.multiple_of((half * HALF + g) * FEAT, FEAT), FEAT)


def lanes_of(half, g, start=0):
    return pl.ds(pl.multiple_of(start + (half * HALF + g) * DIM, DIM), DIM)


def doubled(state_ref, out_ref):
    rows = lax.broadcasted_iota(jnp.int32, (ROWS, DIM), 0)
    pair = ((rows >= FEAT) & (rows < LIN)) | ((rows >= TAIL) & (rows < TAIL + 8))
    weight = jnp.where(pair, 2.0, 1.0).astype(F32)
    for g in range(HALF):
        out_ref[g] = (state_ref[g].astype(F32) * weight).astype(BF16)


def head_mask(h):
    lanes = lax.broadcasted_iota(jnp.int32, (1, LANES), 1)
    return jnp.where(lanes // FEAT == h, 1.0, 0.0).astype(F32).astype(BF16)


def fill(wide, rim, rest):
    wide[0:RIM] = rim.astype(F32)
    wide[RIM : RIM + rest.shape[0]] = rest.astype(F32)


def end_kernel(query, key, value, out, sems):
    start = query.shape[0] - RIM
    copies = [
        pltpu.make_async_copy(ref.at[pl.ds(start, RIM)], out.at[:, pl.ds(lane, ref.shape[1])], sems.at[i])
        for i, (ref, lane) in enumerate(((query, 0), (key, LANES), (value, 2 * LANES)))
    ]
    for copy in copies:
        copy.start()
    for copy in copies:
        copy.wait()


def bulk_kernel(
    key, value, taps_k, taps_v, k_out, kt_out, v_b, f_b, state_b, v_a, f_a, state_a, wide
):
    rows = key.shape[0] - CUT
    fill(wide, key[CUT - RIM : CUT], key[CUT:])
    k = conv(wide, taps_k[...], rows).astype(BF16)
    k_out[...] = k
    kt_out[...] = k.astype(F32).T.astype(BF16)
    for own, v_out, f_out, state_out in ((False, v_b, f_b, state_b), (True, v_a, f_a, state_a)):
        half = half_index(own)
        for g in range(HALF):
            f_out[g] = features(kt_out[rows_of(half, g)].astype(F32))
        for g in range(HALF):
            lanes = lanes_of(half, g)
            fill(wide, value[CUT - RIM : CUT, lanes], value[CUT:, lanes])
            v_out[:, head_lanes(g)] = conv(wide, taps_v[:, lanes], rows).astype(BF16)
        for g in range(HALF):
            state_out[g] = dot(f_out[g], v_out[:, head_lanes(g)], NN)


def value_states(half, kt, value, rim, taps_v, v_rest, f_rest, state_rest, v_out, f_out, state_out, wide):
    for g in range(HALF):
        f_out[g, :, 0:CUT] = features(kt[rows_of(half, g), 0:CUT].astype(F32))
        f_out[g, :, CUT:] = f_rest[g]
    v_out[CUT:] = v_rest[...]
    for g in range(HALF):
        lanes = lanes_of(half, g)
        fill(wide, rim[:, lanes_of(half, g, 2 * LANES)], value[0:CUT, lanes])
        v_out[0:CUT, head_lanes(g)] = conv(wide, taps_v[:, lanes], CUT).astype(BF16)
    for g in range(HALF):
        first = dot(f_out[g, :, 0:CUT], v_out[0:CUT, head_lanes(g)], NN)
        state_out[g] = (state_rest[g] + first).astype(BF16)


def first_key_kernel(
    key, value, rim, taps_k, taps_v, k_rest, kt_rest, v_rest, f_rest, state_rest,
    k_out, kt_out, v_out, f_out, state_out, wide,
):
    fill(wide, rim[:, LANES : 2 * LANES], key[0:CUT])
    k = conv(wide, taps_k[...], CUT).astype(BF16)
    k_out[0:CUT] = k
    k_out[CUT:] = k_rest[...]
    kt_out[:, 0:CUT] = k.astype(F32).T.astype(BF16)
    kt_out[:, CUT:] = kt_rest[...]
    value_states(
        half_index(False), kt_out, value, rim, taps_v, v_rest, f_rest, state_rest, v_out, f_out, state_out, wide
    )


def second_key_kernel(kt, value, rim, taps_v, v_rest, f_rest, state_rest, v_out, f_out, state_out, wide):
    value_states(
        half_index(True), kt, value, rim, taps_v, v_rest, f_rest, state_rest, v_out, f_out, state_out, wide
    )


def query_kernel(query, rim, taps_q, q_out, qt_out, fq_out, wide):
    rows = query.shape[0]
    fill(wide, rim[:, 0:LANES], query[...])
    q = conv(wide, taps_q[...], rows).astype(BF16)
    q_out[...] = q
    qt = q.astype(F32).T
    qt_out[...] = qt.astype(BF16)
    for h in range(HEADS):
        fq_out[h] = features(qt[head_rows(h)])


def local_kernel(own, q_ref, k_ref, v_ref, out):
    rows = q_ref.shape[0]
    half = half_index(own)
    quarter = q_ref[...] * jnp.asarray(FEAT ** (-0.5), BF16)
    for g in range(HALF):
        qs = quarter * head_mask(half * HALF + g)
        for start in range(0, rows, STEP):
            stop = start + STEP
            t = dot(qs[start:stop], k_ref[0:stop], NT)
            w = (0.5 * t + 1.0) * t + 1.0
            at = lax.broadcasted_iota(jnp.int32, (STEP, stop), 0) + start
            w = jnp.where(at >= lax.broadcasted_iota(jnp.int32, (STEP, stop), 1), w, 0.0)
            out[start:stop, head_lanes(g)] = dot(w.astype(BF16), v_ref[0:stop, head_lanes(g)], NN)


def norm_kernel(own, local, fq, prefix, grad, gain, *refs):
    *others, out, gs_out, state_out, gain_out, pre, summed_ref = refs
    half = half_index(own)
    doubled(prefix, pre)
    for other in others:
        for g in range(HALF):
            out[:, lanes_of(1 - half, g)] = other[:, head_lanes(g)]
    for g in range(HALF):
        place = head_lanes(g)
        summed_ref[:, place] = local[:, place] + dot(fq[half * HALF + g], pre[g], TN)
    for g in range(HALF):
        place = head_lanes(g)
        summed = summed_ref[:, place]
        scale = lax.rsqrt(jnp.mean(summed * summed, axis=-1, keepdims=True) + EPSILON)
        normal = summed * scale
        weight = gain[pl.ds(half * HALF + g, 1)]
        out[:, place if own else lanes_of(half, g)] = (normal * weight).astype(BF16)
        incoming = grad[:, lanes_of(half, g)].astype(F32)
        gain_out[g : g + 1] = jnp.sum(incoming * normal, axis=0, keepdims=True)
        upstream = incoming * weight
        gs = scale * (upstream - normal * jnp.mean(normal * upstream, axis=-1, keepdims=True))
        gs = gs.astype(BF16)
        gs_out[:, place] = gs
        state_out[g] = dot(fq[half * HALF + g], gs, NN).astype(BF16)


def first_back_kernel(q_ref, k_ref, qt_ref, kt_ref, v_ref, gs_ref, tokens, gv_out, gq_out, gk_out, out, sem):
    copy = pltpu.make_async_copy(tokens, out, sem)
    copy.start()
    back_kernel(True, 0, q_ref, k_ref, qt_ref, kt_ref, v_ref, gs_ref, gv_out, gq_out, gk_out)
    copy.wait()


def back_kernel(own, part, q_ref, k_ref, qt_ref, kt_ref, v_ref, gs_ref, gv_out, gq_out, gk_out):
    rows = q_ref.shape[0]
    half = half_index(own)
    quarter = q_ref[...] * jnp.asarray(FEAT ** (-0.5), BF16)
    for i in range(PART):
        g = part * PART + i
        ks = k_ref[...] * head_mask(half * HALF + g)
        qt = qt_ref[rows_of(half, g)]
        kt = kt_ref[rows_of(half, g)]
        for start in range(0, rows, STEP):
            stop = start + STEP
            shape = (STEP, rows - start)
            t = dot(ks[start:stop], quarter[start:], NT)
            seen = lax.broadcasted_iota(jnp.int32, shape, 1) >= lax.broadcasted_iota(jnp.int32, shape, 0)
            w = jnp.where(seen, (0.5 * t + 1.0) * t + 1.0, 0.0).astype(BF16)
            gs = gs_ref[start:, head_lanes(g)]
            gv_out[start:stop, head_lanes(i)] = dot(w, gs, NN)
            gw = dot(v_ref[start:stop, head_lanes(g)], gs, NT)
            s = jnp.where(seen, gw * (FEAT ** (-0.5) + FEAT ** (-0.5) * t), 0.0).astype(BF16)
            part_q = dot(kt[:, start:stop], s, NN)
            if start == 0:
                gq_out[head_rows(i)] = part_q
            else:
                gq_out[head_rows(i), start:] += part_q
            gk_out[head_rows(i), start:stop] = dot(qt[:, start:], s, NT)


def query_grad_kernel(
    query, rim, qt_ref, gs_a, gs_b, pre_a, pre_b, a0, a1, b0, b1, taps_q, g_out, sums, wide, pre, turned_grad
):
    for own, gs, prefix, locals_ in ((True, gs_a, pre_a, (a0, a1)), (False, gs_b, pre_b, (b0, b1))):
        half = half_index(own)
        doubled(prefix, pre)
        for g in range(HALF):
            x = qt_ref[rows_of(half, g)].astype(F32)
            turned_grad[rows_of(half, g)] = locals_[g // PART][head_rows(g % PART)] + feature_grad(
                x, pre[g], gs[:, head_lanes(g)]
            )
    grad = turned_grad[...].T
    g_out[...] = grad
    fill(wide, rim[:, 0:LANES], query[...])
    for o, row in enumerate(tap_sums(grad, wide, taps_q.shape[0])):
        sums[o : o + 1] = row


def later_half(half, value, rim, kt, fk, v, state, locals_v, locals_k, gv_out, gk_put, sums_put, wide, post, taps):
    doubled(state, post)
    for g in range(HALF):
        local = locals_v[g // PART][:, head_lanes(g % PART)]
        gv_out[:, head_lanes(g)] = local + dot(fk[g], post[g], TN)
    for g in range(HALF):
        local = locals_k[g // PART][head_rows(g % PART)]
        x = kt[rows_of(half, g)].astype(F32)
        gk_put(g, local + feature_grad(x, post[g], v[:, head_lanes(g)]))
    for g in range(HALF):
        fill(wide, rim[:, lanes_of(half, g, 2 * LANES)], value[:, lanes_of(half, g)])
        for o, row in enumerate(tap_sums(gv_out[:, head_lanes(g)], wide, taps)):
            sums_put(o, g, row)


def first_later_kernel(value, rim, kt, fk, v, state, v0, v1, k0, k1, gv_out, gk_out, sums, wide, post):
    def gk_put(g, x):
        gk_out[head_rows(g)] = x

    def sums_put(o, g, row):
        sums[o : o + 1, head_lanes(g)] = row

    later_half(
        half_index(False), value, rim, kt, fk, v, state, (v0, v1), (k0, k1), gv_out, gk_put, sums_put, wide, post,
        sums.shape[0],
    )


def second_later_kernel(
    key, value, rim, kt, fk, v, state, v0, v1, k0, k1, gv_b, gk_b, sums_b, gq, sums_q, gain_a, gain_b,
    gv_out, gk_out, head_out, sums, wide, post, turned_grad,
):
    taps = sums_q.shape[0]
    rows = key.shape[0]
    half_a, half_b = half_index(True), half_index(False)

    def gk_put(g, x):
        turned_grad[rows_of(half_a, g)] = x

    def sums_put(o, g, row):
        sums[o : o + 1, lanes_of(half_a, g, 2 * LANES)] = row

    turned_grad[pl.ds(pl.multiple_of(half_b * HALF * FEAT, HALF * FEAT), HALF * FEAT)] = gk_b[...]
    later_half(
        half_a, value, rim, kt, fk, v, state, (v0, v1), (k0, k1), gv_out, gk_put, sums_put, wide, post, taps
    )
    grad = turned_grad[...].T
    gk_out[...] = grad
    fill(wide, rim[:, LANES : 2 * LANES], key[...])
    for o, row in enumerate(tap_sums(grad, wide, taps)):
        sums[o : o + 1, LANES : 2 * LANES] = row
    sums[0:taps, 0:LANES] = sums_q[...]
    sums[taps : taps + 1, 0 : 2 * LANES] = jnp.zeros((1, 2 * LANES), F32)
    head_out[:, 0:LANES] = gq[0:8]
    head_out[:, LANES : 2 * LANES] = grad[0:8]
    for g in range(HALF):
        sums[0:taps, lanes_of(half_b, g, 2 * LANES)] = sums_b[:, head_lanes(g)]
        for half, gain, gv in ((half_a, gain_a, gv_out), (half_b, gain_b, gv_b)):
            sums[taps : taps + 1, lanes_of(half, g, 2 * LANES)] = gain[g : g + 1]
            head_out[:, lanes_of(half, g, 2 * LANES)] = gv[0:8, head_lanes(g)]


def signal_kernel(
    gq, gk, gv_a, gv_b, follow, taps_q, taps_k, taps_v, q_out, k_out, v_out, wide, q_part, k_part, v_part, sems
):
    rows = gq.shape[0]
    count = taps_q.shape[0]
    copies = []

    def one(grad, place, start, stop, after, taps, part, lanes):
        last = stop == rows
        body = stop - start - (RIM if last else 0)
        total = taps[0:1] * grad[start + count - 1 : start + count - 1 + body, place]
        for o in range(1, count):
            total = total + taps[o : o + 1] * grad[start + count - 1 - o : start + count - 1 - o + body, place]
        part[start : start + body, lanes] = total.astype(BF16)
        if last:
            wide[0:RIM] = grad[rows - RIM :, place]
            wide[RIM : RIM + 8] = after
            total = taps[0:1] * wide[count - 1 : count - 1 + RIM]
            for o in range(1, count):
                total = total + taps[o : o + 1] * wide[count - 1 - o : count - 1 - o + RIM]
            part[rows - RIM :, lanes] = total.astype(BF16)

    def move(part, out):
        copies.append(pltpu.make_async_copy(part, out, sems.at[len(copies)]))
        copies[-1].start()

    for start in reversed(range(0, rows, STEP)):
        stop = start + STEP
        for own, gv in ((True, gv_a), (False, gv_b)):
            half = half_index(own)
            for g in range(HALF):
                lanes = lanes_of(half, g)
                after = follow[:, lanes_of(half, g, 2 * LANES)]
                one(gv, head_lanes(g), start, stop, after, taps_v[:, lanes], v_part, lanes)
        move(v_part.at[start:stop], v_out.at[start:stop])
    for grad, place, taps, part, out in (
        (gq, slice(0, LANES), taps_q, q_part, q_out), (gk, slice(LANES, 2 * LANES), taps_k, k_part, k_out)
    ):
        one(grad, slice(0, LANES), 0, rows, follow[:, place], taps[...], part, slice(0, LANES))
        move(part, out)
    for copy in copies:
        copy.wait()


def finish_kernel(factor, *refs):
    *terms, q_out, k_out, v_out, gain_out = refs
    taps = q_out.shape[0]
    total = terms[0][...]
    for term in terms[1:]:
        total = total + term[...]
    total = total * factor
    q_out[...] = total[0:taps, 0:LANES]
    k_out[...] = total[0:taps, LANES : 2 * LANES]
    v_out[...] = total[0:taps, 2 * LANES :]
    gain_out[...] = total[taps : taps + 1, 2 * LANES :]


def far(x):
    return pltpu.with_memory_space_constraint(x, pltpu.HBM)


def held(*xs):
    return [pltpu.with_memory_space_constraint(x, pltpu.VMEM) for x in xs]


def call(kernel, outs, scratch, args, flops, limit=16, loose=(), **specs):
    size = lambda a: a.size * a.dtype.itemsize
    moved = sum(size(a) for a in args) + sum(size(o) for o in outs)
    return pl.pallas_call(
        kernel,
        out_shape=[o if i in loose else pltpu.VMEM(o.shape, o.dtype) for i, o in enumerate(outs)],
        scratch_shapes=scratch,
        compiler_params=pltpu.CompilerParams(vmem_limit_bytes=limit * 2**20),
        cost_estimate=pl.CostEstimate(flops=flops, bytes_accessed=moved, transcendentals=0),
        **specs,
    )(*args)


def exchange(x, distance):
    count = lax.axis_size("seq")
    return lax.ppermute(x, "seq", [(i, i ^ distance) for i in range(count)])


def tie(x, *others):
    return lax.optimization_barrier((x, *others))[0]


def on_side(bit, reverse):
    set_ = lax.rem(lax.div(lax.axis_index("seq"), bit), 2)
    return set_ == (0 if reverse else 1)


def chosen(flag, x):
    return jnp.where(flag, x, jnp.zeros_like(x))


def pair_kernel(keep, near, part, their):
    upper = lax.rem(lax.div(lax.axis_index("seq"), 2), 2)

    def half(which):
        place = pl.ds(which * PART, PART)
        return keep[place].astype(F32) + near[place].astype(F32)

    part[...] = half(upper)
    their[...] = half(1 - upper).astype(BF16)


def step_kernel(part, *refs):
    *gots, send = refs
    total = part[...]
    for got in gots:
        total = total + got[...].astype(F32)
    send[...] = total.astype(BF16)


def part_kernel(reverse, part, got_y, *rest):
    *gots, own, give = rest
    before = jnp.zeros(part.shape, F32)
    for i, got in enumerate(gots):
        before = before + chosen(on_side(4 << i, reverse), got[...].astype(F32))
    own[...] = before + chosen(on_side(2, reverse), got_y[...].astype(F32))
    give[...] = (before + chosen(jnp.logical_not(on_side(2, reverse)), part[...])).astype(BF16)


def merge_kernel(reverse, own_part, other_part, keep, near, own, give):
    upper = lax.rem(lax.div(lax.axis_index("seq"), 2), 2)
    side = on_side(1, reverse)
    for part, which in ((own_part, upper), (other_part, 1 - upper)):
        place = pl.ds(which * PART, PART)
        before = part[...].astype(F32)
        own[place] = (before + chosen(side, near[place].astype(F32))).astype(BF16)
        give[place] = (before + chosen(jnp.logical_not(side), keep[place].astype(F32))).astype(BF16)


def beyond(keep, send, reverse, works, last):
    count = lax.axis_size("seq")
    works = list(works)
    st = jax.ShapeDtypeStruct
    whole, part_shape = keep.shape, (PART, *keep.shape[1:])
    wide, narrow = st(part_shape, F32), st(part_shape, BF16)
    cost = 4 * keep.size

    def under(x):
        return tie(x, *works.pop(0)()) if works else x

    near = exchange(send, 1)
    part, their = call(pair_kernel, [wide, narrow], [], (keep, near), cost)
    got_y = exchange(their, 2)
    gots = []
    bit = 4
    while bit < count:
        send = call(step_kernel, [narrow], [], (part, got_y, *gots), cost)[0]
        gots.append(exchange(under(send), bit))
        bit *= 2
    own_part, give_part = call(
        functools.partial(part_kernel, reverse), [wide, narrow], [], (part, got_y, *gots), cost
    )
    other_part = exchange(under(give_part), 2)
    own, give = call(
        functools.partial(merge_kernel, reverse), [st(whole, BF16)] * 2, [], (own_part, other_part, keep, near), cost
    )
    other = exchange(under(give), 1)
    return own, tie(other, last(own))


def shards(query_in, key_in, value_in, conv_query, conv_key, conv_value, norm_gain, grad_out):
    rows = query_in.shape[0]
    taps = conv_query.shape[0]
    count = lax.axis_size("seq")
    total_rows = rows * count
    st = jax.ShapeDtypeStruct
    half_width = HALF * DIM
    half_state, half_wide = st((HALF, ROWS, DIM), BF16), st((rows, half_width), F32)
    half_narrow, half_features = st((rows, half_width), BF16), st((HALF, ROWS, rows), BF16)
    flat, turned_flat = st((rows, LANES), F32), st((LANES, rows), BF16)
    state_scratch = pltpu.VMEM((HALF, ROWS, DIM), BF16)
    wide = pltpu.VMEM((RIM + rows, DIM), F32)
    gain = norm_gain.reshape(HEADS, DIM)
    state_flops = HEADS * ROWS * DIM * rows
    square_flops = 2 * HALF * rows * rows * DIM

    apart = pl.BlockSpec(memory_space=pltpu.HBM)
    near = pl.BlockSpec(memory_space=pltpu.VMEM)
    ends = call(
        end_kernel,
        [st((RIM, ALL), BF16)],
        [pltpu.SemaphoreType.DMA((3,))],
        (far(query_in), far(key_in), far(value_in)),
        rows,
        in_specs=[apart] * 3,
    )[0]
    rim = lax.ppermute(ends, "seq", [(i, i + 1) for i in range(count - 1)])

    rest = rows - CUT
    half_rest = [st((rest, half_width), BF16), st((HALF, ROWS, rest), BF16), st((HALF, ROWS, DIM), F32)]
    k_rest, kt_rest, *rests = call(
        bulk_kernel,
        [st((rest, LANES), BF16), st((LANES, rest), BF16), *half_rest, *half_rest],
        [wide],
        (key_in, value_in, conv_key, conv_value),
        2 * state_flops,
    )
    k, kt, v_b, fk_b, state_b = call(
        first_key_kernel,
        [st((rows, LANES), BF16), turned_flat, half_narrow, half_features, half_state],
        [wide],
        (key_in, value_in, rim, conv_key, conv_value, *held(k_rest, kt_rest, *rests[:3])),
        state_flops,
    )
    v_a, fk_a, state_a = call(
        second_key_kernel,
        [half_narrow, half_features, half_state],
        [wide],
        (*held(kt), value_in, rim, conv_value, *held(*rests[3:])),
        state_flops,
    )
    made = {}

    def local_work(own, v):
        def work():
            if "q" not in made:
                made["q"] = call(
                    query_kernel,
                    [st((rows, LANES), BF16), turned_flat, st((HEADS, ROWS, rows), BF16)],
                    [wide],
                    (query_in, rim, conv_query),
                    state_flops,
                )
            made[own] = call(
                functools.partial(local_kernel, own),
                [half_wide],
                [],
                held(made["q"][0], k, v),
                2 * square_flops,
            )[0]
            return (made[own],)

        return work

    def norm(own, prefix, *others):
        return call(
            functools.partial(norm_kernel, own),
            [half_narrow if own else st((rows, WIDE), BF16), half_narrow, half_state, st((HALF, DIM), F32)],
            [state_scratch, pltpu.VMEM((rows, half_width), F32)],
            (*held(made[own], made["q"][2]), prefix, grad_out, gain, *held(*others)),
            2 * state_flops,
        )

    def first_norm(prefix):
        made["norm"] = norm(True, prefix)
        return made["norm"][0]

    pre_a, pre_b = beyond(
        state_a, state_b, False, [local_work(True, v_a), local_work(False, v_b)], first_norm
    )
    q, qt, fq = made["q"]
    out_a, gs_a, state_a, gain_a = made["norm"]
    tokens, gs_b, state_b, gain_b = norm(False, pre_b, out_a)
    back = []

    def first_back():
        *parts, made["out"] = call(
            first_back_kernel,
            [st((rows, PART * DIM), F32), st((PART * FEAT, rows), F32), st((PART * FEAT, rows), F32),
             st((rows, WIDE), BF16)],
            [pltpu.SemaphoreType.DMA],
            held(q, k, qt, kt, v_a, gs_a, tokens),
            2 * square_flops,
            loose=(3,),
            out_specs=[near] * 3 + [apart],
        )
        back.append(parts)
        return (parts[0],)

    def back_work(own, part, v, gs):
        def work():
            back.append(
                call(
                    functools.partial(back_kernel, own, part),
                    [st((rows, PART * DIM), F32), st((PART * FEAT, rows), F32), st((PART * FEAT, rows), F32)],
                    [],
                    held(q, k, qt, kt, v, gs),
                    2 * square_flops,
                )
            )
            return (back[-1][0],)

        return work

    def last_work():
        work = back_work(False, 1, v_b, gs_b)()[0]
        made["gq"] = call(
            query_grad_kernel,
            [flat, st((taps, LANES), F32)],
            [wide, state_scratch, pltpu.VMEM((LANES, rows), F32)],
            (query_in, rim, *held(qt, gs_a, gs_b), pre_a, pre_b, *held(*[b[1] for b in back]), conv_query),
            state_flops,
        )
        return (work, made["gq"][0])

    def first_later(state):
        made["later"] = call(
            first_later_kernel,
            [half_wide, st((HALF * FEAT, rows), F32), st((taps, half_width), F32)],
            [wide, state_scratch],
            (value_in, rim, *held(kt, fk_b, v_b), state, *held(back[2][0], back[3][0], back[2][2], back[3][2])),
            2 * state_flops,
        )
        return made["later"][0]

    works = [first_back, back_work(True, 1, v_a, gs_a), back_work(False, 0, v_b, gs_b), last_work]
    _, post_a = beyond(state_b, state_a, True, works, first_later)
    gv_b, gk_b, sums_b = made["later"]
    gq, sums_q = made["gq"]
    gv_a, gk, heads, sums = call(
        second_later_kernel,
        [half_wide, flat, st((8, ALL), F32), st((taps + 1, ALL), F32)],
        [wide, state_scratch, pltpu.VMEM((LANES, rows), F32)],
        (key_in, value_in, rim, *held(kt, fk_a, v_a), post_a,
         *held(back[0][0], back[1][0], back[0][2], back[1][2], gv_b, gk_b, sums_b, gq, sums_q, gain_a, gain_b)),
        2 * state_flops,
    )
    follow = lax.ppermute(heads, "seq", [(i + 1, i) for i in range(count - 1)])
    bit = 4
    while bit < count:
        group = (bit, 2 * bit, 3 * bit) if 2 * bit < count else (bit,)
        for got in [exchange(sums, distance) for distance in group]:
            sums = sums + got
        bit *= len(group) + 1
    flat_narrow = st((rows, LANES), BF16)
    grad_query, grad_key, grad_value = call(
        signal_kernel,
        [flat_narrow, flat_narrow, st((rows, WIDE), BF16)],
        [pltpu.VMEM((RIM + 8, DIM), F32), pltpu.VMEM((rows, LANES), BF16), pltpu.VMEM((rows, LANES), BF16),
         pltpu.VMEM((rows, WIDE), BF16), pltpu.SemaphoreType.DMA((rows // STEP + 2,))],
        (*held(gq, gk, gv_a, gv_b), follow, conv_query, conv_key, conv_value),
        2 * state_flops,
        loose=(0, 1, 2),
        out_specs=[apart] * 3,
    )
    taps_query, taps_key, taps_value, taps_gain = call(
        functools.partial(finish_kernel, total_rows ** (-0.5)),
        [st((taps, LANES), F32), st((taps, LANES), F32), st((taps, WIDE), F32), st((1, WIDE), F32)],
        [],
        (tie(sums, grad_value), *[exchange(sums, distance) for distance in (3, 2, 1)]),
        rows,
        loose=(0, 1, 2, 3),
    )
    return (
        made["out"],
        grad_query,
        grad_key,
        grad_value,
        taps_query,
        taps_key,
        taps_value,
        taps_gain.reshape(WIDE),
    )


def solution(mesh):
    rows = P(("groups", "seq"), None)
    return jax.shard_map(
        shards,
        mesh=mesh,
        in_specs=(rows, rows, rows, P(), P(), P(), P(), rows),
        out_specs=(rows, rows, rows, rows, P("groups", None), P("groups", None), P("groups", None), P("groups")),
        check_vma=False,
    )
```

```python
import functools

import jax
import jax.numpy as jnp
from jax import lax
from jax.experimental import pallas as pl
from jax.experimental.pallas import tpu as pltpu
from jax.sharding import PartitionSpec as P

HEADS = 8
HALF = HEADS // 2
PART = HEADS // 4
FEAT = 16
DIM = 128
EPSILON = 1e-06
LANES = HEADS * FEAT
WIDE = HEADS * DIM
ALL = 2 * LANES + WIDE
ROWS = 160
LIN = 128
TAIL = 144
RIM = 16
STEP = 128
CUT = 128
F32 = jnp.float32
BF16 = jnp.bfloat16

NN = (((1,), (0,)), ((), ()))
NT = (((1,), (1,)), ((), ()))
TN = (((0,), (0,)), ((), ()))


def dot(a, b, dims):
    return lax.dot_general(a, b, dims, preferred_element_type=F32)


def head_rows(h):
    return slice(h * FEAT, (h + 1) * FEAT)


def head_lanes(h):
    return slice(h * DIM, (h + 1) * DIM)


def conv(wide_ref, taps, rows):
    margin = taps.shape[0] - 1
    total = taps[0:1] * wide_ref[RIM - margin : RIM - margin + rows]
    for o in range(1, margin + 1):
        total = total + taps[o : o + 1] * wide_ref[RIM - margin + o : RIM - margin + o + rows]
    return total


def tap_sums(grad, wide_ref, taps):
    rows = grad.shape[0]
    start = RIM - (taps - 1)
    return [
        jnp.sum(grad * wide_ref[start + o : start + o + rows], axis=0, keepdims=True)
        for o in range(taps)
    ]


def turned(x, shift):
    return x if shift % FEAT == 0 else pltpu.roll(x, shift % FEAT, 0)


def features(x):
    half = (0.5 / FEAT) ** 0.5
    pieces = [(x * turned(x, FEAT - d) * half).astype(BF16) for d in range(8)]
    pieces.append((x * FEAT ** (-0.25)).astype(BF16))
    rows = lax.broadcasted_iota(jnp.int32, (8, x.shape[1]), 0)
    one = jnp.where(rows == 0, 1.0, 0.0).astype(F32)
    pieces.append(jnp.concatenate([x[:8] * x[8:] * half, one], axis=0).astype(BF16))
    return jnp.concatenate(pieces, axis=0)


def feature_grad(x, state, vector):
    g = dot(state, vector, NT)
    crossed = 2.0 * g[0:FEAT] * x
    for d in range(1, 8):
        part = g[d * FEAT : (d + 1) * FEAT]
        crossed = crossed + part * turned(x, FEAT - d) + turned(part * x, d)
    part = g[TAIL : TAIL + 8]
    crossed = crossed + jnp.concatenate([part * x[8:], part * x[:8]], axis=0)
    return g[LIN:TAIL] * FEAT ** (-0.25) + crossed * (0.5 / FEAT) ** 0.5


def half_index(own):
    core = lax.rem(lax.axis_index("seq"), 2)
    return core if own else 1 - core


def rows_of(half, g):
    return pl.ds(pl.multiple_of((half * HALF + g) * FEAT, FEAT), FEAT)


def lanes_of(half, g, start=0):
    return pl.ds(pl.multiple_of(start + (half * HALF + g) * DIM, DIM), DIM)


def doubled(state_ref, out_ref):
    rows = lax.broadcasted_iota(jnp.int32, (ROWS, DIM), 0)
    pair = ((rows >= FEAT) & (rows < LIN)) | ((rows >= TAIL) & (rows < TAIL + 8))
    weight = jnp.where(pair, 2.0, 1.0).astype(F32)
    for g in range(HALF):
        out_ref[g] = (state_ref[g].astype(F32) * weight).astype(BF16)


def head_mask(h):
    lanes = lax.broadcasted_iota(jnp.int32, (1, LANES), 1)
    return jnp.where(lanes // FEAT == h, 1.0, 0.0).astype(F32).astype(BF16)


def fill(wide, rim, rest):
    wide[0:RIM] = rim.astype(F32)
    wide[RIM : RIM + rest.shape[0]] = rest.astype(F32)


def end_kernel(query, key, value, out, sems):
    start = query.shape[0] - RIM
    copies = [
        pltpu.make_async_copy(ref.at[pl.ds(start, RIM)], out.at[:, pl.ds(lane, ref.shape[1])], sems.at[i])
        for i, (ref, lane) in enumerate(((query, 0), (key, LANES), (value, 2 * LANES)))
    ]
    for copy in copies:
        copy.start()
    for copy in copies:
        copy.wait()


def bulk_kernel(
    key, value, taps_k, taps_v, k_out, kt_out, v_b, f_b, state_b, v_a, f_a, state_a, wide
):
    rows = key.shape[0] - CUT
    fill(wide, key[CUT - RIM : CUT], key[CUT:])
    k = conv(wide, taps_k[...], rows).astype(BF16)
    k_out[...] = k
    kt_out[...] = k.astype(F32).T.astype(BF16)
    for own, v_out, f_out, state_out in ((False, v_b, f_b, state_b), (True, v_a, f_a, state_a)):
        half = half_index(own)
        for g in range(HALF):
            f_out[g] = features(kt_out[rows_of(half, g)].astype(F32))
        for g in range(HALF):
            lanes = lanes_of(half, g)
            fill(wide, value[CUT - RIM : CUT, lanes], value[CUT:, lanes])
            v_out[:, head_lanes(g)] = conv(wide, taps_v[:, lanes], rows).astype(BF16)
        for g in range(HALF):
            state_out[g] = dot(f_out[g], v_out[:, head_lanes(g)], NN)


def value_states(half, kt, value, rim, taps_v, v_rest, f_rest, state_rest, v_out, f_out, state_out, wide):
    for g in range(HALF):
        f_out[g, :, 0:CUT] = features(kt[rows_of(half, g), 0:CUT].astype(F32))
        f_out[g, :, CUT:] = f_rest[g]
    v_out[CUT:] = v_rest[...]
    for g in range(HALF):
        lanes = lanes_of(half, g)
        fill(wide, rim[:, lanes_of(half, g, 2 * LANES)], value[0:CUT, lanes])
        v_out[0:CUT, head_lanes(g)] = conv(wide, taps_v[:, lanes], CUT).astype(BF16)
    for g in range(HALF):
        first = dot(f_out[g, :, 0:CUT], v_out[0:CUT, head_lanes(g)], NN)
        state_out[g] = (state_rest[g] + first).astype(BF16)


def first_key_kernel(
    key, value, rim, taps_k, taps_v, k_rest, kt_rest, v_rest, f_rest, state_rest,
    k_out, kt_out, v_out, f_out, state_out, wide,
):
    fill(wide, rim[:, LANES : 2 * LANES], key[0:CUT])
    k = conv(wide, taps_k[...], CUT).astype(BF16)
    k_out[0:CUT] = k
    k_out[CUT:] = k_rest[...]
    kt_out[:, 0:CUT] = k.astype(F32).T.astype(BF16)
    kt_out[:, CUT:] = kt_rest[...]
    value_states(
        half_index(False), kt_out, value, rim, taps_v, v_rest, f_rest, state_rest, v_out, f_out, state_out, wide
    )


def second_key_kernel(kt, value, rim, taps_v, v_rest, f_rest, state_rest, v_out, f_out, state_out, wide):
    value_states(
        half_index(True), kt, value, rim, taps_v, v_rest, f_rest, state_rest, v_out, f_out, state_out, wide
    )


def query_kernel(query, rim, taps_q, q_out, qt_out, fq_out, wide):
    rows = query.shape[0]
    fill(wide, rim[:, 0:LANES], query[...])
    q = conv(wide, taps_q[...], rows).astype(BF16)
    q_out[...] = q
    qt = q.astype(F32).T
    qt_out[...] = qt.astype(BF16)
    for h in range(HEADS):
        fq_out[h] = features(qt[head_rows(h)])


def local_kernel(own, q_ref, k_ref, v_ref, out):
    rows = q_ref.shape[0]
    half = half_index(own)
    quarter = q_ref[...] * jnp.asarray(FEAT ** (-0.5), BF16)
    for g in range(HALF):
        qs = quarter * head_mask(half * HALF + g)
        for start in range(0, rows, STEP):
            stop = start + STEP
            t = dot(qs[start:stop], k_ref[0:stop], NT)
            w = (0.5 * t + 1.0) * t + 1.0
            at = lax.broadcasted_iota(jnp.int32, (STEP, stop), 0) + start
            w = jnp.where(at >= lax.broadcasted_iota(jnp.int32, (STEP, stop), 1), w, 0.0)
            out[start:stop, head_lanes(g)] = dot(w.astype(BF16), v_ref[0:stop, head_lanes(g)], NN)


def norm_kernel(own, local, fq, prefix, grad, gain, *refs):
    *others, out, gs_out, state_out, gain_out, pre, summed_ref = refs
    half = half_index(own)
    doubled(prefix, pre)
    for other in others:
        for g in range(HALF):
            out[:, lanes_of(1 - half, g)] = other[:, head_lanes(g)]
    for g in range(HALF):
        place = head_lanes(g)
        summed_ref[:, place] = local[:, place] + dot(fq[half * HALF + g], pre[g], TN)
    for g in range(HALF):
        place = head_lanes(g)
        summed = summed_ref[:, place]
        scale = lax.rsqrt(jnp.mean(summed * summed, axis=-1, keepdims=True) + EPSILON)
        normal = summed * scale
        weight = gain[pl.ds(half * HALF + g, 1)]
        out[:, place if own else lanes_of(half, g)] = (normal * weight).astype(BF16)
        incoming = grad[:, lanes_of(half, g)].astype(F32)
        gain_out[g : g + 1] = jnp.sum(incoming * normal, axis=0, keepdims=True)
        upstream = incoming * weight
        gs = scale * (upstream - normal * jnp.mean(normal * upstream, axis=-1, keepdims=True))
        gs = gs.astype(BF16)
        gs_out[:, place] = gs
        state_out[g] = dot(fq[half * HALF + g], gs, NN).astype(BF16)


def first_back_kernel(q_ref, k_ref, qt_ref, kt_ref, v_ref, gs_ref, tokens, gv_out, gq_out, gk_out, out, sem):
    copy = pltpu.make_async_copy(tokens, out, sem)
    copy.start()
    back_kernel(True, 0, q_ref, k_ref, qt_ref, kt_ref, v_ref, gs_ref, gv_out, gq_out, gk_out)
    copy.wait()


def back_kernel(own, part, q_ref, k_ref, qt_ref, kt_ref, v_ref, gs_ref, gv_out, gq_out, gk_out):
    rows = q_ref.shape[0]
    half = half_index(own)
    quarter = q_ref[...] * jnp.asarray(FEAT ** (-0.5), BF16)
    for i in range(PART):
        g = part * PART + i
        ks = k_ref[...] * head_mask(half * HALF + g)
        qt = qt_ref[rows_of(half, g)]
        kt = kt_ref[rows_of(half, g)]
        for start in range(0, rows, STEP):
            stop = start + STEP
            shape = (STEP, rows - start)
            t = dot(ks[start:stop], quarter[start:], NT)
            seen = lax.broadcasted_iota(jnp.int32, shape, 1) >= lax.broadcasted_iota(jnp.int32, shape, 0)
            w = jnp.where(seen, (0.5 * t + 1.0) * t + 1.0, 0.0).astype(BF16)
            gs = gs_ref[start:, head_lanes(g)]
            gv_out[start:stop, head_lanes(i)] = dot(w, gs, NN)
            gw = dot(v_ref[start:stop, head_lanes(g)], gs, NT)
            s = jnp.where(seen, gw * (FEAT ** (-0.5) + FEAT ** (-0.5) * t), 0.0).astype(BF16)
            part_q = dot(kt[:, start:stop], s, NN)
            if start == 0:
                gq_out[head_rows(i)] = part_q
            else:
                gq_out[head_rows(i), start:] += part_q
            gk_out[head_rows(i), start:stop] = dot(qt[:, start:], s, NT)


def query_grad_kernel(
    query, rim, qt_ref, gs_a, gs_b, pre_a, pre_b, a0, a1, b0, b1, taps_q, g_out, sums, wide, pre, turned_grad
):
    for own, gs, prefix, locals_ in ((True, gs_a, pre_a, (a0, a1)), (False, gs_b, pre_b, (b0, b1))):
        half = half_index(own)
        doubled(prefix, pre)
        for g in range(HALF):
            x = qt_ref[rows_of(half, g)].astype(F32)
            turned_grad[rows_of(half, g)] = locals_[g // PART][head_rows(g % PART)] + feature_grad(
                x, pre[g], gs[:, head_lanes(g)]
            )
    grad = turned_grad[...].T
    g_out[...] = grad
    fill(wide, rim[:, 0:LANES], query[...])
    for o, row in enumerate(tap_sums(grad, wide, taps_q.shape[0])):
        sums[o : o + 1] = row


def later_half(half, value, rim, kt, fk, v, state, locals_v, locals_k, gv_out, gk_put, sums_put, wide, post, taps):
    doubled(state, post)
    for g in range(HALF):
        local = locals_v[g // PART][:, head_lanes(g % PART)]
        gv_out[:, head_lanes(g)] = local + dot(fk[g], post[g], TN)
    for g in range(HALF):
        local = locals_k[g // PART][head_rows(g % PART)]
        x = kt[rows_of(half, g)].astype(F32)
        gk_put(g, local + feature_grad(x, post[g], v[:, head_lanes(g)]))
    for g in range(HALF):
        fill(wide, rim[:, lanes_of(half, g, 2 * LANES)], value[:, lanes_of(half, g)])
        for o, row in enumerate(tap_sums(gv_out[:, head_lanes(g)], wide, taps)):
            sums_put(o, g, row)


def first_later_kernel(value, rim, kt, fk, v, state, v0, v1, k0, k1, gv_out, gk_out, sums, wide, post):
    def gk_put(g, x):
        gk_out[head_rows(g)] = x

    def sums_put(o, g, row):
        sums[o : o + 1, head_lanes(g)] = row

    later_half(
        half_index(False), value, rim, kt, fk, v, state, (v0, v1), (k0, k1), gv_out, gk_put, sums_put, wide, post,
        sums.shape[0],
    )


def second_later_kernel(
    key, value, rim, kt, fk, v, state, v0, v1, k0, k1, gv_b, gk_b, sums_b, gq, sums_q, gain_a, gain_b,
    gv_out, gk_out, head_out, sums, wide, post, turned_grad,
):
    taps = sums_q.shape[0]
    rows = key.shape[0]
    half_a, half_b = half_index(True), half_index(False)

    def gk_put(g, x):
        turned_grad[rows_of(half_a, g)] = x

    def sums_put(o, g, row):
        sums[o : o + 1, lanes_of(half_a, g, 2 * LANES)] = row

    turned_grad[pl.ds(pl.multiple_of(half_b * HALF * FEAT, HALF * FEAT), HALF * FEAT)] = gk_b[...]
    later_half(
        half_a, value, rim, kt, fk, v, state, (v0, v1), (k0, k1), gv_out, gk_put, sums_put, wide, post, taps
    )
    grad = turned_grad[...].T
    gk_out[...] = grad
    fill(wide, rim[:, LANES : 2 * LANES], key[...])
    for o, row in enumerate(tap_sums(grad, wide, taps)):
        sums[o : o + 1, LANES : 2 * LANES] = row
    sums[0:taps, 0:LANES] = sums_q[...]
    sums[taps : taps + 1, 0 : 2 * LANES] = jnp.zeros((1, 2 * LANES), F32)
    head_out[:, 0:LANES] = gq[0:8]
    head_out[:, LANES : 2 * LANES] = grad[0:8]
    for g in range(HALF):
        sums[0:taps, lanes_of(half_b, g, 2 * LANES)] = sums_b[:, head_lanes(g)]
        for half, gain, gv in ((half_a, gain_a, gv_out), (half_b, gain_b, gv_b)):
            sums[taps : taps + 1, lanes_of(half, g, 2 * LANES)] = gain[g : g + 1]
            head_out[:, lanes_of(half, g, 2 * LANES)] = gv[0:8, head_lanes(g)]


def signal_kernel(
    gq, gk, gv_a, gv_b, follow, taps_q, taps_k, taps_v, q_out, k_out, v_out, wide, q_part, k_part, v_part, sems
):
    rows = gq.shape[0]
    count = taps_q.shape[0]
    copies = []

    def one(grad, place, start, stop, after, taps, part, lanes):
        last = stop == rows
        body = stop - start - (RIM if last else 0)
        total = taps[0:1] * grad[start + count - 1 : start + count - 1 + body, place]
        for o in range(1, count):
            total = total + taps[o : o + 1] * grad[start + count - 1 - o : start + count - 1 - o + body, place]
        part[start : start + body, lanes] = total.astype(BF16)
        if last:
            wide[0:RIM] = grad[rows - RIM :, place]
            wide[RIM : RIM + 8] = after
            total = taps[0:1] * wide[count - 1 : count - 1 + RIM]
            for o in range(1, count):
                total = total + taps[o : o + 1] * wide[count - 1 - o : count - 1 - o + RIM]
            part[rows - RIM :, lanes] = total.astype(BF16)

    def move(part, out):
        copies.append(pltpu.make_async_copy(part, out, sems.at[len(copies)]))
        copies[-1].start()

    for start in reversed(range(0, rows, STEP)):
        stop = start + STEP
        for own, gv in ((True, gv_a), (False, gv_b)):
            half = half_index(own)
            for g in range(HALF):
                lanes = lanes_of(half, g)
                after = follow[:, lanes_of(half, g, 2 * LANES)]
                one(gv, head_lanes(g), start, stop, after, taps_v[:, lanes], v_part, lanes)
        move(v_part.at[start:stop], v_out.at[start:stop])
    for grad, place, taps, part, out in (
        (gq, slice(0, LANES), taps_q, q_part, q_out), (gk, slice(LANES, 2 * LANES), taps_k, k_part, k_out)
    ):
        one(grad, slice(0, LANES), 0, rows, follow[:, place], taps[...], part, slice(0, LANES))
        move(part, out)
    for copy in copies:
        copy.wait()


def finish_kernel(factor, *refs):
    *terms, q_out, k_out, v_out, gain_out = refs
    taps = q_out.shape[0]
    total = terms[0][...]
    for term in terms[1:]:
        total = total + term[...]
    total = total * factor
    q_out[...] = total[0:taps, 0:LANES]
    k_out[...] = total[0:taps, LANES : 2 * LANES]
    v_out[...] = total[0:taps, 2 * LANES :]
    gain_out[...] = total[taps : taps + 1, 2 * LANES :]


def far(x):
    return pltpu.with_memory_space_constraint(x, pltpu.HBM)


def held(*xs):
    return [pltpu.with_memory_space_constraint(x, pltpu.VMEM) for x in xs]


def call(kernel, outs, scratch, args, flops, limit=16, loose=(), **specs):
    size = lambda a: a.size * a.dtype.itemsize
    moved = sum(size(a) for a in args) + sum(size(o) for o in outs)
    return pl.pallas_call(
        kernel,
        out_shape=[o if i in loose else pltpu.VMEM(o.shape, o.dtype) for i, o in enumerate(outs)],
        scratch_shapes=scratch,
        compiler_params=pltpu.CompilerParams(vmem_limit_bytes=limit * 2**20),
        cost_estimate=pl.CostEstimate(flops=flops, bytes_accessed=moved, transcendentals=0),
        **specs,
    )(*args)


def exchange(x, distance):
    count = lax.axis_size("seq")
    return lax.ppermute(x, "seq", [(i, i ^ distance) for i in range(count)])


def tie(x, *others):
    return lax.optimization_barrier((x, *others))[0]


def on_side(bit, reverse):
    set_ = lax.rem(lax.div(lax.axis_index("seq"), bit), 2)
    return set_ == (0 if reverse else 1)


def chosen(flag, x):
    return jnp.where(flag, x, jnp.zeros_like(x))


def pair_kernel(keep, near, part, their):
    upper = lax.rem(lax.div(lax.axis_index("seq"), 2), 2)

    def half(which):
        place = pl.ds(which * PART, PART)
        return keep[place].astype(F32) + near[place].astype(F32)

    part[...] = half(upper)
    their[...] = half(1 - upper).astype(BF16)


def step_kernel(part, *refs):
    *gots, send = refs
    total = part[...]
    for got in gots:
        total = total + got[...].astype(F32)
    send[...] = total.astype(BF16)


def part_kernel(reverse, part, got_y, *rest):
    *gots, own, give = rest
    before = jnp.zeros(part.shape, F32)
    for i, got in enumerate(gots):
        before = before + chosen(on_side(4 << i, reverse), got[...].astype(F32))
    own[...] = before + chosen(on_side(2, reverse), got_y[...].astype(F32))
    give[...] = (before + chosen(jnp.logical_not(on_side(2, reverse)), part[...])).astype(BF16)


def merge_kernel(reverse, own_part, other_part, keep, near, own, give):
    upper = lax.rem(lax.div(lax.axis_index("seq"), 2), 2)
    side = on_side(1, reverse)
    for part, which in ((own_part, upper), (other_part, 1 - upper)):
        place = pl.ds(which * PART, PART)
        before = part[...].astype(F32)
        own[place] = (before + chosen(side, near[place].astype(F32))).astype(BF16)
        give[place] = (before + chosen(jnp.logical_not(side), keep[place].astype(F32))).astype(BF16)


def beyond(keep, send, reverse, works, last):
    count = lax.axis_size("seq")
    works = list(works)
    st = jax.ShapeDtypeStruct
    whole, part_shape = keep.shape, (PART, *keep.shape[1:])
    wide, narrow = st(part_shape, F32), st(part_shape, BF16)
    cost = 4 * keep.size

    def under(x):
        return tie(x, *works.pop(0)()) if works else x

    near = exchange(send, 1)
    part, their = call(pair_kernel, [wide, narrow], [], (keep, near), cost)
    got_y = exchange(their, 2)
    gots = []
    bit = 4
    while bit < count:
        send = call(step_kernel, [narrow], [], (part, got_y, *gots), cost)[0]
        gots.append(exchange(under(send), bit))
        bit *= 2
    own_part, give_part = call(
        functools.partial(part_kernel, reverse), [wide, narrow], [], (part, got_y, *gots), cost
    )
    other_part = exchange(under(give_part), 2)
    own, give = call(
        functools.partial(merge_kernel, reverse), [st(whole, BF16)] * 2, [], (own_part, other_part, keep, near), cost
    )
    other = exchange(under(give), 1)
    return own, tie(other, last(own))


def shards(query_in, key_in, value_in, conv_query, conv_key, conv_value, norm_gain, grad_out):
    rows = query_in.shape[0]
    taps = conv_query.shape[0]
    count = lax.axis_size("seq")
    total_rows = rows * count
    st = jax.ShapeDtypeStruct
    half_width = HALF * DIM
    half_state, half_wide = st((HALF, ROWS, DIM), BF16), st((rows, half_width), F32)
    half_narrow, half_features = st((rows, half_width), BF16), st((HALF, ROWS, rows), BF16)
    flat, turned_flat = st((rows, LANES), F32), st((LANES, rows), BF16)
    state_scratch = pltpu.VMEM((HALF, ROWS, DIM), BF16)
    wide = pltpu.VMEM((RIM + rows, DIM), F32)
    gain = norm_gain.reshape(HEADS, DIM)
    state_flops = HEADS * ROWS * DIM * rows
    square_flops = 2 * HALF * rows * rows * DIM

    apart = pl.BlockSpec(memory_space=pltpu.HBM)
    near = pl.BlockSpec(memory_space=pltpu.VMEM)
    ends = call(
        end_kernel,
        [st((RIM, ALL), BF16)],
        [pltpu.SemaphoreType.DMA((3,))],
        (far(query_in), far(key_in), far(value_in)),
        rows,
        in_specs=[apart] * 3,
    )[0]
    rim = lax.ppermute(ends, "seq", [(i, i + 1) for i in range(count - 1)])

    rest = rows - CUT
    half_rest = [st((rest, half_width), BF16), st((HALF, ROWS, rest), BF16), st((HALF, ROWS, DIM), F32)]
    k_rest, kt_rest, *rests = call(
        bulk_kernel,
        [st((rest, LANES), BF16), st((LANES, rest), BF16), *half_rest, *half_rest],
        [wide],
        (key_in, value_in, conv_key, conv_value),
        2 * state_flops,
    )
    k, kt, v_b, fk_b, state_b = call(
        first_key_kernel,
        [st((rows, LANES), BF16), turned_flat, half_narrow, half_features, half_state],
        [wide],
        (key_in, value_in, rim, conv_key, conv_value, *held(k_rest, kt_rest, *rests[:3])),
        state_flops,
    )
    v_a, fk_a, state_a = call(
        second_key_kernel,
        [half_narrow, half_features, half_state],
        [wide],
        (*held(kt), value_in, rim, conv_value, *held(*rests[3:])),
        state_flops,
    )
    made = {}

    def local_work(own, v):
        def work():
            if "q" not in made:
                made["q"] = call(
                    query_kernel,
                    [st((rows, LANES), BF16), turned_flat, st((HEADS, ROWS, rows), BF16)],
                    [wide],
                    (query_in, rim, conv_query),
                    state_flops,
                )
            made[own] = call(
                functools.partial(local_kernel, own),
                [half_wide],
                [],
                held(made["q"][0], k, v),
                2 * square_flops,
            )[0]
            return (made[own],)

        return work

    def norm(own, prefix, *others):
        return call(
            functools.partial(norm_kernel, own),
            [half_narrow if own else st((rows, WIDE), BF16), half_narrow, half_state, st((HALF, DIM), F32)],
            [state_scratch, pltpu.VMEM((rows, half_width), F32)],
            (*held(made[own], made["q"][2]), prefix, grad_out, gain, *held(*others)),
            2 * state_flops,
        )

    def first_norm(prefix):
        made["norm"] = norm(True, prefix)
        return made["norm"][0]

    pre_a, pre_b = beyond(
        state_a, state_b, False, [local_work(True, v_a), local_work(False, v_b)], first_norm
    )
    q, qt, fq = made["q"]
    out_a, gs_a, state_a, gain_a = made["norm"]
    tokens, gs_b, state_b, gain_b = norm(False, pre_b, out_a)
    back = []

    def first_back():
        *parts, made["out"] = call(
            first_back_kernel,
            [st((rows, PART * DIM), F32), st((PART * FEAT, rows), F32), st((PART * FEAT, rows), F32),
             st((rows, WIDE), BF16)],
            [pltpu.SemaphoreType.DMA],
            held(q, k, qt, kt, v_a, gs_a, tokens),
            2 * square_flops,
            loose=(3,),
            out_specs=[near] * 3 + [apart],
        )
        back.append(parts)
        return (parts[0],)

    def back_work(own, part, v, gs):
        def work():
            back.append(
                call(
                    functools.partial(back_kernel, own, part),
                    [st((rows, PART * DIM), F32), st((PART * FEAT, rows), F32), st((PART * FEAT, rows), F32)],
                    [],
                    held(q, k, qt, kt, v, gs),
                    2 * square_flops,
                )
            )
            return (back[-1][0],)

        return work

    def last_work():
        work = back_work(False, 1, v_b, gs_b)()[0]
        made["gq"] = call(
            query_grad_kernel,
            [flat, st((taps, LANES), F32)],
            [wide, state_scratch, pltpu.VMEM((LANES, rows), F32)],
            (query_in, rim, *held(qt, gs_a, gs_b), pre_a, pre_b, *held(*[b[1] for b in back]), conv_query),
            state_flops,
        )
        return (work, made["gq"][0])

    def first_later(state):
        made["later"] = call(
            first_later_kernel,
            [half_wide, st((HALF * FEAT, rows), F32), st((taps, half_width), F32)],
            [wide, state_scratch],
            (value_in, rim, *held(kt, fk_b, v_b), state, *held(back[2][0], back[3][0], back[2][2], back[3][2])),
            2 * state_flops,
        )
        return made["later"][0]

    works = [first_back, back_work(True, 1, v_a, gs_a), back_work(False, 0, v_b, gs_b), last_work]
    _, post_a = beyond(state_b, state_a, True, works, first_later)
    gv_b, gk_b, sums_b = made["later"]
    gq, sums_q = made["gq"]
    gv_a, gk, heads, sums = call(
        second_later_kernel,
        [half_wide, flat, st((8, ALL), F32), st((taps + 1, ALL), F32)],
        [wide, state_scratch, pltpu.VMEM((LANES, rows), F32)],
        (key_in, value_in, rim, *held(kt, fk_a, v_a), post_a,
         *held(back[0][0], back[1][0], back[0][2], back[1][2], gv_b, gk_b, sums_b, gq, sums_q, gain_a, gain_b)),
        2 * state_flops,
    )
    follow = lax.ppermute(heads, "seq", [(i + 1, i) for i in range(count - 1)])
    bit = 4
    while bit < count:
        group = (bit, 3 * bit, 2 * bit) if 2 * bit < count else (bit,)
        for got in [exchange(sums, distance) for distance in group]:
            sums = sums + got
        bit *= len(group) + 1
    flat_narrow = st((rows, LANES), BF16)
    grad_query, grad_key, grad_value = call(
        signal_kernel,
        [flat_narrow, flat_narrow, st((rows, WIDE), BF16)],
        [pltpu.VMEM((RIM + 8, DIM), F32), pltpu.VMEM((rows, LANES), BF16), pltpu.VMEM((rows, LANES), BF16),
         pltpu.VMEM((rows, WIDE), BF16), pltpu.SemaphoreType.DMA((rows // STEP + 2,))],
        (*held(gq, gk, gv_a, gv_b), follow, conv_query, conv_key, conv_value),
        2 * state_flops,
        loose=(0, 1, 2),
        out_specs=[apart] * 3,
    )
    taps_query, taps_key, taps_value, taps_gain = call(
        functools.partial(finish_kernel, total_rows ** (-0.5)),
        [st((taps, LANES), F32), st((taps, LANES), F32), st((taps, WIDE), F32), st((1, WIDE), F32)],
        [],
        (tie(sums, grad_value), *[exchange(sums, distance) for distance in (3, 2, 1)]),
        rows,
        loose=(0, 1, 2, 3),
    )
    return (
        made["out"],
        grad_query,
        grad_key,
        grad_value,
        taps_query,
        taps_key,
        taps_value,
        taps_gain.reshape(WIDE),
    )


def solution(mesh):
    rows = P(("groups", "seq"), None)
    return jax.shard_map(
        shards,
        mesh=mesh,
        in_specs=(rows, rows, rows, P(), P(), P(), P(), rows),
        out_specs=(rows, rows, rows, rows, P("groups", None), P("groups", None), P("groups", None), P("groups")),
        check_vma=False,
    )
```

```python
import functools

import jax
import jax.numpy as jnp
from jax import lax
from jax.experimental import pallas as pl
from jax.experimental.pallas import tpu as pltpu
from jax.sharding import PartitionSpec as P

HEADS = 8
HALF = HEADS // 2
PART = HEADS // 4
FEAT = 16
DIM = 128
EPSILON = 1e-06
LANES = HEADS * FEAT
WIDE = HEADS * DIM
ALL = 2 * LANES + WIDE
ROWS = 160
LIN = 128
TAIL = 144
RIM = 16
STEP = 128
CUT = 128
F32 = jnp.float32
BF16 = jnp.bfloat16

NN = (((1,), (0,)), ((), ()))
NT = (((1,), (1,)), ((), ()))
TN = (((0,), (0,)), ((), ()))


def dot(a, b, dims):
    return lax.dot_general(a, b, dims, preferred_element_type=F32)


def head_rows(h):
    return slice(h * FEAT, (h + 1) * FEAT)


def head_lanes(h):
    return slice(h * DIM, (h + 1) * DIM)


def conv(wide_ref, taps, rows):
    margin = taps.shape[0] - 1
    total = taps[0:1] * wide_ref[RIM - margin : RIM - margin + rows]
    for o in range(1, margin + 1):
        total = total + taps[o : o + 1] * wide_ref[RIM - margin + o : RIM - margin + o + rows]
    return total


def tap_sums(grad, wide_ref, taps):
    rows = grad.shape[0]
    start = RIM - (taps - 1)
    return [
        jnp.sum(grad * wide_ref[start + o : start + o + rows], axis=0, keepdims=True)
        for o in range(taps)
    ]


def turned(x, shift):
    return x if shift % FEAT == 0 else pltpu.roll(x, shift % FEAT, 0)


def features(x):
    half = (0.5 / FEAT) ** 0.5
    pieces = [(x * turned(x, FEAT - d) * half).astype(BF16) for d in range(8)]
    pieces.append((x * FEAT ** (-0.25)).astype(BF16))
    rows = lax.broadcasted_iota(jnp.int32, (8, x.shape[1]), 0)
    one = jnp.where(rows == 0, 1.0, 0.0).astype(F32)
    pieces.append(jnp.concatenate([x[:8] * x[8:] * half, one], axis=0).astype(BF16))
    return jnp.concatenate(pieces, axis=0)


def feature_grad(x, state, vector):
    g = dot(state, vector, NT)
    crossed = 2.0 * g[0:FEAT] * x
    for d in range(1, 8):
        part = g[d * FEAT : (d + 1) * FEAT]
        crossed = crossed + part * turned(x, FEAT - d) + turned(part * x, d)
    part = g[TAIL : TAIL + 8]
    crossed = crossed + jnp.concatenate([part * x[8:], part * x[:8]], axis=0)
    return g[LIN:TAIL] * FEAT ** (-0.25) + crossed * (0.5 / FEAT) ** 0.5


def half_index(own):
    core = lax.rem(lax.axis_index("seq"), 2)
    return core if own else 1 - core


def rows_of(half, g):
    return pl.ds(pl.multiple_of((half * HALF + g) * FEAT, FEAT), FEAT)


def lanes_of(half, g, start=0):
    return pl.ds(pl.multiple_of(start + (half * HALF + g) * DIM, DIM), DIM)


def doubled(state_ref, out_ref):
    rows = lax.broadcasted_iota(jnp.int32, (ROWS, DIM), 0)
    pair = ((rows >= FEAT) & (rows < LIN)) | ((rows >= TAIL) & (rows < TAIL + 8))
    weight = jnp.where(pair, 2.0, 1.0).astype(F32)
    for g in range(HALF):
        out_ref[g] = (state_ref[g].astype(F32) * weight).astype(BF16)


def head_mask(h):
    lanes = lax.broadcasted_iota(jnp.int32, (1, LANES), 1)
    return jnp.where(lanes // FEAT == h, 1.0, 0.0).astype(F32).astype(BF16)


def fill(wide, rim, rest):
    wide[RIM - rim.shape[0] : RIM] = rim.astype(F32)
    wide[RIM : RIM + rest.shape[0]] = rest.astype(F32)


def end_kernel(query, key, value, out, ends, sems):
    start = query.shape[0] - RIM
    copies = [
        pltpu.make_async_copy(ref.at[pl.ds(start, RIM)], ends.at[:, pl.ds(lane, ref.shape[1])], sems.at[i])
        for i, (ref, lane) in enumerate(((query, 0), (key, LANES), (value, 2 * LANES)))
    ]
    for copy in copies:
        copy.start()
    for copy in copies:
        copy.wait()
    out[...] = ends[...].astype(F32)[RIM - out.shape[0] :].astype(BF16)


def bulk_kernel(
    key, value, taps_k, taps_v, k_out, kt_out, v_b, f_b, state_b, v_a, f_a, state_a, wide
):
    rows = key.shape[0] - CUT
    fill(wide, key[CUT - RIM : CUT], key[CUT:])
    k = conv(wide, taps_k[...], rows).astype(BF16)
    k_out[...] = k
    kt_out[...] = k.astype(F32).T.astype(BF16)
    for own, v_out, f_out, state_out in ((False, v_b, f_b, state_b), (True, v_a, f_a, state_a)):
        half = half_index(own)
        for g in range(HALF):
            f_out[g] = features(kt_out[rows_of(half, g)].astype(F32))
        for g in range(HALF):
            lanes = lanes_of(half, g)
            fill(wide, value[CUT - RIM : CUT, lanes], value[CUT:, lanes])
            v_out[:, head_lanes(g)] = conv(wide, taps_v[:, lanes], rows).astype(BF16)
        for g in range(HALF):
            state_out[g] = dot(f_out[g], v_out[:, head_lanes(g)], NN)


def value_states(half, kt, value, rim, taps_v, v_rest, f_rest, state_rest, v_out, f_out, state_out, wide):
    for g in range(HALF):
        f_out[g, :, 0:CUT] = features(kt[rows_of(half, g), 0:CUT].astype(F32))
        f_out[g, :, CUT:] = f_rest[g]
    v_out[CUT:] = v_rest[...]
    for g in range(HALF):
        lanes = lanes_of(half, g)
        fill(wide, rim[:, lanes_of(half, g, 2 * LANES)], value[0:CUT, lanes])
        v_out[0:CUT, head_lanes(g)] = conv(wide, taps_v[:, lanes], CUT).astype(BF16)
    for g in range(HALF):
        first = dot(f_out[g, :, 0:CUT], v_out[0:CUT, head_lanes(g)], NN)
        state_out[g] = (state_rest[g] + first).astype(BF16)


def first_key_kernel(
    key, value, rim, taps_k, taps_v, k_rest, kt_rest, v_rest, f_rest, state_rest,
    k_out, kt_out, v_out, f_out, state_out, wide,
):
    fill(wide, rim[:, LANES : 2 * LANES], key[0:CUT])
    k = conv(wide, taps_k[...], CUT).astype(BF16)
    k_out[0:CUT] = k
    k_out[CUT:] = k_rest[...]
    kt_out[:, 0:CUT] = k.astype(F32).T.astype(BF16)
    kt_out[:, CUT:] = kt_rest[...]
    value_states(
        half_index(False), kt_out, value, rim, taps_v, v_rest, f_rest, state_rest, v_out, f_out, state_out, wide
    )


def second_key_kernel(kt, value, rim, taps_v, v_rest, f_rest, state_rest, v_out, f_out, state_out, wide):
    value_states(
        half_index(True), kt, value, rim, taps_v, v_rest, f_rest, state_rest, v_out, f_out, state_out, wide
    )


def query_kernel(query, rim, taps_q, q_out, qt_out, fq_out, wide):
    rows = query.shape[0]
    fill(wide, rim[:, 0:LANES], query[...])
    q = conv(wide, taps_q[...], rows).astype(BF16)
    q_out[...] = q
    qt = q.astype(F32).T
    qt_out[...] = qt.astype(BF16)
    for h in range(HEADS):
        fq_out[h] = features(qt[head_rows(h)])


def local_kernel(own, q_ref, k_ref, v_ref, out):
    rows = q_ref.shape[0]
    half = half_index(own)
    quarter = q_ref[...] * jnp.asarray(FEAT ** (-0.5), BF16)
    for g in range(HALF):
        qs = quarter * head_mask(half * HALF + g)
        for start in range(0, rows, STEP):
            stop = start + STEP
            t = dot(qs[start:stop], k_ref[0:stop], NT)
            w = (0.5 * t + 1.0) * t + 1.0
            at = lax.broadcasted_iota(jnp.int32, (STEP, stop), 0) + start
            w = jnp.where(at >= lax.broadcasted_iota(jnp.int32, (STEP, stop), 1), w, 0.0)
            out[start:stop, head_lanes(g)] = dot(w.astype(BF16), v_ref[0:stop, head_lanes(g)], NN)


def norm_kernel(own, local, fq, prefix, grad, gain, *refs):
    *others, out, gs_out, state_out, gain_out, pre, summed_ref = refs
    half = half_index(own)
    doubled(prefix, pre)
    for other in others:
        for g in range(HALF):
            out[:, lanes_of(1 - half, g)] = other[:, head_lanes(g)]
    for g in range(HALF):
        place = head_lanes(g)
        summed_ref[:, place] = local[:, place] + dot(fq[half * HALF + g], pre[g], TN)
    for g in range(HALF):
        place = head_lanes(g)
        summed = summed_ref[:, place]
        scale = lax.rsqrt(jnp.mean(summed * summed, axis=-1, keepdims=True) + EPSILON)
        normal = summed * scale
        weight = gain[pl.ds(half * HALF + g, 1)]
        out[:, place if own else lanes_of(half, g)] = (normal * weight).astype(BF16)
        incoming = grad[:, lanes_of(half, g)].astype(F32)
        gain_out[g : g + 1] = jnp.sum(incoming * normal, axis=0, keepdims=True)
        upstream = incoming * weight
        gs = scale * (upstream - normal * jnp.mean(normal * upstream, axis=-1, keepdims=True))
        gs = gs.astype(BF16)
        gs_out[:, place] = gs
        state_out[g] = dot(fq[half * HALF + g], gs, NN).astype(BF16)


def first_back_kernel(q_ref, k_ref, qt_ref, kt_ref, v_ref, gs_ref, tokens, gv_out, gq_out, gk_out, out, sem):
    copy = pltpu.make_async_copy(tokens, out, sem)
    copy.start()
    back_kernel(True, 0, q_ref, k_ref, qt_ref, kt_ref, v_ref, gs_ref, gv_out, gq_out, gk_out)
    copy.wait()


def back_kernel(own, part, q_ref, k_ref, qt_ref, kt_ref, v_ref, gs_ref, gv_out, gq_out, gk_out):
    rows = q_ref.shape[0]
    half = half_index(own)
    quarter = q_ref[...] * jnp.asarray(FEAT ** (-0.5), BF16)
    for i in range(PART):
        g = part * PART + i
        ks = k_ref[...] * head_mask(half * HALF + g)
        qt = qt_ref[rows_of(half, g)]
        kt = kt_ref[rows_of(half, g)]
        for start in range(0, rows, STEP):
            stop = start + STEP
            shape = (STEP, rows - start)
            t = dot(ks[start:stop], quarter[start:], NT)
            seen = lax.broadcasted_iota(jnp.int32, shape, 1) >= lax.broadcasted_iota(jnp.int32, shape, 0)
            w = jnp.where(seen, (0.5 * t + 1.0) * t + 1.0, 0.0).astype(BF16)
            gs = gs_ref[start:, head_lanes(g)]
            gv_out[start:stop, head_lanes(i)] = dot(w, gs, NN)
            gw = dot(v_ref[start:stop, head_lanes(g)], gs, NT)
            s = jnp.where(seen, gw * (FEAT ** (-0.5) + FEAT ** (-0.5) * t), 0.0).astype(BF16)
            part_q = dot(kt[:, start:stop], s, NN)
            if start == 0:
                gq_out[head_rows(i)] = part_q
            else:
                gq_out[head_rows(i), start:] += part_q
            gk_out[head_rows(i), start:stop] = dot(qt[:, start:], s, NT)


def query_grad_kernel(
    query, rim, qt_ref, gs_a, gs_b, pre_a, pre_b, a0, a1, b0, b1, taps_q, g_out, sums, wide, pre, turned_grad
):
    for own, gs, prefix, locals_ in ((True, gs_a, pre_a, (a0, a1)), (False, gs_b, pre_b, (b0, b1))):
        half = half_index(own)
        doubled(prefix, pre)
        for g in range(HALF):
            x = qt_ref[rows_of(half, g)].astype(F32)
            turned_grad[rows_of(half, g)] = locals_[g // PART][head_rows(g % PART)] + feature_grad(
                x, pre[g], gs[:, head_lanes(g)]
            )
    grad = turned_grad[...].T
    g_out[...] = grad
    fill(wide, rim[:, 0:LANES], query[...])
    for o, row in enumerate(tap_sums(grad, wide, taps_q.shape[0])):
        sums[o : o + 1] = row


def later_half(half, value, rim, kt, fk, v, state, locals_v, locals_k, gv_out, gk_put, sums_put, wide, post, taps):
    doubled(state, post)
    for g in range(HALF):
        local = locals_v[g // PART][:, head_lanes(g % PART)]
        gv_out[:, head_lanes(g)] = local + dot(fk[g], post[g], TN)
    for g in range(HALF):
        local = locals_k[g // PART][head_rows(g % PART)]
        x = kt[rows_of(half, g)].astype(F32)
        gk_put(g, local + feature_grad(x, post[g], v[:, head_lanes(g)]))
    for g in range(HALF):
        fill(wide, rim[:, lanes_of(half, g, 2 * LANES)], value[:, lanes_of(half, g)])
        for o, row in enumerate(tap_sums(gv_out[:, head_lanes(g)], wide, taps)):
            sums_put(o, g, row)


def first_later_kernel(value, rim, kt, fk, v, state, v0, v1, k0, k1, gv_out, gk_out, sums, wide, post):
    def gk_put(g, x):
        gk_out[head_rows(g)] = x

    def sums_put(o, g, row):
        sums[o : o + 1, head_lanes(g)] = row

    later_half(
        half_index(False), value, rim, kt, fk, v, state, (v0, v1), (k0, k1), gv_out, gk_put, sums_put, wide, post,
        sums.shape[0],
    )


def second_later_kernel(
    key, value, rim, kt, fk, v, state, v0, v1, k0, k1, gv_b, gk_b, sums_b, gq, sums_q, gain_a, gain_b,
    gv_out, gk_out, head_out, sums, wide, post, turned_grad,
):
    taps = sums_q.shape[0]
    rows = key.shape[0]
    half_a, half_b = half_index(True), half_index(False)

    def gk_put(g, x):
        turned_grad[rows_of(half_a, g)] = x

    def sums_put(o, g, row):
        sums[o : o + 1, lanes_of(half_a, g, 2 * LANES)] = row

    turned_grad[pl.ds(pl.multiple_of(half_b * HALF * FEAT, HALF * FEAT), HALF * FEAT)] = gk_b[...]
    later_half(
        half_a, value, rim, kt, fk, v, state, (v0, v1), (k0, k1), gv_out, gk_put, sums_put, wide, post, taps
    )
    grad = turned_grad[...].T
    gk_out[...] = grad
    fill(wide, rim[:, LANES : 2 * LANES], key[...])
    for o, row in enumerate(tap_sums(grad, wide, taps)):
        sums[o : o + 1, LANES : 2 * LANES] = row
    sums[0:taps, 0:LANES] = sums_q[...]
    sums[taps : taps + 1, 0 : 2 * LANES] = jnp.zeros((1, 2 * LANES), F32)
    head_out[:, 0:LANES] = gq[0 : taps - 1]
    head_out[:, LANES : 2 * LANES] = grad[0 : taps - 1]
    for g in range(HALF):
        sums[0:taps, lanes_of(half_b, g, 2 * LANES)] = sums_b[:, head_lanes(g)]
        for half, gain, gv in ((half_a, gain_a, gv_out), (half_b, gain_b, gv_b)):
            sums[taps : taps + 1, lanes_of(half, g, 2 * LANES)] = gain[g : g + 1]
            head_out[:, lanes_of(half, g, 2 * LANES)] = gv[0 : taps - 1, head_lanes(g)]


def signal_kernel(
    gq, gk, gv_a, gv_b, follow, taps_q, taps_k, taps_v, q_out, k_out, v_out, wide, q_part, k_part, v_part, sems
):
    rows = gq.shape[0]
    count = taps_q.shape[0]
    copies = []

    def one(grad, place, start, stop, after, taps, part, lanes):
        last = stop == rows
        body = stop - start - (RIM if last else 0)
        total = taps[0:1] * grad[start + count - 1 : start + count - 1 + body, place]
        for o in range(1, count):
            total = total + taps[o : o + 1] * grad[start + count - 1 - o : start + count - 1 - o + body, place]
        part[start : start + body, lanes] = total.astype(BF16)
        if last:
            wide[0:RIM] = grad[rows - RIM :, place]
            wide[RIM : RIM + count - 1] = after
            total = taps[0:1] * wide[count - 1 : count - 1 + RIM]
            for o in range(1, count):
                total = total + taps[o : o + 1] * wide[count - 1 - o : count - 1 - o + RIM]
            part[rows - RIM :, lanes] = total.astype(BF16)

    def move(part, out):
        copies.append(pltpu.make_async_copy(part, out, sems.at[len(copies)]))
        copies[-1].start()

    for start in reversed(range(0, rows, STEP)):
        stop = start + STEP
        for own, gv in ((True, gv_a), (False, gv_b)):
            half = half_index(own)
            for g in range(HALF):
                lanes = lanes_of(half, g)
                after = follow[:, lanes_of(half, g, 2 * LANES)]
                one(gv, head_lanes(g), start, stop, after, taps_v[:, lanes], v_part, lanes)
        move(v_part.at[start:stop], v_out.at[start:stop])
    for grad, place, taps, part, out in (
        (gq, slice(0, LANES), taps_q, q_part, q_out), (gk, slice(LANES, 2 * LANES), taps_k, k_part, k_out)
    ):
        one(grad, slice(0, LANES), 0, rows, follow[:, place], taps[...], part, slice(0, LANES))
        move(part, out)
    for copy in copies:
        copy.wait()


def finish_kernel(factor, *refs):
    *terms, q_out, k_out, v_out, gain_out = refs
    taps = q_out.shape[0]
    total = terms[0][...]
    for term in terms[1:]:
        total = total + term[...]
    total = total * factor
    q_out[...] = total[0:taps, 0:LANES]
    k_out[...] = total[0:taps, LANES : 2 * LANES]
    v_out[...] = total[0:taps, 2 * LANES :]
    gain_out[...] = total[taps : taps + 1, 2 * LANES :]


def far(x):
    return pltpu.with_memory_space_constraint(x, pltpu.HBM)


def held(*xs):
    return [pltpu.with_memory_space_constraint(x, pltpu.VMEM) for x in xs]


def call(kernel, outs, scratch, args, flops, limit=16, loose=(), **specs):
    size = lambda a: a.size * a.dtype.itemsize
    moved = sum(size(a) for a in args) + sum(size(o) for o in outs)
    return pl.pallas_call(
        kernel,
        out_shape=[o if i in loose else pltpu.VMEM(o.shape, o.dtype) for i, o in enumerate(outs)],
        scratch_shapes=scratch,
        compiler_params=pltpu.CompilerParams(vmem_limit_bytes=limit * 2**20),
        cost_estimate=pl.CostEstimate(flops=flops, bytes_accessed=moved, transcendentals=0),
        **specs,
    )(*args)


def exchange(x, distance):
    count = lax.axis_size("seq")
    return lax.ppermute(x, "seq", [(i, i ^ distance) for i in range(count)])


def tie(x, *others):
    return lax.optimization_barrier((x, *others))[0]


def on_side(bit, reverse):
    set_ = lax.rem(lax.div(lax.axis_index("seq"), bit), 2)
    return set_ == (0 if reverse else 1)


def chosen(flag, x):
    return jnp.where(flag, x, jnp.zeros_like(x))


def pair_kernel(keep, near, part, their):
    upper = lax.rem(lax.div(lax.axis_index("seq"), 2), 2)

    def half(which):
        place = pl.ds(which * PART, PART)
        return keep[place].astype(F32) + near[place].astype(F32)

    part[...] = half(upper)
    their[...] = half(1 - upper).astype(BF16)


def step_kernel(part, *refs):
    *gots, send = refs
    total = part[...]
    for got in gots:
        total = total + got[...].astype(F32)
    send[...] = total.astype(BF16)


def part_kernel(reverse, part, got_y, *rest):
    *gots, own, give = rest
    before = jnp.zeros(part.shape, F32)
    for i, got in enumerate(gots):
        before = before + chosen(on_side(4 << i, reverse), got[...].astype(F32))
    own[...] = before + chosen(on_side(2, reverse), got_y[...].astype(F32))
    give[...] = (before + chosen(jnp.logical_not(on_side(2, reverse)), part[...])).astype(BF16)


def merge_kernel(reverse, own_part, other_part, keep, near, own, give):
    upper = lax.rem(lax.div(lax.axis_index("seq"), 2), 2)
    side = on_side(1, reverse)
    for part, which in ((own_part, upper), (other_part, 1 - upper)):
        place = pl.ds(which * PART, PART)
        before = part[...].astype(F32)
        own[place] = (before + chosen(side, near[place].astype(F32))).astype(BF16)
        give[place] = (before + chosen(jnp.logical_not(side), keep[place].astype(F32))).astype(BF16)


def beyond(keep, send, reverse, works, last):
    count = lax.axis_size("seq")
    works = list(works)
    st = jax.ShapeDtypeStruct
    whole, part_shape = keep.shape, (PART, *keep.shape[1:])
    wide, narrow = st(part_shape, F32), st(part_shape, BF16)
    cost = 4 * keep.size

    def under(x):
        return tie(x, *works.pop(0)()) if works else x

    near = exchange(send, 1)
    part, their = call(pair_kernel, [wide, narrow], [], (keep, near), cost)
    got_y = exchange(their, 2)
    gots = []
    bit = 4
    while bit < count:
        send = call(step_kernel, [narrow], [], (part, got_y, *gots), cost)[0]
        gots.append(exchange(under(send), bit))
        bit *= 2
    own_part, give_part = call(
        functools.partial(part_kernel, reverse), [wide, narrow], [], (part, got_y, *gots), cost
    )
    other_part = exchange(under(give_part), 2)
    own, give = call(
        functools.partial(merge_kernel, reverse), [st(whole, BF16)] * 2, [], (own_part, other_part, keep, near), cost
    )
    other = exchange(under(give), 1)
    return own, tie(other, last(own))


def shards(query_in, key_in, value_in, conv_query, conv_key, conv_value, norm_gain, grad_out):
    rows = query_in.shape[0]
    taps = conv_query.shape[0]
    count = lax.axis_size("seq")
    total_rows = rows * count
    st = jax.ShapeDtypeStruct
    half_width = HALF * DIM
    half_state, half_wide = st((HALF, ROWS, DIM), BF16), st((rows, half_width), F32)
    half_narrow, half_features = st((rows, half_width), BF16), st((HALF, ROWS, rows), BF16)
    flat, turned_flat = st((rows, LANES), F32), st((LANES, rows), BF16)
    state_scratch = pltpu.VMEM((HALF, ROWS, DIM), BF16)
    wide = pltpu.VMEM((RIM + rows, DIM), F32)
    gain = norm_gain.reshape(HEADS, DIM)
    state_flops = HEADS * ROWS * DIM * rows
    square_flops = 2 * HALF * rows * rows * DIM

    apart = pl.BlockSpec(memory_space=pltpu.HBM)
    near = pl.BlockSpec(memory_space=pltpu.VMEM)
    ends = call(
        end_kernel,
        [st((taps - 1, ALL), BF16)],
        [pltpu.VMEM((RIM, ALL), BF16), pltpu.SemaphoreType.DMA((3,))],
        (far(query_in), far(key_in), far(value_in)),
        rows,
        in_specs=[apart] * 3,
    )[0]
    rim = lax.ppermute(ends, "seq", [(i, i + 1) for i in range(count - 1)])

    rest = rows - CUT
    half_rest = [st((rest, half_width), BF16), st((HALF, ROWS, rest), BF16), st((HALF, ROWS, DIM), F32)]
    k_rest, kt_rest, *rests = call(
        bulk_kernel,
        [st((rest, LANES), BF16), st((LANES, rest), BF16), *half_rest, *half_rest],
        [wide],
        (key_in, value_in, conv_key, conv_value),
        2 * state_flops,
    )
    k, kt, v_b, fk_b, state_b = call(
        first_key_kernel,
        [st((rows, LANES), BF16), turned_flat, half_narrow, half_features, half_state],
        [wide],
        (key_in, value_in, rim, conv_key, conv_value, *held(k_rest, kt_rest, *rests[:3])),
        state_flops,
    )
    v_a, fk_a, state_a = call(
        second_key_kernel,
        [half_narrow, half_features, half_state],
        [wide],
        (*held(kt), value_in, rim, conv_value, *held(*rests[3:])),
        state_flops,
    )
    made = {}

    def local_work(own, v):
        def work():
            if "q" not in made:
                made["q"] = call(
                    query_kernel,
                    [st((rows, LANES), BF16), turned_flat, st((HEADS, ROWS, rows), BF16)],
                    [wide],
                    (query_in, rim, conv_query),
                    state_flops,
                )
            made[own] = call(
                functools.partial(local_kernel, own),
                [half_wide],
                [],
                held(made["q"][0], k, v),
                2 * square_flops,
            )[0]
            return (made[own],)

        return work

    def norm(own, prefix, *others):
        return call(
            functools.partial(norm_kernel, own),
            [half_narrow if own else st((rows, WIDE), BF16), half_narrow, half_state, st((HALF, DIM), F32)],
            [state_scratch, pltpu.VMEM((rows, half_width), F32)],
            (*held(made[own], made["q"][2]), prefix, grad_out, gain, *held(*others)),
            2 * state_flops,
        )

    def first_norm(prefix):
        made["norm"] = norm(True, prefix)
        return made["norm"][0]

    pre_a, pre_b = beyond(
        state_a, state_b, False, [local_work(True, v_a), local_work(False, v_b)], first_norm
    )
    q, qt, fq = made["q"]
    out_a, gs_a, state_a, gain_a = made["norm"]
    tokens, gs_b, state_b, gain_b = norm(False, pre_b, out_a)
    back = []

    def first_back():
        *parts, made["out"] = call(
            first_back_kernel,
            [st((rows, PART * DIM), F32), st((PART * FEAT, rows), F32), st((PART * FEAT, rows), F32),
             st((rows, WIDE), BF16)],
            [pltpu.SemaphoreType.DMA],
            held(q, k, qt, kt, v_a, gs_a, tokens),
            2 * square_flops,
            loose=(3,),
            out_specs=[near] * 3 + [apart],
        )
        back.append(parts)
        return (parts[0],)

    def back_work(own, part, v, gs):
        def work():
            back.append(
                call(
                    functools.partial(back_kernel, own, part),
                    [st((rows, PART * DIM), F32), st((PART * FEAT, rows), F32), st((PART * FEAT, rows), F32)],
                    [],
                    held(q, k, qt, kt, v, gs),
                    2 * square_flops,
                )
            )
            return (back[-1][0],)

        return work

    def last_work():
        work = back_work(False, 1, v_b, gs_b)()[0]
        made["gq"] = call(
            query_grad_kernel,
            [flat, st((taps, LANES), F32)],
            [wide, state_scratch, pltpu.VMEM((LANES, rows), F32)],
            (query_in, rim, *held(qt, gs_a, gs_b), pre_a, pre_b, *held(*[b[1] for b in back]), conv_query),
            state_flops,
        )
        return (work, made["gq"][0])

    def first_later(state):
        made["later"] = call(
            first_later_kernel,
            [half_wide, st((HALF * FEAT, rows), F32), st((taps, half_width), F32)],
            [wide, state_scratch],
            (value_in, rim, *held(kt, fk_b, v_b), state, *held(back[2][0], back[3][0], back[2][2], back[3][2])),
            2 * state_flops,
        )
        return made["later"][0]

    works = [first_back, back_work(True, 1, v_a, gs_a), back_work(False, 0, v_b, gs_b), last_work]
    _, post_a = beyond(state_b, state_a, True, works, first_later)
    gv_b, gk_b, sums_b = made["later"]
    gq, sums_q = made["gq"]
    gv_a, gk, heads, sums = call(
        second_later_kernel,
        [half_wide, flat, st((taps - 1, ALL), F32), st((taps + 1, ALL), F32)],
        [wide, state_scratch, pltpu.VMEM((LANES, rows), F32)],
        (key_in, value_in, rim, *held(kt, fk_a, v_a), post_a,
         *held(back[0][0], back[1][0], back[0][2], back[1][2], gv_b, gk_b, sums_b, gq, sums_q, gain_a, gain_b)),
        2 * state_flops,
    )
    follow = lax.ppermute(heads, "seq", [(i + 1, i) for i in range(count - 1)])
    bit = 4
    while bit < count:
        group = (bit, 3 * bit, 2 * bit) if 2 * bit < count else (bit,)
        for got in [exchange(sums, distance) for distance in group]:
            sums = sums + got
        bit *= len(group) + 1
    flat_narrow = st((rows, LANES), BF16)
    grad_query, grad_key, grad_value = call(
        signal_kernel,
        [flat_narrow, flat_narrow, st((rows, WIDE), BF16)],
        [pltpu.VMEM((RIM + 8, DIM), F32), pltpu.VMEM((rows, LANES), BF16), pltpu.VMEM((rows, LANES), BF16),
         pltpu.VMEM((rows, WIDE), BF16), pltpu.SemaphoreType.DMA((rows // STEP + 2,))],
        (*held(gq, gk, gv_a, gv_b), follow, conv_query, conv_key, conv_value),
        2 * state_flops,
        loose=(0, 1, 2),
        out_specs=[apart] * 3,
    )
    taps_query, taps_key, taps_value, taps_gain = call(
        functools.partial(finish_kernel, total_rows ** (-0.5)),
        [st((taps, LANES), F32), st((taps, LANES), F32), st((taps, WIDE), F32), st((1, WIDE), F32)],
        [],
        (tie(sums, grad_value), *[exchange(sums, distance) for distance in (3, 2, 1)]),
        rows,
        loose=(0, 1, 2, 3),
    )
    return (
        made["out"],
        grad_query,
        grad_key,
        grad_value,
        taps_query,
        taps_key,
        taps_value,
        taps_gain.reshape(WIDE),
    )


def solution(mesh):
    rows = P(("groups", "seq"), None)
    return jax.shard_map(
        shards,
        mesh=mesh,
        in_specs=(rows, rows, rows, P(), P(), P(), P(), rows),
        out_specs=(rows, rows, rows, rows, P("groups", None), P("groups", None), P("groups", None), P("groups")),
        check_vma=False,
    )
```

```python
import functools

import jax
import jax.numpy as jnp
from jax import lax
from jax.experimental import pallas as pl
from jax.experimental.pallas import tpu as pltpu
from jax.sharding import PartitionSpec as P

HEADS = 8
HALF = HEADS // 2
PART = HEADS // 4
FEAT = 16
DIM = 128
EPSILON = 1e-06
LANES = HEADS * FEAT
WIDE = HEADS * DIM
ALL = 2 * LANES + WIDE
ROWS = 160
LIN = 128
TAIL = 144
RIM = 16
STEP = 128
CUT = 128
F32 = jnp.float32
BF16 = jnp.bfloat16

NN = (((1,), (0,)), ((), ()))
NT = (((1,), (1,)), ((), ()))
TN = (((0,), (0,)), ((), ()))


def dot(a, b, dims):
    return lax.dot_general(a, b, dims, preferred_element_type=F32)


def head_rows(h):
    return slice(h * FEAT, (h + 1) * FEAT)


def head_lanes(h):
    return slice(h * DIM, (h + 1) * DIM)


def conv(wide_ref, taps, rows):
    margin = taps.shape[0] - 1
    total = taps[0:1] * wide_ref[RIM - margin : RIM - margin + rows]
    for o in range(1, margin + 1):
        total = total + taps[o : o + 1] * wide_ref[RIM - margin + o : RIM - margin + o + rows]
    return total


def tap_sums(grad, wide_ref, taps):
    rows = grad.shape[0]
    start = RIM - (taps - 1)
    return [
        jnp.sum(grad * wide_ref[start + o : start + o + rows], axis=0, keepdims=True)
        for o in range(taps)
    ]


def turned(x, shift):
    return x if shift % FEAT == 0 else pltpu.roll(x, shift % FEAT, 0)


def features(x):
    half = (0.5 / FEAT) ** 0.5
    pieces = [(x * turned(x, FEAT - d) * half).astype(BF16) for d in range(8)]
    pieces.append((x * FEAT ** (-0.25)).astype(BF16))
    rows = lax.broadcasted_iota(jnp.int32, (8, x.shape[1]), 0)
    one = jnp.where(rows == 0, 1.0, 0.0).astype(F32)
    pieces.append(jnp.concatenate([x[:8] * x[8:] * half, one], axis=0).astype(BF16))
    return jnp.concatenate(pieces, axis=0)


def feature_grad(x, state, vector):
    g = dot(state, vector, NT)
    crossed = 2.0 * g[0:FEAT] * x
    for d in range(1, 8):
        part = g[d * FEAT : (d + 1) * FEAT]
        crossed = crossed + part * turned(x, FEAT - d) + turned(part * x, d)
    part = g[TAIL : TAIL + 8]
    crossed = crossed + jnp.concatenate([part * x[8:], part * x[:8]], axis=0)
    return g[LIN:TAIL] * FEAT ** (-0.25) + crossed * (0.5 / FEAT) ** 0.5


def half_index(own):
    core = lax.rem(lax.axis_index("seq"), 2)
    return core if own else 1 - core


def rows_of(half, g):
    return pl.ds(pl.multiple_of((half * HALF + g) * FEAT, FEAT), FEAT)


def lanes_of(half, g, start=0):
    return pl.ds(pl.multiple_of(start + (half * HALF + g) * DIM, DIM), DIM)


def pair_weight():
    rows = lax.broadcasted_iota(jnp.int32, (ROWS, DIM), 0)
    pair = ((rows >= FEAT) & (rows < LIN)) | ((rows >= TAIL) & (rows < TAIL + 8))
    return jnp.where(pair, 2.0, 1.0).astype(F32)


def head_mask(h):
    lanes = lax.broadcasted_iota(jnp.int32, (1, LANES), 1)
    return jnp.where(lanes // FEAT == h, 1.0, 0.0).astype(F32).astype(BF16)


def fill(wide, rim, rest):
    wide[RIM - rim.shape[0] : RIM] = rim.astype(F32)
    wide[RIM : RIM + rest.shape[0]] = rest.astype(F32)


def end_kernel(query, key, value, out, ends, sems):
    start = query.shape[0] - RIM
    copies = [
        pltpu.make_async_copy(ref.at[pl.ds(start, RIM)], ends.at[:, pl.ds(lane, ref.shape[1])], sems.at[i])
        for i, (ref, lane) in enumerate(((query, 0), (key, LANES), (value, 2 * LANES)))
    ]
    for copy in copies:
        copy.start()
    for copy in copies:
        copy.wait()
    out[...] = ends[...].astype(F32)[RIM - out.shape[0] :].astype(BF16)


def bulk_kernel(
    key, value, taps_k, taps_v, k_out, kt_out, v_b, f_b, state_b, v_a, f_a, state_a, wide
):
    rows = key.shape[0] - CUT
    fill(wide, key[CUT - RIM : CUT], key[CUT:])
    k = conv(wide, taps_k[...], rows).astype(BF16)
    k_out[...] = k
    kt_out[...] = k.astype(F32).T.astype(BF16)
    for own, v_out, f_out, state_out in ((False, v_b, f_b, state_b), (True, v_a, f_a, state_a)):
        half = half_index(own)
        for g in range(HALF):
            f_out[g] = features(kt_out[rows_of(half, g)].astype(F32))
        for g in range(HALF):
            lanes = lanes_of(half, g)
            fill(wide, value[CUT - RIM : CUT, lanes], value[CUT:, lanes])
            v_out[:, head_lanes(g)] = conv(wide, taps_v[:, lanes], rows).astype(BF16)
        for g in range(HALF):
            state_out[g] = dot(f_out[g], v_out[:, head_lanes(g)], NN)


def value_states(half, kt, value, rim, taps_v, v_rest, f_rest, state_rest, v_out, f_out, state_out, wide):
    for g in range(HALF):
        f_out[g, :, 0:CUT] = features(kt[rows_of(half, g), 0:CUT].astype(F32))
        f_out[g, :, CUT:] = f_rest[g]
    v_out[CUT:] = v_rest[...]
    for g in range(HALF):
        lanes = lanes_of(half, g)
        fill(wide, rim[:, lanes_of(half, g, 2 * LANES)], value[0:CUT, lanes])
        v_out[0:CUT, head_lanes(g)] = conv(wide, taps_v[:, lanes], CUT).astype(BF16)
    for g in range(HALF):
        first = dot(f_out[g, :, 0:CUT], v_out[0:CUT, head_lanes(g)], NN)
        state_out[g] = (state_rest[g] + first).astype(BF16)


def first_key_kernel(
    key, value, rim, taps_k, taps_v, k_rest, kt_rest, v_rest, f_rest, state_rest,
    k_out, kt_out, v_out, f_out, state_out, wide,
):
    fill(wide, rim[:, LANES : 2 * LANES], key[0:CUT])
    k = conv(wide, taps_k[...], CUT).astype(BF16)
    k_out[0:CUT] = k
    k_out[CUT:] = k_rest[...]
    kt_out[:, 0:CUT] = k.astype(F32).T.astype(BF16)
    kt_out[:, CUT:] = kt_rest[...]
    value_states(
        half_index(False), kt_out, value, rim, taps_v, v_rest, f_rest, state_rest, v_out, f_out, state_out, wide
    )


def second_key_kernel(kt, value, rim, taps_v, v_rest, f_rest, state_rest, v_out, f_out, state_out, wide):
    value_states(
        half_index(True), kt, value, rim, taps_v, v_rest, f_rest, state_rest, v_out, f_out, state_out, wide
    )


def query_kernel(query, rim, taps_q, q_out, qt_out, fq_out, wide):
    rows = query.shape[0]
    fill(wide, rim[:, 0:LANES], query[...])
    q = conv(wide, taps_q[...], rows).astype(BF16)
    q_out[...] = q
    qt = q.astype(F32).T
    qt_out[...] = qt.astype(BF16)
    for h in range(HEADS):
        fq_out[h] = features(qt[head_rows(h)])


def local_kernel(own, q_ref, k_ref, v_ref, out):
    rows = q_ref.shape[0]
    half = half_index(own)
    quarter = q_ref[...] * jnp.asarray(FEAT ** (-0.5), BF16)
    for g in range(HALF):
        qs = quarter * head_mask(half * HALF + g)
        for start in range(0, rows, STEP):
            stop = start + STEP
            t = dot(qs[start:stop], k_ref[0:stop], NT)
            w = (0.5 * t + 1.0) * t + 1.0
            at = lax.broadcasted_iota(jnp.int32, (STEP, stop), 0) + start
            w = jnp.where(at >= lax.broadcasted_iota(jnp.int32, (STEP, stop), 1), w, 0.0)
            out[start:stop, head_lanes(g)] = dot(w.astype(BF16), v_ref[0:stop, head_lanes(g)], NN)


def norm_kernel(own, local, fq, prefix, grad, gain, *refs):
    *others, out, gs_out, state_out, gain_out, pre, summed_ref = refs
    half = half_index(own)
    pre = prefix
    for other in others:
        for g in range(HALF):
            out[:, lanes_of(1 - half, g)] = other[:, head_lanes(g)]
    for g in range(HALF):
        place = head_lanes(g)
        summed_ref[:, place] = local[:, place] + dot(fq[half * HALF + g], pre[g], TN)
    for g in range(HALF):
        place = head_lanes(g)
        summed = summed_ref[:, place]
        scale = lax.rsqrt(jnp.mean(summed * summed, axis=-1, keepdims=True) + EPSILON)
        normal = summed * scale
        weight = gain[pl.ds(half * HALF + g, 1)]
        out[:, place if own else lanes_of(half, g)] = (normal * weight).astype(BF16)
        incoming = grad[:, lanes_of(half, g)].astype(F32)
        gain_out[g : g + 1] = jnp.sum(incoming * normal, axis=0, keepdims=True)
        upstream = incoming * weight
        gs = scale * (upstream - normal * jnp.mean(normal * upstream, axis=-1, keepdims=True))
        gs = gs.astype(BF16)
        gs_out[:, place] = gs
        state_out[g] = dot(fq[half * HALF + g], gs, NN).astype(BF16)


def first_back_kernel(q_ref, k_ref, qt_ref, kt_ref, v_ref, gs_ref, tokens, gv_out, gq_out, gk_out, out, sem):
    copy = pltpu.make_async_copy(tokens, out, sem)
    copy.start()
    back_kernel(True, 0, q_ref, k_ref, qt_ref, kt_ref, v_ref, gs_ref, gv_out, gq_out, gk_out)
    copy.wait()


def back_kernel(own, part, q_ref, k_ref, qt_ref, kt_ref, v_ref, gs_ref, gv_out, gq_out, gk_out):
    rows = q_ref.shape[0]
    half = half_index(own)
    quarter = q_ref[...] * jnp.asarray(FEAT ** (-0.5), BF16)
    for i in range(PART):
        g = part * PART + i
        ks = k_ref[...] * head_mask(half * HALF + g)
        qt = qt_ref[rows_of(half, g)]
        kt = kt_ref[rows_of(half, g)]
        for start in range(0, rows, STEP):
            stop = start + STEP
            shape = (STEP, rows - start)
            t = dot(ks[start:stop], quarter[start:], NT)
            seen = lax.broadcasted_iota(jnp.int32, shape, 1) >= lax.broadcasted_iota(jnp.int32, shape, 0)
            w = jnp.where(seen, (0.5 * t + 1.0) * t + 1.0, 0.0).astype(BF16)
            gs = gs_ref[start:, head_lanes(g)]
            gv_out[start:stop, head_lanes(i)] = dot(w, gs, NN)
            gw = dot(v_ref[start:stop, head_lanes(g)], gs, NT)
            s = jnp.where(seen, gw * (FEAT ** (-0.5) + FEAT ** (-0.5) * t), 0.0).astype(BF16)
            part_q = dot(kt[:, start:stop], s, NN)
            if start == 0:
                gq_out[head_rows(i)] = part_q
            else:
                gq_out[head_rows(i), start:] += part_q
            gk_out[head_rows(i), start:stop] = dot(qt[:, start:], s, NT)


def query_grad_kernel(
    query, rim, qt_ref, gs_a, gs_b, pre_a, pre_b, a0, a1, b0, b1, taps_q, g_out, sums, wide, pre, turned_grad
):
    for own, gs, prefix, locals_ in ((True, gs_a, pre_a, (a0, a1)), (False, gs_b, pre_b, (b0, b1))):
        half = half_index(own)
        pre = prefix
        for g in range(HALF):
            x = qt_ref[rows_of(half, g)].astype(F32)
            turned_grad[rows_of(half, g)] = locals_[g // PART][head_rows(g % PART)] + feature_grad(
                x, pre[g], gs[:, head_lanes(g)]
            )
    grad = turned_grad[...].T
    g_out[...] = grad
    fill(wide, rim[:, 0:LANES], query[...])
    for o, row in enumerate(tap_sums(grad, wide, taps_q.shape[0])):
        sums[o : o + 1] = row


def later_half(half, value, rim, kt, fk, v, state, locals_v, locals_k, gv_out, gk_put, sums_put, wide, post, taps):
    post = state
    for g in range(HALF):
        local = locals_v[g // PART][:, head_lanes(g % PART)]
        gv_out[:, head_lanes(g)] = local + dot(fk[g], post[g], TN)
    for g in range(HALF):
        local = locals_k[g // PART][head_rows(g % PART)]
        x = kt[rows_of(half, g)].astype(F32)
        gk_put(g, local + feature_grad(x, post[g], v[:, head_lanes(g)]))
    for g in range(HALF):
        fill(wide, rim[:, lanes_of(half, g, 2 * LANES)], value[:, lanes_of(half, g)])
        for o, row in enumerate(tap_sums(gv_out[:, head_lanes(g)], wide, taps)):
            sums_put(o, g, row)


def first_later_kernel(value, rim, kt, fk, v, state, v0, v1, k0, k1, gv_out, gk_out, sums, wide, post):
    def gk_put(g, x):
        gk_out[head_rows(g)] = x

    def sums_put(o, g, row):
        sums[o : o + 1, head_lanes(g)] = row

    later_half(
        half_index(False), value, rim, kt, fk, v, state, (v0, v1), (k0, k1), gv_out, gk_put, sums_put, wide, post,
        sums.shape[0],
    )


def second_later_kernel(
    key, value, rim, kt, fk, v, state, v0, v1, k0, k1, gv_b, gk_b, sums_b, gq, sums_q, gain_a, gain_b,
    gv_out, gk_out, head_out, sums, wide, post, turned_grad,
):
    taps = sums_q.shape[0]
    rows = key.shape[0]
    half_a, half_b = half_index(True), half_index(False)

    def gk_put(g, x):
        turned_grad[rows_of(half_a, g)] = x

    def sums_put(o, g, row):
        sums[o : o + 1, lanes_of(half_a, g, 2 * LANES)] = row

    turned_grad[pl.ds(pl.multiple_of(half_b * HALF * FEAT, HALF * FEAT), HALF * FEAT)] = gk_b[...]
    later_half(
        half_a, value, rim, kt, fk, v, state, (v0, v1), (k0, k1), gv_out, gk_put, sums_put, wide, post, taps
    )
    grad = turned_grad[...].T
    gk_out[...] = grad
    fill(wide, rim[:, LANES : 2 * LANES], key[...])
    for o, row in enumerate(tap_sums(grad, wide, taps)):
        sums[o : o + 1, LANES : 2 * LANES] = row
    sums[0:taps, 0:LANES] = sums_q[...]
    sums[taps : taps + 1, 0 : 2 * LANES] = jnp.zeros((1, 2 * LANES), F32)
    head_out[:, 0:LANES] = gq[0 : taps - 1]
    head_out[:, LANES : 2 * LANES] = grad[0 : taps - 1]
    for g in range(HALF):
        sums[0:taps, lanes_of(half_b, g, 2 * LANES)] = sums_b[:, head_lanes(g)]
        for half, gain, gv in ((half_a, gain_a, gv_out), (half_b, gain_b, gv_b)):
            sums[taps : taps + 1, lanes_of(half, g, 2 * LANES)] = gain[g : g + 1]
            head_out[:, lanes_of(half, g, 2 * LANES)] = gv[0 : taps - 1, head_lanes(g)]


def signal_kernel(
    gq, gk, gv_a, gv_b, follow, taps_q, taps_k, taps_v, q_out, k_out, v_out, wide, q_part, k_part, v_part, sems
):
    rows = gq.shape[0]
    count = taps_q.shape[0]
    copies = []

    def one(grad, place, start, stop, after, taps, part, lanes):
        last = stop == rows
        body = stop - start - (RIM if last else 0)
        total = taps[0:1] * grad[start + count - 1 : start + count - 1 + body, place]
        for o in range(1, count):
            total = total + taps[o : o + 1] * grad[start + count - 1 - o : start + count - 1 - o + body, place]
        part[start : start + body, lanes] = total.astype(BF16)
        if last:
            wide[0:RIM] = grad[rows - RIM :, place]
            wide[RIM : RIM + count - 1] = after
            total = taps[0:1] * wide[count - 1 : count - 1 + RIM]
            for o in range(1, count):
                total = total + taps[o : o + 1] * wide[count - 1 - o : count - 1 - o + RIM]
            part[rows - RIM :, lanes] = total.astype(BF16)

    def move(part, out):
        copies.append(pltpu.make_async_copy(part, out, sems.at[len(copies)]))
        copies[-1].start()

    for start in reversed(range(0, rows, STEP)):
        stop = start + STEP
        for own, gv in ((True, gv_a), (False, gv_b)):
            half = half_index(own)
            for g in range(HALF):
                lanes = lanes_of(half, g)
                after = follow[:, lanes_of(half, g, 2 * LANES)]
                one(gv, head_lanes(g), start, stop, after, taps_v[:, lanes], v_part, lanes)
        move(v_part.at[start:stop], v_out.at[start:stop])
    for grad, place, taps, part, out in (
        (gq, slice(0, LANES), taps_q, q_part, q_out), (gk, slice(LANES, 2 * LANES), taps_k, k_part, k_out)
    ):
        one(grad, slice(0, LANES), 0, rows, follow[:, place], taps[...], part, slice(0, LANES))
        move(part, out)
    for copy in copies:
        copy.wait()


def finish_kernel(factor, *refs):
    *terms, q_out, k_out, v_out, gain_out = refs
    taps = q_out.shape[0]
    total = terms[0][...]
    for term in terms[1:]:
        total = total + term[...]
    total = total * factor
    q_out[...] = total[0:taps, 0:LANES]
    k_out[...] = total[0:taps, LANES : 2 * LANES]
    v_out[...] = total[0:taps, 2 * LANES :]
    gain_out[...] = total[taps : taps + 1, 2 * LANES :]


def far(x):
    return pltpu.with_memory_space_constraint(x, pltpu.HBM)


def held(*xs):
    return [pltpu.with_memory_space_constraint(x, pltpu.VMEM) for x in xs]


def call(kernel, outs, scratch, args, flops, limit=16, loose=(), **specs):
    size = lambda a: a.size * a.dtype.itemsize
    moved = sum(size(a) for a in args) + sum(size(o) for o in outs)
    return pl.pallas_call(
        kernel,
        out_shape=[o if i in loose else pltpu.VMEM(o.shape, o.dtype) for i, o in enumerate(outs)],
        scratch_shapes=scratch,
        compiler_params=pltpu.CompilerParams(vmem_limit_bytes=limit * 2**20),
        cost_estimate=pl.CostEstimate(flops=flops, bytes_accessed=moved, transcendentals=0),
        **specs,
    )(*args)


def exchange(x, distance):
    count = lax.axis_size("seq")
    return lax.ppermute(x, "seq", [(i, i ^ distance) for i in range(count)])


def tie(x, *others):
    return lax.optimization_barrier((x, *others))[0]


def on_side(bit, reverse):
    set_ = lax.rem(lax.div(lax.axis_index("seq"), bit), 2)
    return set_ == (0 if reverse else 1)


def chosen(flag, x):
    return jnp.where(flag, x, jnp.zeros_like(x))


def pair_kernel(keep, near, part, their):
    upper = lax.rem(lax.div(lax.axis_index("seq"), 2), 2)

    def half(which):
        place = pl.ds(which * PART, PART)
        return keep[place].astype(F32) + near[place].astype(F32)

    part[...] = half(upper)
    their[...] = half(1 - upper).astype(BF16)


def step_kernel(part, *refs):
    *gots, send = refs
    total = part[...]
    for got in gots:
        total = total + got[...].astype(F32)
    send[...] = total.astype(BF16)


def part_kernel(reverse, part, got_y, *rest):
    *gots, own, give = rest
    before = jnp.zeros(part.shape, F32)
    for i, got in enumerate(gots):
        before = before + chosen(on_side(4 << i, reverse), got[...].astype(F32))
    own[...] = before + chosen(on_side(2, reverse), got_y[...].astype(F32))
    give[...] = (before + chosen(jnp.logical_not(on_side(2, reverse)), part[...])).astype(BF16)


def merge_kernel(reverse, own_part, other_part, keep, near, own, give):
    upper = lax.rem(lax.div(lax.axis_index("seq"), 2), 2)
    side = on_side(1, reverse)
    weight = pair_weight()
    for part, which in ((own_part, upper), (other_part, 1 - upper)):
        place = pl.ds(which * PART, PART)
        before = part[...].astype(F32)
        own[place] = ((before + chosen(side, near[place].astype(F32))) * weight).astype(BF16)
        give[place] = ((before + chosen(jnp.logical_not(side), keep[place].astype(F32))) * weight).astype(BF16)


def beyond(keep, send, reverse, works, last):
    count = lax.axis_size("seq")
    works = list(works)
    st = jax.ShapeDtypeStruct
    whole, part_shape = keep.shape, (PART, *keep.shape[1:])
    wide, narrow = st(part_shape, F32), st(part_shape, BF16)
    cost = 4 * keep.size

    def under(x):
        return tie(x, *works.pop(0)()) if works else x

    near = exchange(send, 1)
    part, their = call(pair_kernel, [wide, narrow], [], (keep, near), cost)
    got_y = exchange(their, 2)
    gots = []
    bit = 4
    while bit < count:
        send = call(step_kernel, [narrow], [], (part, got_y, *gots), cost)[0]
        gots.append(exchange(under(send), bit))
        bit *= 2
    own_part, give_part = call(
        functools.partial(part_kernel, reverse), [wide, narrow], [], (part, got_y, *gots), cost
    )
    other_part = exchange(under(give_part), 2)
    own, give = call(
        functools.partial(merge_kernel, reverse), [st(whole, BF16)] * 2, [], (own_part, other_part, keep, near), cost
    )
    other = exchange(under(give), 1)
    return own, tie(other, last(own))


def shards(query_in, key_in, value_in, conv_query, conv_key, conv_value, norm_gain, grad_out):
    rows = query_in.shape[0]
    taps = conv_query.shape[0]
    count = lax.axis_size("seq")
    total_rows = rows * count
    st = jax.ShapeDtypeStruct
    half_width = HALF * DIM
    half_state, half_wide = st((HALF, ROWS, DIM), BF16), st((rows, half_width), F32)
    half_narrow, half_features = st((rows, half_width), BF16), st((HALF, ROWS, rows), BF16)
    flat, turned_flat = st((rows, LANES), F32), st((LANES, rows), BF16)
    state_scratch = pltpu.VMEM((HALF, ROWS, DIM), BF16)
    wide = pltpu.VMEM((RIM + rows, DIM), F32)
    gain = norm_gain.reshape(HEADS, DIM)
    state_flops = HEADS * ROWS * DIM * rows
    square_flops = 2 * HALF * rows * rows * DIM

    apart = pl.BlockSpec(memory_space=pltpu.HBM)
    near = pl.BlockSpec(memory_space=pltpu.VMEM)
    ends = call(
        end_kernel,
        [st((taps - 1, ALL), BF16)],
        [pltpu.VMEM((RIM, ALL), BF16), pltpu.SemaphoreType.DMA((3,))],
        (far(query_in), far(key_in), far(value_in)),
        rows,
        in_specs=[apart] * 3,
    )[0]
    rim = lax.ppermute(ends, "seq", [(i, i + 1) for i in range(count - 1)])

    rest = rows - CUT
    half_rest = [st((rest, half_width), BF16), st((HALF, ROWS, rest), BF16), st((HALF, ROWS, DIM), F32)]
    k_rest, kt_rest, *rests = call(
        bulk_kernel,
        [st((rest, LANES), BF16), st((LANES, rest), BF16), *half_rest, *half_rest],
        [wide],
        (key_in, value_in, conv_key, conv_value),
        2 * state_flops,
    )
    k, kt, v_b, fk_b, state_b = call(
        first_key_kernel,
        [st((rows, LANES), BF16), turned_flat, half_narrow, half_features, half_state],
        [wide],
        (key_in, value_in, rim, conv_key, conv_value, *held(k_rest, kt_rest, *rests[:3])),
        state_flops,
    )
    v_a, fk_a, state_a = call(
        second_key_kernel,
        [half_narrow, half_features, half_state],
        [wide],
        (*held(kt), value_in, rim, conv_value, *held(*rests[3:])),
        state_flops,
    )
    made = {}

    def local_work(own, v):
        def work():
            if "q" not in made:
                made["q"] = call(
                    query_kernel,
                    [st((rows, LANES), BF16), turned_flat, st((HEADS, ROWS, rows), BF16)],
                    [wide],
                    (query_in, rim, conv_query),
                    state_flops,
                )
            made[own] = call(
                functools.partial(local_kernel, own),
                [half_wide],
                [],
                held(made["q"][0], k, v),
                2 * square_flops,
            )[0]
            return (made[own],)

        return work

    def norm(own, prefix, *others):
        return call(
            functools.partial(norm_kernel, own),
            [half_narrow if own else st((rows, WIDE), BF16), half_narrow, half_state, st((HALF, DIM), F32)],
            [state_scratch, pltpu.VMEM((rows, half_width), F32)],
            (*held(made[own], made["q"][2]), prefix, grad_out, gain, *held(*others)),
            2 * state_flops,
        )

    def first_norm(prefix):
        made["norm"] = norm(True, prefix)
        return made["norm"][0]

    pre_a, pre_b = beyond(
        state_a, state_b, False, [local_work(True, v_a), local_work(False, v_b)], first_norm
    )
    q, qt, fq = made["q"]
    out_a, gs_a, state_a, gain_a = made["norm"]
    tokens, gs_b, state_b, gain_b = norm(False, pre_b, out_a)
    back = []

    def first_back():
        *parts, made["out"] = call(
            first_back_kernel,
            [st((rows, PART * DIM), F32), st((PART * FEAT, rows), F32), st((PART * FEAT, rows), F32),
             st((rows, WIDE), BF16)],
            [pltpu.SemaphoreType.DMA],
            held(q, k, qt, kt, v_a, gs_a, tokens),
            2 * square_flops,
            loose=(3,),
            out_specs=[near] * 3 + [apart],
        )
        back.append(parts)
        return (parts[0],)

    def back_work(own, part, v, gs):
        def work():
            back.append(
                call(
                    functools.partial(back_kernel, own, part),
                    [st((rows, PART * DIM), F32), st((PART * FEAT, rows), F32), st((PART * FEAT, rows), F32)],
                    [],
                    held(q, k, qt, kt, v, gs),
                    2 * square_flops,
                )
            )
            return (back[-1][0],)

        return work

    def last_work():
        work = back_work(False, 1, v_b, gs_b)()[0]
        made["gq"] = call(
            query_grad_kernel,
            [flat, st((taps, LANES), F32)],
            [wide, state_scratch, pltpu.VMEM((LANES, rows), F32)],
            (query_in, rim, *held(qt, gs_a, gs_b), pre_a, pre_b, *held(*[b[1] for b in back]), conv_query),
            state_flops,
        )
        return (work, made["gq"][0])

    def first_later(state):
        made["later"] = call(
            first_later_kernel,
            [half_wide, st((HALF * FEAT, rows), F32), st((taps, half_width), F32)],
            [wide, state_scratch],
            (value_in, rim, *held(kt, fk_b, v_b), state, *held(back[2][0], back[3][0], back[2][2], back[3][2])),
            2 * state_flops,
        )
        return made["later"][0]

    works = [first_back, back_work(True, 1, v_a, gs_a), back_work(False, 0, v_b, gs_b), last_work]
    _, post_a = beyond(state_b, state_a, True, works, first_later)
    gv_b, gk_b, sums_b = made["later"]
    gq, sums_q = made["gq"]
    gv_a, gk, heads, sums = call(
        second_later_kernel,
        [half_wide, flat, st((taps - 1, ALL), F32), st((taps + 1, ALL), F32)],
        [wide, state_scratch, pltpu.VMEM((LANES, rows), F32)],
        (key_in, value_in, rim, *held(kt, fk_a, v_a), post_a,
         *held(back[0][0], back[1][0], back[0][2], back[1][2], gv_b, gk_b, sums_b, gq, sums_q, gain_a, gain_b)),
        2 * state_flops,
    )
    follow = lax.ppermute(heads, "seq", [(i + 1, i) for i in range(count - 1)])
    bit = 4
    while bit < count:
        group = (bit, 3 * bit, 2 * bit) if 2 * bit < count else (bit,)
        for got in [exchange(sums, distance) for distance in group]:
            sums = sums + got
        bit *= len(group) + 1
    flat_narrow = st((rows, LANES), BF16)
    grad_query, grad_key, grad_value = call(
        signal_kernel,
        [flat_narrow, flat_narrow, st((rows, WIDE), BF16)],
        [pltpu.VMEM((RIM + 8, DIM), F32), pltpu.VMEM((rows, LANES), BF16), pltpu.VMEM((rows, LANES), BF16),
         pltpu.VMEM((rows, WIDE), BF16), pltpu.SemaphoreType.DMA((rows // STEP + 2,))],
        (*held(gq, gk, gv_a, gv_b), follow, conv_query, conv_key, conv_value),
        2 * state_flops,
        loose=(0, 1, 2),
        out_specs=[apart] * 3,
    )
    taps_query, taps_key, taps_value, taps_gain = call(
        functools.partial(finish_kernel, total_rows ** (-0.5)),
        [st((taps, LANES), F32), st((taps, LANES), F32), st((taps, WIDE), F32), st((1, WIDE), F32)],
        [],
        (tie(sums, grad_value), *[exchange(sums, distance) for distance in (3, 2, 1)]),
        rows,
        loose=(0, 1, 2, 3),
    )
    return (
        made["out"],
        grad_query,
        grad_key,
        grad_value,
        taps_query,
        taps_key,
        taps_value,
        taps_gain.reshape(WIDE),
    )


def solution(mesh):
    rows = P(("groups", "seq"), None)
    return jax.shard_map(
        shards,
        mesh=mesh,
        in_specs=(rows, rows, rows, P(), P(), P(), P(), rows),
        out_specs=(rows, rows, rows, rows, P("groups", None), P("groups", None), P("groups", None), P("groups")),
        check_vma=False,
    )
```
